32 devices in a mesh: wide: 8 (over y, x, core), narrow: 4 (over z).
Axes of the slice: x: 2, y: 2, z: 4, core: 2. Of those that a mesh axis runs over, the one named last changes fastest.
Arguments:
- tokens: bfloat16 [16384, 768], P(('wide', 'narrow')), may hold values from -6 to 6
- lengths: int32 [32], P(('wide', 'narrow')), may hold values from 1 to 512, as said below
- query_weight: bfloat16 [589824], P(('wide', 'narrow')), may hold values from -0.21875 to 0.21875
- query_bias: bfloat16 [768], P(('wide', 'narrow')), may hold values from -3 to 3
- key_weight: bfloat16 [589824], P(('wide', 'narrow')), may hold values from -0.21875 to 0.21875
- value_weight: bfloat16 [589824], P(('wide', 'narrow')), may hold values from -0.21875 to 0.21875
- value_bias: bfloat16 [768], P(('wide', 'narrow')), may hold values from -3 to 3
- output_weight: bfloat16 [589824], P(('wide', 'narrow')), may hold values from -3.5 to 3.5
- output_bias: bfloat16 [768], P(('wide', 'narrow')), may hold values from -3 to 3
- attn_gain: bfloat16 [768], P(('wide', 'narrow')), may hold values from 0.099609375 to 1.8984375
- attn_shift: bfloat16 [768], P(('wide', 'narrow')), may hold values from -3 to 3
- inner_weight: bfloat16 [2359296], P(('wide', 'narrow')), may hold values from -0.21875 to 0.21875
- inner_bias: bfloat16 [3072], P(('wide', 'narrow')), may hold values from -3 to 3
- outer_weight: bfloat16 [2359296], P(('wide', 'narrow')), may hold values from -0.15625 to 0.15625
- outer_bias: bfloat16 [768], P(('wide', 'narrow')), may hold values from -3 to 3
- ffn_gain: bfloat16 [768], P(('wide', 'narrow')), may hold values from 0.099609375 to 1.8984375
- ffn_shift: bfloat16 [768], P(('wide', 'narrow')), may hold values from -3 to 3
- cotangent: bfloat16 [16384, 768], P(('wide', 'narrow')), may hold values from -6 to 6
Outputs:
- output: bfloat16 [16384, 768], P(('wide', 'narrow'))
- tokens_grad: bfloat16 [16384, 768], P(('wide', 'narrow'))
- query_weight_grad: float32 [589824], P(('wide', 'narrow'))
- query_bias_grad: float32 [768], P(('wide', 'narrow'))
- key_weight_grad: float32 [589824], P(('wide', 'narrow'))
- value_weight_grad: float32 [589824], P(('wide', 'narrow'))
- value_bias_grad: float32 [768], P(('wide', 'narrow'))
- output_weight_grad: float32 [589824], P(('wide', 'narrow'))
- output_bias_grad: float32 [768], P(('wide', 'narrow'))
- attn_gain_grad: float32 [768], P(('wide', 'narrow'))
- attn_shift_grad: float32 [768], P(('wide', 'narrow'))
- inner_weight_grad: float32 [2359296], P(('wide', 'narrow'))
- inner_bias_grad: float32 [3072], P(('wide', 'narrow'))
- outer_weight_grad: float32 [2359296], P(('wide', 'narrow'))
- outer_bias_grad: float32 [768], P(('wide', 'narrow'))
- ffn_gain_grad: float32 [768], P(('wide', 'narrow'))
- ffn_shift_grad: float32 [768], P(('wide', 'narrow'))
The draws below stay inside these ranges and needn't reach their ends.
Inputs may be any that keep to these rules, and one draw needn't show every extreme that they name: Every length is 1 to 512; some sequence has exactly 512; lengths vary from device to device.
All inputs are finite; a program needn't handle non-finite values.
Results may differ from the reference program's by a relative error of at most 0.015.
Values may be sent and summed in bfloat16 or wider, within the bound.
No kernel may reach another device: no remote copies, remote signals or barrier semaphores. Data moves between devices by JAX's collectives and lax.ppermute only.
A program may use at most 192 MiB of HBM per device.

```python
import math
import jax
import jax.numpy as jnp
from jax import lax

D = 768
HEADS = 12
HEAD_DIM = 64
FF = 3072
LEN = 512
SEQ_DEV = 1
SEQS = 32
TOKENS = 16384


def draw_lengths(key, part):
    key_caps = jax.random.fold_in(key, 11)
    key_raw = jax.random.fold_in(key, 12)
    key_where = jax.random.fold_in(key, 13)
    device_count = SEQS // SEQ_DEV
    caps = jax.random.randint(key_caps, (device_count, 1), LEN // 2, LEN + 1)
    raw = jax.random.randint(key_raw, (device_count, SEQ_DEV), 0, LEN)
    drawn = caps - raw * caps // (2 * LEN)
    flat = drawn.reshape(SEQS)
    chosen = jax.random.randint(key_where, (), 0, SEQS)
    places = jnp.arange(SEQS, dtype=jnp.int32)
    return jnp.where(places == chosen, LEN, flat).astype(jnp.int32)


def shard_levels(own_key, shape, cuts, least, high):
    def one(axis_at, blocks):
        heights = jax.random.uniform(jax.random.fold_in(jax.random.fold_in(own_key, 6), axis_at), (blocks,), jnp.float32, least / len(cuts), high / len(cuts))
        return jnp.repeat(jnp.exp(heights), shape[axis_at] // blocks).reshape((-1,) + (1,) * (len(shape) - axis_at - 1))

    factor_of = one(*cuts[0])
    for cut in cuts[1:]:
        factor_of = factor_of * one(*cut)
    return factor_of


def noise(key, dims, spread, limit, cuts=(), kind=jnp.bfloat16):
    values = jax.random.normal(key, dims, jnp.float32) * spread
    if len(cuts) > 0:
        values = shard_levels(key, dims, cuts, -0.22, 0.18) * values
    return jnp.clip(values, min=-limit, max=limit).astype(kind)


def setup_inputs(seed: int = 0) -> dict:
    streams_of = jax.random.split(jax.random.key(seed), 19)
    tokens = noise(streams_of[0], (TOKENS, D), 1.0, 6.0, ((0, 32),))
    lengths = draw_lengths(jax.random.fold_in(streams_of[18], 71), 0)
    query_weight = noise(streams_of[2], (D * D,), D ** -0.5, 0.21875, ((0, 32),))
    query_bias = noise(streams_of[3], (D,), 0.5, 3.0, ((0, 32),))
    key_weight = noise(streams_of[4], (D * D,), D ** -0.5, 0.21875, ((0, 32),))
    value_weight = noise(streams_of[5], (D * D,), D ** -0.5, 0.21875, ((0, 32),))
    value_bias = noise(streams_of[6], (D,), 0.5, 3.0, ((0, 32),))
    output_weight = noise(streams_of[7], (D * D,), (max(1, D * 2 // LEN)) ** -0.5, 3.5, ((0, 32),))
    output_bias = noise(streams_of[8], (D,), 0.5, 3.0, ((0, 32),))
    attn_gain = jnp.clip(1.0 + 0.18 * jax.random.normal(streams_of[9], (D,), jnp.float32), 0.099609375, 1.8984375).astype(jnp.bfloat16)
    attn_shift = noise(streams_of[10], (D,), 0.5, 3.0, ((0, 32),))
    inner_weight = noise(streams_of[11], (D * FF,), D ** -0.5, 0.21875, ((0, 32),))
    inner_bias = noise(streams_of[12], (FF,), 0.5, 3.0, ((0, 32),))
    outer_weight = noise(streams_of[13], (FF * D,), (FF // 2) ** -0.5, 0.15625, ((0, 32),))
    outer_bias = noise(streams_of[14], (D,), 0.5, 3.0, ((0, 32),))
    ffn_gain = jnp.clip(1.0 + 0.18 * jax.random.normal(streams_of[15], (D,), jnp.float32), 0.099609375, 1.8984375).astype(jnp.bfloat16)
    ffn_shift = noise(streams_of[16], (D,), 0.5, 3.0, ((0, 32),))
    cotangent = noise(streams_of[17], (TOKENS, D), 1.0, 6.0, ((0, 32),))
    return dict(tokens=tokens, lengths=lengths, query_weight=query_weight, query_bias=query_bias, key_weight=key_weight, value_weight=value_weight, value_bias=value_bias, output_weight=output_weight, output_bias=output_bias, attn_gain=attn_gain, attn_shift=attn_shift, inner_weight=inner_weight, inner_bias=inner_bias, outer_weight=outer_weight, outer_bias=outer_bias, ffn_gain=ffn_gain, ffn_shift=ffn_shift, cotangent=cotangent)


HIGH = lax.Precision.HIGHEST
EPSILON = 1e-06
SCALE = 0.125

@jax.custom_vjp
def low(v):
    return lax.optimization_barrier(v.astype(jnp.bfloat16)).astype(jnp.float32)

@jax.custom_vjp
def low_back(v):
    return v

def low_keep(v):
    return (low(v), None)

def low_pass(kept, grad):
    return (grad,)

def back_keep(v):
    return (v, None)

def back_low(kept, grad):
    return (low(grad),)
low.defvjp(low_keep, low_pass)
low_back.defvjp(back_keep, back_low)

def matmul(left, right):
    return jnp.dot(left, right, precision=HIGH, preferred_element_type=jnp.float32)

def layer_norm(values, norm_gain, norm_shift):
    row_mean = lax.optimization_barrier(jnp.mean(values, axis=-1, keepdims=True))
    centred = values - row_mean
    row_var = lax.optimization_barrier(jnp.mean(centred * centred, axis=-1, keepdims=True))
    return centred * lax.rsqrt(row_var + EPSILON) * norm_gain + norm_shift

def attend(block_item):
    query_seq, key_seq, value_seq, keep_row = block_item
    scores = jnp.einsum('qhd,khd->hqk', query_seq, key_seq, precision=HIGH) * SCALE
    scores = low_back(scores)
    scores = jnp.where(keep_row[None, None, :], scores, -1e+30)
    probs = jax.nn.softmax(scores, axis=-1)
    mixed = jnp.einsum('hqk,khd->qhd', low(probs), value_seq, precision=HIGH)
    return low_back(low(mixed))

def forward(weight_set, block_in, keep, row_valid):
    query_weight, query_bias, key_weight, value_weight, value_bias, output_weight, output_bias, attn_gain, attn_shift, inner_weight, inner_bias, outer_weight, outer_bias, ffn_gain, ffn_shift = weight_set
    group = block_in.shape[0]
    seq_len = block_in.shape[1]
    rows = block_in.reshape(group * seq_len, D)
    queries = low_back(low(matmul(rows, query_weight.reshape(D, D)) + query_bias))
    key_rows = low_back(low(matmul(rows, key_weight.reshape(D, D))))
    value_rows = low_back(low(matmul(rows, value_weight.reshape(D, D)) + value_bias))
    shape_four = (group, seq_len, HEADS, HEAD_DIM)
    mixed = lax.map(jax.checkpoint(attend), (queries.reshape(shape_four), key_rows.reshape(shape_four), value_rows.reshape(shape_four), keep))
    attn_out = low_back(matmul(mixed.reshape(group * seq_len, D), output_weight.reshape(D, D)) + output_bias)
    normed_one = low(layer_norm(rows + attn_out, attn_gain, attn_shift))
    inner = low_back(matmul(normed_one, inner_weight.reshape(D, FF)) + inner_bias)
    activ = low(jax.nn.gelu(inner, approximate=False))
    outer = low_back(matmul(activ, outer_weight.reshape(FF, D)) + outer_bias)
    final = layer_norm(normed_one + outer, ffn_gain, ffn_shift)
    return final * row_valid

def reference(tokens, lengths, query_weight, query_bias, key_weight, value_weight, value_bias, output_weight, output_bias, attn_gain, attn_shift, inner_weight, inner_bias, outer_weight, outer_bias, ffn_gain, ffn_shift, cotangent):
    weight_set = tuple((member.astype(jnp.float32) for member in (query_weight, query_bias, key_weight, value_weight, value_bias, output_weight, output_bias, attn_gain, attn_shift, inner_weight, inner_bias, outer_weight, outer_bias, ffn_gain, ffn_shift)))
    group = math.gcd(SEQS, max(1, 4096 // LEN))
    blocks = SEQS // group
    inputs = tokens.astype(jnp.float32).reshape(blocks, group, LEN, D)
    cot_rows = cotangent.astype(jnp.float32).reshape(blocks, group * LEN, D)
    seq_lengths = lengths.reshape(blocks, group)
    positions = jnp.arange(LEN, dtype=jnp.int32)

    def block_step(totals, block_item):
        block_in, block_cot, block_len = block_item
        keep = positions[None, :] < block_len[:, None]
        row_valid = keep.reshape(group * LEN, 1).astype(jnp.float32)

        def apply_layer(weights_now, inputs_now):
            return forward(weights_now, inputs_now, keep, row_valid)
        result, pull = jax.vjp(apply_layer, weight_set, block_in)
        weight_grads, input_grad = pull(block_cot)
        totals = tuple((total_now + extra for total_now, extra in zip(totals, weight_grads)))
        return (totals, (result.astype(jnp.bfloat16), input_grad.reshape(group * LEN, D).astype(jnp.bfloat16)))
    zero_set = tuple((jnp.zeros_like(member) for member in weight_set))
    totals, (results, input_grads) = lax.scan(block_step, zero_set, (inputs, cot_rows, seq_lengths))
    g_qw, g_qb, g_kw, g_vw, g_vb, g_ow, g_ob, g_ag, g_as, g_iw, g_ib, g_uw, g_ub, g_fg, g_fs = totals
    return (results.reshape(TOKENS, D), input_grads.reshape(TOKENS, D), g_qw, g_qb, g_kw, g_vw, g_vb, g_ow, g_ob, g_ag, g_as, g_iw, g_ib, g_uw, g_ub, g_fg, g_fs)
```

```python
import functools

import jax
import jax.numpy as jnp
from jax import lax
from jax.experimental import pallas as pl
from jax.experimental.pallas import tpu as pltpu
from jax.sharding import PartitionSpec as P

HEADS = 12
HEAD_DIM = 64
EPSILON = 1e-06
SCALE = 0.125
AXES = ("wide", "narrow")
SMALL = 128
F32 = jnp.float32
BF16 = jnp.bfloat16
NT = (((1,), (1,)), ((), ()))
TN = (((0,), (0,)), ((), ()))
NN = (((1,), (0,)), ((), ()))
VMEM_LIMIT = 48 * 1024 * 1024


def dot(left, right, dims=NN):
    return lax.dot_general(left, right, dims, preferred_element_type=F32)


def call(kernel, out_shape, grid=None, in_specs=None, out_specs=None, scratch=(), flops=0, moved=0, prefetch=0):
    whole = pl.BlockSpec(memory_space=pltpu.VMEM)
    many = isinstance(out_shape, (tuple, list))
    if grid is None:
        spec = dict(
            in_specs=in_specs,
            out_specs=out_specs if out_specs is not None else (tuple(whole for _ in out_shape) if many else whole),
            scratch_shapes=list(scratch),
        )
    else:
        spec = dict(
            grid_spec=pltpu.PrefetchScalarGridSpec(
                num_scalar_prefetch=prefetch,
                grid=grid,
                in_specs=in_specs,
                out_specs=out_specs,
                scratch_shapes=list(scratch),
            )
        )
    return pl.pallas_call(
        kernel,
        out_shape=out_shape,
        compiler_params=pltpu.CompilerParams(vmem_limit_bytes=VMEM_LIMIT),
        cost_estimate=pl.CostEstimate(flops=flops, bytes_accessed=moved, transcendentals=0),
        **spec,
    )


def vmem():
    return pl.BlockSpec(memory_space=pltpu.VMEM)


def smem():
    return pl.BlockSpec(memory_space=pltpu.SMEM)


def anywhere():
    return pl.BlockSpec(memory_space=pl.ANY)


def sds(shape, dtype=BF16):
    return jax.ShapeDtypeStruct(shape, dtype)


def z_join_kernel(at_ref, a0, a1, a2, a3, out):
    rows = a0.shape[0]
    z = lax.rem(at_ref[0], 4)
    for m, piece in enumerate((a0, a1, a2, a3)):
        out[pl.ds(pl.multiple_of((z ^ m) * rows, 8), rows), :] = piece[...]


def z_join(at, pieces):
    rows, cols = pieces[0].shape
    return call(
        z_join_kernel,
        sds((4 * rows, cols)),
        in_specs=[smem()] + [vmem()] * 4,
        moved=rows * cols * 16,
    )(at, *pieces)


def assemble_kernel(at_ref, *refs):
    blocks, out, sem = refs[:8], refs[8], refs[9]
    rows = blocks[0].shape[0]
    group = at_ref[0] // 4
    copies = []
    for m, block in enumerate(blocks):
        start = pl.multiple_of((group ^ m) * rows, 8)
        copies.append(pltpu.make_async_copy(block, out.at[pl.ds(start, rows), :], sem.at[m]))
    for copy in copies:
        copy.start()
    for copy in copies:
        copy.wait()


def assemble(at, blocks):
    rows, cols = blocks[0].shape
    return call(
        assemble_kernel,
        sds((8 * rows, cols)),
        in_specs=[smem()] + [anywhere()] * 8,
        scratch=[pltpu.SemaphoreType.DMA((8,))],
        moved=rows * cols * 32,
    )(at, *blocks)


def swap(value, mask):
    return lax.ppermute(value, AXES, [(i, i ^ mask) for i in range(32)])


def gather_rows(at, own):
    block = z_join(at, [own] + [swap(own, m) for m in (1, 2, 3)])
    spread = [block] + [swap(block, m) for m in (8, 16, 24)]
    blocks = []
    for piece in spread:
        blocks += [piece, swap(piece, 4)]
    return assemble(at, blocks)


def split_tall_kernel(at_ref, left, right, keep, send):
    core = pl.program_id(0)
    value = dot(left[...], right[...], TN).astype(BF16)

    @pl.when(core == 0)
    def _():
        keep[0] = value

    @pl.when(core == 1)
    def _():
        send[0] = value


def grad_tall(at, left, right):
    rows, height = left.shape
    cols = right.shape[1]
    part = height // 8
    out = sds((4, part, cols))
    return call(
        split_tall_kernel,
        (out, out),
        grid=(2, 4),
        prefetch=1,
        in_specs=[
            pl.BlockSpec((rows, part), lambda c, s, at: (0, (at[0] // 4) ^ (2 * s + c))),
            pl.BlockSpec((rows, cols), lambda c, s, at: (0, 0)),
        ],
        out_specs=(
            pl.BlockSpec((1, part, cols), lambda c, s, at: (s + c * (3 - s), 0, 0)),
            pl.BlockSpec((1, part, cols), lambda c, s, at: (s * c, 0, 0)),
        ),
        flops=2 * rows * height * cols,
        moved=2 * (rows * height + rows * cols + height * cols),
    )(at, left, right)


def store_split(at_ref, value, keep, send, col):
    part = keep.shape[1]
    cols = value.shape[1]
    group = at_ref[0] // 4
    core = lax.rem(group, 2)
    for b in range(8):
        slot = (group ^ b) // 2
        piece = value[b * part : (b + 1) * part]

        @pl.when(core == b % 2)
        def _():
            keep[pl.ds(slot, 1), :, col : col + cols] = piece[None]

        @pl.when(core != b % 2)
        def _():
            send[pl.ds(slot, 1), :, col : col + cols] = piece[None]


def grad_wide_kernel(pairs, at_ref, *refs):
    keep, send = refs[-2], refs[-1]
    col = 0
    for left, right in pairs:
        a = refs[left][...]
        for start in range(0, refs[right].shape[1], 768):
            value = dot(a, refs[right][:, start : start + 768], TN)
            store_split(at_ref, value.astype(BF16), keep, send, col)
            col += 768
    if len(refs) > 2 + 1 + max(max(p) for p in pairs):
        rows = refs[-3]
        padded = jnp.concatenate([rows[...], jnp.zeros((SMALL - rows.shape[0], rows.shape[1]), F32)], axis=0)
        store_split(at_ref, padded.T.astype(BF16), keep, send, col)


def grad_wide(at, arrays, pairs, small=None):
    rows, height = arrays[0].shape
    cols = sum(arrays[right].shape[1] for _, right in pairs)
    flops = 2 * rows * height * cols
    if small is not None:
        arrays = arrays + [small]
        cols += SMALL
    part = height // 8
    out = sds((4, part, cols))
    return call(
        functools.partial(grad_wide_kernel, pairs),
        (out, out),
        in_specs=[smem()] + [vmem()] * len(arrays),
        flops=flops,
        moved=2 * height * cols + sum(a.size * a.dtype.itemsize for a in arrays),
    )(at, *arrays)


def core_sum_kernel(keep, came, *outs):
    for s, out in enumerate(outs):
        out[...] = (keep[s].astype(F32) + came[s].astype(F32)).astype(BF16)


def core_sum(keep, came):
    _, part, cols = keep.shape
    width = 384 if cols % 384 == 0 else 128
    return call(
        core_sum_kernel,
        tuple(sds((part, cols)) for _ in range(4)),
        grid=(cols // width,),
        in_specs=[pl.BlockSpec((4, part, width), lambda i: (0, 0, i))] * 2,
        out_specs=tuple(pl.BlockSpec((part, width), lambda i: (0, i)) for _ in range(4)),
        flops=keep.size,
        moved=keep.size * 6,
    )(keep, came)


def plane_sum_kernel(at_ref, a0, a1, a2, a3, z0, z1, z2, z3, total):
    total[...] = (a0[...].astype(F32) + a1[...].astype(F32)) + (a2[...].astype(F32) + a3[...].astype(F32))
    rows = z0.shape[0]
    z = lax.rem(at_ref[0], 4)
    for m, out in enumerate((z0, z1, z2, z3)):
        out[...] = total[pl.ds(pl.multiple_of((z ^ m) * rows, 8), rows), :].astype(BF16)


def plane_sum(at, pieces):
    part, cols = pieces[0].shape
    return call(
        plane_sum_kernel,
        tuple(sds((part // 4, cols)) for _ in range(4)),
        in_specs=[smem()] + [vmem()] * 4,
        scratch=[pltpu.VMEM((part, cols), F32)],
        flops=part * cols * 3,
        moved=part * cols * 10,
    )(at, *pieces)


def reduce_rows(at, keep, send):
    came = swap(send, 4)
    sums = core_sum(keep, came)
    pieces = plane_sum(at, [sums[0]] + [swap(sums[s], 8 * s) for s in (1, 2, 3)])
    last = [pieces[0]] + [swap(pieces[m], m) for m in (1, 2, 3)]
    return sum(p.astype(F32) for p in last)


def head_lanes(h):
    lane = lax.broadcasted_iota(jnp.int32, (1, 2 * HEAD_DIM), 1)
    return (lane // HEAD_DIM) == h


def attend_kernel(len_ref, q_ref, k_ref, v_ref, mixed_ref, lse_ref):
    length = len_ref[0]
    q, k, v = q_ref[...], k_ref[...], v_ref[...]
    size = q.shape[0]
    keep = lax.broadcasted_iota(jnp.int32, (size, 1), 0) < length
    v_t = v.astype(F32).T.astype(BF16)
    parts = []
    for h in range(2):
        q_head = jnp.where(head_lanes(h), q.astype(F32) * SCALE, 0.0).astype(BF16)
        scores = jnp.where(keep, dot(k, q_head, NT), -1e30)
        top = jnp.max(scores, axis=0, keepdims=True)
        shifted = jnp.exp(scores - top)
        total = jnp.sum(shifted, axis=0, keepdims=True)
        mixed = dot(v_t[h * HEAD_DIM : (h + 1) * HEAD_DIM], shifted.astype(BF16)) / total
        parts.append(mixed)
        lse_ref[0, h : h + 1, :] = top + jnp.log(total)
    mixed_ref[...] = jnp.concatenate(parts, axis=0).T.astype(BF16)


def attend(lengths, q, k, v):
    size, width = q.shape
    pairs = width // 128
    tile = pl.BlockSpec((size, 128), lambda i, n: (0, i))
    return call(
        attend_kernel,
        (sds((size, width)), sds((pairs, 2, size), F32)),
        grid=(pairs,),
        prefetch=1,
        in_specs=[tile] * 3,
        out_specs=(tile, pl.BlockSpec((1, 2, size), lambda i, n: (i, 0, 0))),
        flops=4 * size * size * width,
        moved=8 * size * width,
    )(lengths, q, k, v)


def attend_back_kernel(len_ref, q_ref, k_ref, v_ref, mixed_ref, grad_ref, lse_ref, dq_ref, dk_ref, dv_ref):
    length = len_ref[0]
    q, k, v, grad = q_ref[...], k_ref[...], v_ref[...], grad_ref[...]
    size = q.shape[0]
    keep = lax.broadcasted_iota(jnp.int32, (size, 1), 0) < length
    k_t = k.astype(F32).T.astype(BF16)
    prod_t = (grad.astype(F32) * mixed_ref[...].astype(F32)).T
    q_grad, k_grad, v_grad = [], 0.0, 0.0
    for h in range(2):
        mine = head_lanes(h)
        q_head = jnp.where(mine, q.astype(F32) * SCALE, 0.0).astype(BF16)
        g_head = jnp.where(mine, grad, jnp.zeros_like(grad))
        scores = jnp.where(keep, dot(k, q_head, NT), -1e30)
        probs = jnp.exp(scores - lse_ref[0, h : h + 1, :])
        delta = jnp.sum(prod_t[h * HEAD_DIM : (h + 1) * HEAD_DIM], axis=0, keepdims=True)
        prob_grad = dot(v, g_head, NT)
        score_grad = (probs * (prob_grad - delta)).astype(BF16)
        v_grad += dot(probs.astype(BF16), g_head)
        k_grad += dot(score_grad, q_head)
        q_grad.append(dot(k_t[h * HEAD_DIM : (h + 1) * HEAD_DIM], score_grad))
    dq_ref[...] = (jnp.concatenate(q_grad, axis=0) * SCALE).T.astype(BF16)
    dk_ref[...] = k_grad.astype(BF16)
    dv_ref[...] = v_grad.astype(BF16)


def attend_back(lengths, q, k, v, mixed, grad, lse):
    size, width = q.shape
    pairs = width // 128
    tile = pl.BlockSpec((size, 128), lambda i, n: (0, i))
    return call(
        attend_back_kernel,
        (sds((size, width)),) * 3,
        grid=(pairs,),
        prefetch=1,
        in_specs=[tile] * 5 + [pl.BlockSpec((1, 2, size), lambda i, n: (i, 0, 0))],
        out_specs=(tile,) * 3,
        flops=10 * size * size * width,
        moved=16 * size * width,
    )(lengths, q, k, v, mixed, grad, lse)


def layer_norm(values, norm_gain, norm_shift):
    row_mean = jnp.mean(values, axis=-1, keepdims=True)
    centred = values - row_mean
    row_var = jnp.mean(centred * centred, axis=-1, keepdims=True)
    return centred * lax.rsqrt(row_var + EPSILON) * norm_gain + norm_shift


def gelu_exact(values):
    return jax.nn.gelu(values, approximate=False)


def right_product(left, right):
    return dot(left, right, NT)


def column_sums(values):
    return jnp.sum(values.astype(F32), axis=0)


def on_device(
    blocked,
    tokens,
    lengths,
    query_weight,
    query_bias,
    key_weight,
    value_weight,
    value_bias,
    output_weight,
    output_bias,
    attn_gain,
    attn_shift,
    inner_weight,
    inner_bias,
    outer_weight,
    outer_bias,
    ffn_gain,
    ffn_shift,
    cotangent,
):
    row_count, width = tokens.shape
    rows = query_weight.shape[0] // width
    hidden = inner_weight.shape[0] // rows
    ratio = hidden // width
    at = lax.axis_index(AXES).astype(jnp.int32).reshape(1)

    vectors = [query_bias, value_bias, output_bias, attn_gain, attn_shift, outer_bias, ffn_gain, ffn_shift]
    small = jnp.concatenate(
        [v.reshape(rows, 1) for v in vectors]
        + [inner_bias.reshape(rows, ratio), jnp.zeros((rows, SMALL - 8 - ratio), BF16)],
        axis=1,
    )
    first = jnp.concatenate(
        [w.reshape(rows, width) for w in (query_weight, key_weight, value_weight)] + [small], axis=1
    )
    second = jnp.concatenate([output_weight.reshape(rows, width), inner_weight.reshape(rows, hidden)], axis=1)
    third = outer_weight.reshape(rows * ratio, width)

    if blocked:
        gather = functools.partial(gather_rows, at)
    else:

        def gather(own):
            return lax.all_gather(own, AXES, axis=0, tiled=True)

    w_first, w_second, w_third = gather(first), gather(second), gather(third)
    w_q, w_k, w_v = (w_first[:, i * width : (i + 1) * width] for i in range(3))
    tails = w_first[:, 3 * width :]
    tails_t = tails.T.astype(F32)
    qb, vb, ob, ag, ash, ub, fg, fs = (tails_t[i] for i in range(8))
    ib = tails[:, 8 : 8 + ratio].reshape(hidden).astype(F32)
    w_o, w_i, w_u = w_second[:, :width], w_second[:, width:], w_third

    row_valid = (jnp.arange(row_count, dtype=jnp.int32) < lengths[0]).astype(F32)[:, None]
    queries = (dot(tokens, w_q) + qb).astype(BF16)
    key_rows = dot(tokens, w_k).astype(BF16)
    value_rows = (dot(tokens, w_v) + vb).astype(BF16)
    mixed, lse = attend(lengths, queries, key_rows, value_rows)
    resid_one = tokens.astype(F32) + dot(mixed, w_o) + ob
    normed_one = layer_norm(resid_one, ag, ash).astype(BF16)
    inner = dot(normed_one, w_i) + ib
    activ = gelu_exact(inner).astype(BF16)
    resid_two = normed_one.astype(F32) + dot(activ, w_u) + ub
    output = (layer_norm(resid_two, fg, fs) * row_valid).astype(BF16)

    out_grad = cotangent.astype(F32) * row_valid
    _, pull_two = jax.vjp(layer_norm, resid_two, fg, fs)
    resid_two_grad, fg_grad, fs_grad = pull_two(out_grad)
    outer_grad = resid_two_grad.astype(BF16)
    ub_grad = column_sums(outer_grad)
    activ_grad = right_product(outer_grad, w_u)
    _, pull_gelu = jax.vjp(gelu_exact, inner)
    inner_grad = pull_gelu(activ_grad)[0].astype(BF16)
    ib_grad = column_sums(inner_grad)
    normed_grad = resid_two_grad + right_product(inner_grad, w_i)
    _, pull_one = jax.vjp(layer_norm, resid_one, ag, ash)
    resid_one_grad, ag_grad, as_grad = pull_one(normed_grad)
    attn_grad = resid_one_grad.astype(BF16)
    ob_grad = column_sums(attn_grad)
    mixed_grad = right_product(attn_grad, w_o).astype(BF16)
    query_grad, key_grad, value_grad = attend_back(
        lengths, queries, key_rows, value_rows, mixed, mixed_grad, lse
    )
    qb_grad, vb_grad = column_sums(query_grad), column_sums(value_grad)
    tokens_grad = (
        resid_one_grad
        + right_product(query_grad, w_q)
        + right_product(key_grad, w_k)
        + right_product(value_grad, w_v)
    ).astype(BF16)
    small_grad = jnp.concatenate(
        [jnp.stack([qb_grad, vb_grad, ob_grad, ag_grad, as_grad, ub_grad, fg_grad, fs_grad])]
        + [ib_grad.reshape(width, ratio).T, jnp.zeros((16 - 8 - ratio, width), F32)],
        axis=0,
    )

    if blocked:
        own_third = reduce_rows(at, *grad_tall(at, activ, outer_grad))
        own_second = reduce_rows(
            at, *grad_wide(at, [mixed, attn_grad, normed_one, inner_grad], [(0, 1), (2, 3)])
        )
        own_first = reduce_rows(
            at,
            *grad_wide(
                at, [tokens, query_grad, key_grad, value_grad], [(0, 1), (0, 2), (0, 3)], small_grad
            ),
        )
    else:

        def scatter(value):
            return lax.psum_scatter(value, AXES, scatter_dimension=0, tiled=True)

        own_third = scatter(dot(activ, outer_grad, TN))
        own_second = scatter(
            jnp.concatenate([dot(mixed, attn_grad, TN), dot(normed_one, inner_grad, TN)], axis=1)
        )
        own_first = scatter(
            jnp.concatenate(
                [dot(tokens, g, TN) for g in (query_grad, key_grad, value_grad)] + [small_grad.T], axis=1
            )
        )
    own_q, own_k, own_v = (own_first[:, i * width : (i + 1) * width].reshape(-1) for i in range(3))
    tail = own_first[:, 3 * width :]
    own_qb, own_vb, own_ob, own_ag, own_as, own_ub, own_fg, own_fs = (tail[:, i] for i in range(8))
    own_ib = tail[:, 8 : 8 + ratio].reshape(-1)
    return (
        output,
        tokens_grad,
        own_q,
        own_qb,
        own_k,
        own_v,
        own_vb,
        own_second[:, :width].reshape(-1),
        own_ob,
        own_ag,
        own_as,
        own_second[:, width:].reshape(-1),
        own_ib,
        own_third.reshape(-1),
        own_ub,
        own_fg,
        own_fs,
    )


def solution(mesh):
    split = P(AXES)
    rows = P(AXES, None)
    blocked = mesh.shape["wide"] == 8 and mesh.shape["narrow"] == 4
    return jax.shard_map(
        functools.partial(on_device, blocked),
        mesh=mesh,
        in_specs=(rows,) + (split,) * 16 + (rows,),
        out_specs=(rows, rows) + (split,) * 15,
        check_vma=False,
    )
```

```python
import functools

import jax
import jax.numpy as jnp
from jax import lax
from jax.experimental import pallas as pl
from jax.experimental.pallas import tpu as pltpu
from jax.sharding import PartitionSpec as P

HEADS = 12
HEAD_DIM = 64
EPSILON = 1e-06
SCALE = 0.125
AXES = ("wide", "narrow")
SMALL = 128
BIAS_AT = 16
F32 = jnp.float32
BF16 = jnp.bfloat16
NT = (((1,), (1,)), ((), ()))
NN = (((1,), (0,)), ((), ()))
MIB = 1024 * 1024
TIMES = {
    "pack": 1.3,
    "z_join": 0.3,
    "turn_tokens": 1.0,
    "project": 4.0,
    "attend": 8.4,
    "inner": 14.0,
    "outer": 8.0,
    "slope": 6.0,
    "grad_outer": 2.6,
    "normed_back": 5.0,
    "add_halves": 0.5,
    "grad_inner": 3.2,
    "attend_back": 5.7,
    "plane_sum": 0.6,
    "stack_small": 0.5,
    "grad_first": 2.7,
    "tokens_back": 5.6,
    "finish": 0.8,
}


def dot(left, right, dims=NN):
    return lax.dot_general(left, right, dims, preferred_element_type=F32)


def vmem():
    return pl.BlockSpec(memory_space=pltpu.VMEM)


def smem():
    return pl.BlockSpec(memory_space=pltpu.SMEM)


def hbm():
    return pl.BlockSpec(memory_space=pltpu.HBM)


def sds(shape, dtype=BF16):
    return jax.ShapeDtypeStruct(shape, dtype)


def call(kernel, name, args, in_specs, out_shape, out_specs=None, scratch=(), limit=32, grid=None, prefetch=0, alias=None):
    many = isinstance(out_shape, (tuple, list))
    if out_specs is None:
        out_specs = tuple(vmem() for _ in out_shape) if many else vmem()
    if grid is None:
        spec = dict(in_specs=in_specs, out_specs=out_specs, scratch_shapes=list(scratch))
    else:
        spec = dict(
            grid_spec=pltpu.PrefetchScalarGridSpec(
                num_scalar_prefetch=prefetch,
                grid=grid,
                in_specs=in_specs,
                out_specs=out_specs,
                scratch_shapes=list(scratch),
            )
        )
    args = [
        pltpu.with_memory_space_constraint(a, pltpu.HBM) if i >= prefetch and in_specs[i - prefetch].memory_space is pltpu.HBM else a
        for i, a in enumerate(args)
    ]
    return pl.pallas_call(
        kernel,
        out_shape=out_shape,
        name=name,
        input_output_aliases=alias or {},
        compiler_params=pltpu.CompilerParams(vmem_limit_bytes=limit * MIB),
        cost_estimate=pl.CostEstimate(flops=int(TIMES[name] * 4.4e9), bytes_accessed=int(TIMES[name] * 3.6e6), transcendentals=0),
        **spec,
    )(*args)


def swap(value, mask):
    return lax.ppermute(value, AXES, [(i, i ^ mask) for i in range(32)])


def after(value, *others):
    return lax.optimization_barrier((value,) + others)[0]


def pack_kernel(*refs):
    given, (first, second, third), rest = refs[:15], refs[15:18], refs[18:]
    held, (scr, sems) = rest[:15], rest[15:]
    copies = [pltpu.make_async_copy(src, dst, sems.at[i]) for i, (src, dst) in enumerate(zip(given, held))]
    for copy in copies:
        copy.start()

    def spread(i, dst, col):
        copies[i].wait()
        total = held[i].shape[0]
        rows = dst.shape[0]
        blocks = total // rows
        scr[0:total] = held[i][...].astype(F32)
        for c in range(blocks):
            dst[:, col + c * 128 : col + (c + 1) * 128] = scr[pl.ds(c, rows, stride=blocks), :].astype(BF16)
        return col + blocks * 128

    col = 0
    for i in range(3):
        col = spread(i, first, col)
    for copy in copies[6:]:
        copy.wait()
    rows = first.shape[0]
    lines = [held[6 + i][...].astype(F32).reshape(1, rows) for i in range(8)]
    block = jnp.concatenate(lines, axis=0)
    block = jnp.concatenate([block, jnp.zeros((8, 128 - rows), F32)], axis=1)
    block = jnp.concatenate([block, jnp.zeros((120, 128), F32)], axis=0)
    scr[0:128] = block.T
    wide = held[14][...].astype(F32).reshape(1, 4 * rows)
    scr[0:1, BIAS_AT : BIAS_AT + 4 * rows] = wide
    first[:, col : col + SMALL] = scr[0:rows].astype(BF16)
    spread(4, second, spread(3, second, 0))
    spread(5, third, 0)


def pack(weights, vectors, rows, width, hidden):
    flat = [w.reshape(-1, 128) for w in weights]
    ratio = hidden // width
    args = flat + vectors
    return call(
        pack_kernel,
        "pack",
        args,
        [hbm()] * len(args),
        (sds((rows, 3 * width + SMALL)), sds((rows, width + hidden)), sds((rows * ratio, width))),
        scratch=[pltpu.VMEM(a.shape, BF16) for a in args]
        + [pltpu.VMEM((max(f.shape[0] for f in flat), 128), F32), pltpu.SemaphoreType.DMA((15,))],
        limit=8,
    )


def z_join_kernel(at_ref, a0, a1, a2, a3, out):
    rows = a0.shape[0]
    z = lax.rem(at_ref[0], 4)
    for m, piece in enumerate((a0, a1, a2, a3)):
        out[pl.ds(pl.multiple_of((z ^ m) * rows, 8), rows), :] = piece[...]


def z_swaps(own):
    return [own] + [swap(own, m) for m in (1, 2, 3)]


def z_join(at, pieces):
    rows, cols = pieces[0].shape
    return call(z_join_kernel, "z_join", [at] + pieces, [smem()] + [vmem()] * 4, sds((4 * rows, cols)), limit=8)


def forward_halves(x, y):
    half = x.shape[1] // 256 * 128
    return [swap(x[:, :half], 16), swap(y[:, half:], 8)]


def row_blocks(own, x, y, diag):
    out = []
    for pieces in ([own], [x], [y], diag):
        out += [pieces, [swap(p, 4) for p in pieces]]
    return out


def flat_blocks(blocks):
    return [p for pieces in blocks for p in pieces]


PIECES = 10


def block_copies(at_ref, refs, scr, sems):
    group = at_ref[0] // 4
    lists, k = [], 0
    for m in range(8):
        halves = 2 if m >= 6 else 1
        col, mine = 0, []
        for _ in range(halves):
            rows, cols = refs[k].shape
            start = pl.multiple_of((group ^ m) * rows, 8)
            mine.append(pltpu.make_async_copy(refs[k], scr.at[pl.ds(start, rows), pl.ds(col, cols)], sems.at[k]))
            col += cols
            k += 1
        lists.append(mine)
    return lists


def fetch_all(at_ref, refs, scr, sems):
    lists = block_copies(at_ref, refs, scr, sems)
    for mine in lists:
        for copy in mine:
            copy.start()
    for mine in lists:
        for copy in mine:
            copy.wait()


def store_halves(group, value, keep, send, lead=()):
    part = value.shape[0] // 8
    core = lax.rem(group, 2)
    for b in range(8):
        slot = (group ^ b) // 2
        piece = value[b * part : (b + 1) * part]

        @pl.when(core == b % 2)
        def _():
            keep[lead + (pl.ds(slot, 1),)] = piece[None]

        @pl.when(core != b % 2)
        def _():
            send[lead + (pl.ds(slot, 1),)] = piece[None]


def turned(value):
    return value.astype(F32).T.astype(BF16)


def turn_kernel(at_ref, tokens, keep, send):
    store_halves(at_ref[0] // 4, turned(tokens[...]), keep, send)


def turn_tokens(at, tokens):
    size, width = tokens.shape
    out = sds((4, width // 8, size))
    return call(turn_kernel, "turn_tokens", [at, tokens], [smem(), vmem()], (out, out), limit=8)


def qkv_kernel(at_ref, tokens, *refs):
    pieces, (q, k, v, lines, bias, scr, sems) = refs[:PIECES], refs[PIECES:]
    width = tokens.shape[1]
    fetch_all(at_ref, pieces, scr, sems)
    tails = scr[:, 3 * width :].astype(F32)
    rows = tails.T[:16]
    lines[...] = rows
    each = width // 32
    for d in range(32):
        bias[:, 4 * each * d : 4 * each * (d + 1)] = tails[each * d : each * d + 1, BIAS_AT : BIAS_AT + 4 * each]
    x = tokens[...]
    q[...] = (dot(x, scr[:, :width]) + rows[0:1]).astype(BF16)
    k[...] = dot(x, scr[:, width : 2 * width]).astype(BF16)
    v[...] = (dot(x, scr[:, 2 * width : 3 * width]) + rows[1:2]).astype(BF16)


def project(at, tokens, blocks):
    size, width = tokens.shape
    cols = blocks[0][0].shape[1]
    args = [at, tokens] + flat_blocks(blocks)
    return call(
        qkv_kernel,
        "project",
        args,
        [smem(), vmem()] + [hbm()] * PIECES,
        (sds((size, width)),) * 3 + (sds((16, width), F32), sds((1, 4 * width), F32)),
        scratch=[pltpu.VMEM((width, cols), BF16), pltpu.SemaphoreType.DMA((PIECES,))],
        limit=20,
    )


def head_lanes(h):
    lane = lax.broadcasted_iota(jnp.int32, (1, 2 * HEAD_DIM), 1)
    return (lane // HEAD_DIM) == h


def attend_kernel(len_ref, q_ref, k_ref, v_ref, mixed_ref, turned_ref, lse_ref):
    length = len_ref[0]
    q, k, v = q_ref[...], k_ref[...], v_ref[...]
    size = q.shape[0]
    keep = lax.broadcasted_iota(jnp.int32, (size, 1), 0) < length
    v_t = turned(v)
    parts = []
    for h in range(2):
        q_head = jnp.where(head_lanes(h), q.astype(F32) * SCALE, 0.0).astype(BF16)
        scores = jnp.where(keep, dot(k, q_head, NT), -1e30)
        top = jnp.max(scores, axis=0, keepdims=True)
        shifted = jnp.exp(scores - top)
        total = jnp.sum(shifted, axis=0, keepdims=True)
        mixed = dot(v_t[h * HEAD_DIM : (h + 1) * HEAD_DIM], shifted.astype(BF16)) / total
        parts.append(mixed)
        lse_ref[0, h : h + 1, :] = top + jnp.log(total)
    mixed = jnp.concatenate(parts, axis=0)
    turned_ref[...] = mixed.astype(BF16)
    mixed_ref[...] = mixed.T.astype(BF16)


def attend(lengths, q, k, v):
    size, width = q.shape
    pairs = width // 128
    tile = pl.BlockSpec((size, 128), lambda i, n: (0, i))
    return call(
        attend_kernel,
        "attend",
        [lengths, q, k, v],
        [tile] * 3,
        (sds((size, width)), sds((width, size)), sds((pairs, 2, size), F32)),
        out_specs=(
            tile,
            pl.BlockSpec((128, size), lambda i, n: (i, 0)),
            pl.BlockSpec((1, 2, size), lambda i, n: (i, 0, 0)),
        ),
        grid=(pairs,),
        prefetch=1,
        limit=16,
    )


def normed(values):
    centred = values - jnp.mean(values, axis=-1, keepdims=True)
    scale = lax.rsqrt(jnp.mean(centred * centred, axis=-1, keepdims=True) + EPSILON)
    return centred * scale, scale


def norm_back(grad, unit, scale):
    return scale * (
        grad - jnp.mean(grad, axis=-1, keepdims=True) - unit * jnp.mean(grad * unit, axis=-1, keepdims=True)
    )


def inner_kernel(at_ref, tokens, mixed, mixed_t, lines, bias, *refs):
    pieces = refs[:PIECES]
    (unit_out, scale_out, normed_out, activ, slope, weights, keep_b, send_b, keep_a, send_a, scr, sems, out_sem) = refs[PIECES:]
    width = tokens.shape[1]
    hidden = activ.shape[1]
    part = hidden // 8
    group = at_ref[0] // 4
    core = lax.rem(group, 2)
    fetch_all(at_ref, pieces, scr, sems)
    copy = pltpu.make_async_copy(scr, weights, out_sem)
    copy.start()
    resid = tokens[...].astype(F32) + dot(mixed[...], scr[:, :width]) + lines[2:3]
    unit, scale = normed(resid)
    unit_out[...] = unit
    scale_out[...] = jnp.broadcast_to(scale, scale_out.shape)
    values = (unit * lines[3:4] + lines[4:5]).astype(BF16)
    normed_out[...] = values
    store_halves(group, mixed_t[...], keep_b, send_b, (0,))
    store_halves(group, turned(values), keep_b, send_b, (1,))

    def step(b, carry):
        at = pl.multiple_of(b * part, 128)
        x = normed_out[...]
        inner = dot(x, scr[:, pl.ds(pl.multiple_of(width + at, 128), part)]) + bias[:, pl.ds(at, part)]
        share = 0.5 * (1.0 + lax.erf(inner * 0.7071067811865476))
        result = inner * share
        activ[:, pl.ds(at, part)] = result.astype(BF16)
        slope[:, pl.ds(at, part)] = (share + inner * (0.3989422804014327 * jnp.exp(-0.5 * inner * inner))).astype(BF16)
        across = result.T.astype(BF16)
        slot = (group ^ b) // 2

        @pl.when(core == lax.rem(b, 2))
        def _():
            keep_a[pl.ds(slot, 1)] = across[None]

        @pl.when(core != lax.rem(b, 2))
        def _():
            send_a[pl.ds(slot, 1)] = across[None]

        return carry

    lax.fori_loop(0, 8, step, 0)
    copy.wait()


def inner_stage(at, tokens, mixed, mixed_t, lines, bias, blocks):
    size, width = tokens.shape
    hidden = bias.shape[1]
    args = [at, tokens, mixed, mixed_t, lines, bias] + flat_blocks(blocks)
    half_b = sds((2, 4, width // 8, size))
    half_a = sds((4, hidden // 8, size))
    return call(
        inner_kernel,
        "inner",
        args,
        [smem()] + [vmem()] * 5 + [hbm()] * PIECES,
        (
            sds((size, width), F32),
            sds((size, 128), F32),
            sds((size, width)),
            sds((size, hidden)),
            sds((size, hidden)),
            sds((width, width + hidden)),
            half_b,
            half_b,
            half_a,
            half_a,
        ),
        out_specs=(vmem(),) * 5 + (hbm(),) + (vmem(),) * 4,
        scratch=[
            pltpu.VMEM((width, width + hidden), BF16),
            pltpu.SemaphoreType.DMA((PIECES,)),
            pltpu.SemaphoreType.DMA,
        ],
        limit=40,
    )


def outer_kernel(at_ref, len_ref, activ, values, lines, cot, *refs):
    pieces, (output, resid_grad, outer_grad, sums, scr, acc, sems) = refs[:PIECES], refs[PIECES:]
    size = values.shape[0]
    part = activ.shape[1] // 8
    group = at_ref[0] // 4
    lists = block_copies(at_ref, pieces, scr, sems)
    for mine in lists:
        for copy in mine:
            copy.start()
    resid = values[...].astype(F32) + lines[5:6]
    for m, mine in enumerate(lists):
        for copy in mine:
            copy.wait()
        at = pl.multiple_of((group ^ m) * part, 128)
        resid += dot(activ[:, pl.ds(at, part)], scr[pl.ds(at, part), :])
    acc[...] = resid
    gain, shift = lines[6:7], lines[7:8]
    sums[...] = jnp.zeros_like(sums)
    step = 128

    def rows(i, carry):
        part = pl.ds(pl.multiple_of(i * step, step), step)
        unit, scale = normed(acc[part, :])
        valid = lax.broadcasted_iota(jnp.int32, (step, 1), 0) + i * step < len_ref[0]
        output[part, :] = jnp.where(valid, unit * gain + shift, 0.0).astype(BF16)
        grad = jnp.where(valid, cot[part, :].astype(F32), 0.0)
        sums[6:7] += jnp.sum(grad * unit, axis=0, keepdims=True)
        sums[7:8] += jnp.sum(grad, axis=0, keepdims=True)
        grad = norm_back(grad * gain, unit, scale)
        resid_grad[part, :] = grad
        rounded = grad.astype(BF16)
        outer_grad[part, :] = rounded
        sums[5:6] += jnp.sum(rounded.astype(F32), axis=0, keepdims=True)
        return carry

    lax.fori_loop(0, size // step, rows, 0)


def outer_stage(at, lengths, activ, values, lines, cot, blocks):
    size, width = values.shape
    hidden = activ.shape[1]
    args = [at, lengths, activ, values, lines, cot] + flat_blocks(blocks)
    return call(
        outer_kernel,
        "outer",
        args,
        [smem(), smem()] + [vmem()] * 4 + [hbm()] * PIECES,
        (sds((size, width)), sds((size, width), F32), sds((size, width)), sds((8, width), F32)),
        scratch=[
            pltpu.VMEM((hidden, width), BF16),
            pltpu.VMEM((size, width), F32),
            pltpu.SemaphoreType.DMA((PIECES,)),
        ],
        limit=32,
    )


def slope_kernel(at_ref, outer_grad, slope, *refs):
    pieces, (inner_grad, sums, scr, sems) = refs[:PIECES], refs[PIECES:]
    part = slope.shape[1] // 8
    group = at_ref[0] // 4
    lists = block_copies(at_ref, pieces, scr, sems)
    for mine in lists:
        for copy in mine:
            copy.start()
    grad = outer_grad[...]
    for m, mine in enumerate(lists):
        for copy in mine:
            copy.wait()
        at = pl.multiple_of((group ^ m) * part, 128)
        back = dot(grad, scr[pl.ds(at, part), :], NT) * slope[:, pl.ds(at, part)].astype(F32)
        rounded = back.astype(BF16)
        inner_grad[:, pl.ds(at, part)] = rounded
        sums[:, pl.ds(at, part)] = jnp.sum(rounded.astype(F32), axis=0, keepdims=True)


def slope_stage(at, outer_grad, slope, blocks):
    size, width = outer_grad.shape
    hidden = slope.shape[1]
    args = [at, outer_grad, slope] + flat_blocks(blocks)
    return call(
        slope_kernel,
        "slope",
        args,
        [smem()] + [vmem()] * 2 + [hbm()] * PIECES,
        (sds((size, hidden)), sds((1, hidden), F32)),
        scratch=[pltpu.VMEM((hidden, width), BF16), pltpu.SemaphoreType.DMA((PIECES,))],
        limit=32,
    )


def normed_back_kernel(inner_grad, resid_two, unit_ref, scale_ref, lines, weights, resid_grad, attn_grad, mixed_grad, sums):
    width = unit_ref.shape[1]
    hidden = inner_grad.shape[1]
    grad = resid_two[...]
    for c in range(0, hidden, width):
        grad += dot(inner_grad[:, c : c + width], weights[:, width + c : 2 * width + c], NT)
    resid_grad[...] = grad
    sums[...] = jnp.zeros_like(sums)
    step = 128

    def rows(i, carry):
        part = pl.ds(pl.multiple_of(i * step, step), step)
        unit = unit_ref[part, :]
        grad = resid_grad[part, :]
        sums[3:4] += jnp.sum(grad * unit, axis=0, keepdims=True)
        sums[4:5] += jnp.sum(grad, axis=0, keepdims=True)
        grad = norm_back(grad * lines[3:4], unit, scale_ref[part, 0:1])
        resid_grad[part, :] = grad
        rounded = grad.astype(BF16)
        attn_grad[part, :] = rounded
        sums[2:3] += jnp.sum(rounded.astype(F32), axis=0, keepdims=True)
        return carry

    lax.fori_loop(0, grad.shape[0] // step, rows, 0)
    mixed_grad[...] = dot(attn_grad[...], weights[:, :width], NT).astype(BF16)


def normed_back(inner_grad, resid_two, unit, scale, lines, weights):
    size, width = unit.shape
    hidden = inner_grad.shape[1]
    args = [inner_grad, resid_two, unit, scale, lines, weights]
    return call(
        normed_back_kernel,
        "normed_back",
        args,
        [vmem()] * 6,
        (sds((size, width), F32), sds((size, width)), sds((size, width)), sds((8, width), F32)),
        limit=32,
    )


def attend_back_kernel(len_ref, q_ref, k_ref, v_ref, mixed_ref, grad_ref, lse_ref, dq_ref, dk_ref, dv_ref, qs_ref, vs_ref):
    length = len_ref[0]
    q, k, v, grad = q_ref[...], k_ref[...], v_ref[...], grad_ref[...]
    size = q.shape[0]
    keep = lax.broadcasted_iota(jnp.int32, (size, 1), 0) < length
    k_t = turned(k)
    prod_t = turned(grad).astype(F32) * mixed_ref[...].astype(F32)
    q_grad, k_grad, v_grad = [], 0.0, 0.0
    for h in range(2):
        mine = head_lanes(h)
        q_head = jnp.where(mine, q.astype(F32) * SCALE, 0.0).astype(BF16)
        g_head = jnp.where(mine, grad, jnp.zeros_like(grad))
        scores = jnp.where(keep, dot(k, q_head, NT), -1e30)
        probs = jnp.exp(scores - lse_ref[0, h : h + 1, :])
        delta = jnp.sum(prod_t[h * HEAD_DIM : (h + 1) * HEAD_DIM], axis=0, keepdims=True)
        prob_grad = dot(v, g_head, NT)
        score_grad = (probs * (prob_grad - delta)).astype(BF16)
        v_grad += dot(probs.astype(BF16), g_head)
        k_grad += dot(score_grad, q_head)
        q_grad.append(dot(k_t[h * HEAD_DIM : (h + 1) * HEAD_DIM], score_grad))
    q_rounded = (jnp.concatenate(q_grad, axis=0) * SCALE).T.astype(BF16)
    v_rounded = v_grad.astype(BF16)
    dq_ref[...] = q_rounded
    dk_ref[...] = k_grad.astype(BF16)
    dv_ref[...] = v_rounded
    qs_ref[...] = jnp.sum(q_rounded.astype(F32), axis=0, keepdims=True)
    vs_ref[...] = jnp.sum(v_rounded.astype(F32), axis=0, keepdims=True)


def attend_back(lengths, q, k, v, mixed_t, grad, lse, side):
    size, width = q.shape
    pairs = width // 256
    base = side * pairs
    tile = pl.BlockSpec((size, 128), lambda i, n: (0, base + i))
    out = pl.BlockSpec((size, 128), lambda i, n: (0, i))
    line = pl.BlockSpec((1, 128), lambda i, n: (0, i))
    return call(
        attend_back_kernel,
        "attend_back",
        [lengths, q, k, v, mixed_t, grad, lse],
        [tile] * 3
        + [
            pl.BlockSpec((128, size), lambda i, n: (base + i, 0)),
            tile,
            pl.BlockSpec((1, 2, size), lambda i, n: (base + i, 0, 0)),
        ],
        (sds((size, width // 2)),) * 3 + (sds((1, width // 2), F32),) * 2,
        out_specs=(out,) * 3 + (line,) * 2,
        grid=(pairs,),
        prefetch=1,
        limit=16,
    )


def tokens_kernel(at_ref, resid_grad, *refs):
    grads, pieces, (out, scr, sems) = refs[:6], refs[6 : 6 + PIECES], refs[6 + PIECES :]
    half = resid_grad.shape[1] // 2
    fetch_all(at_ref, pieces, scr, sems)
    total = resid_grad[...]
    for i, grad in enumerate(grads):
        total += dot(grad[...], scr[:, i * half : (i + 1) * half], NT)
    out[...] = total.astype(BF16)


def tokens_back(at, resid_grad, grads, blocks):
    size, width = resid_grad.shape
    cols = blocks[0][0].shape[1]
    args = [at, resid_grad] + list(grads) + flat_blocks(blocks)
    return call(
        tokens_kernel,
        "tokens_back",
        args,
        [smem()] + [vmem()] * 7 + [hbm()] * PIECES,
        sds((size, width)),
        scratch=[pltpu.VMEM((width, cols), BF16), pltpu.SemaphoreType.DMA((PIECES,))],
        limit=24,
    )


def small_kernel(one, two, q_low, v_low, q_high, v_high, bias, out):
    half = q_low.shape[1]
    width = one.shape[1]
    out[0:8] = one[...] + two[...]
    out[8:16] = jnp.zeros((8, width), F32)
    out[0:1, :half], out[0:1, half:] = q_low[...], q_high[...]
    out[1:2, :half], out[1:2, half:] = v_low[...], v_high[...]
    for r in range(4):
        out[12 + r : 13 + r] = bias[:, r * width : (r + 1) * width]


def stack_small(one, two, low, high, bias):
    args = [one, two, low[0], low[1], high[0], high[1], bias]
    return call(small_kernel, "stack_small", args, [vmem()] * 7, sds((16, one.shape[1]), F32), limit=4)


def put_slots(value, col, outs):
    s0, s1, s2, s3a, s3b = outs
    part, cols = s0.shape
    half = s3a.shape[1]
    width = value.shape[1]
    for s, out in enumerate((s0, s1, s2)):
        out[:, col : col + width] = value[s * part : (s + 1) * part]
    last = value[3 * part : 4 * part]
    cut = min(max(half - col, 0), width)
    if cut > 0:
        s3a[:, col : col + cut] = last[:, :cut]
    if cut < width:
        s3b[:, col + cut - half : col + width - half] = last[:, cut:]


def slot_shapes(part, cols):
    half = cols // 256 * 128
    return (sds((part, cols)),) * 3 + (sds((part, half)), sds((part, cols - half)))


def grad_kernel(plan, small, *refs):
    outs = refs[-5:]
    if small:
        outs, scr = refs[-6:-1], refs[-1]
    part = outs[0].shape[0]
    col = 0
    for left, lead, mine, came in plan:
        rows = 4 * part
        size = refs[left].shape[-1]
        a = refs[left][lead] if lead is not None else refs[left][...]
        b = refs[left + 1][lead] if lead is not None else refs[left + 1][...]
        a, b = a.reshape(rows, size), b.reshape(rows, size)
        total = refs[mine].shape[1]
        step = min(total, 768)
        for start in range(0, total, step):
            value = dot(a, refs[mine][:, start : start + step]) + dot(b, refs[came][:, start : start + step])
            put_slots(value.astype(BF16), col, outs)
            col += step
    if small:
        at_ref, own, came = refs[small], refs[small + 1], refs[small + 2]
        both = own[...] + came[...]
        padded = jnp.concatenate([both, jnp.zeros((SMALL - both.shape[0], both.shape[1]), F32)], axis=0)
        scr[...] = padded.T
        each = 4 * scr.shape[0] // 32
        wide = scr.shape[0]
        for d in range(32):
            row, lane = 12 + each * d // wide, each * d % wide
            scr[wide // 32 * d : wide // 32 * d + 1, BIAS_AT : BIAS_AT + each] = both[row : row + 1, lane : lane + each]
        group = at_ref[0] // 4
        value = jnp.concatenate(
            [scr[pl.ds(pl.multiple_of((group ^ (2 * s)) * part, 8), part), :] for s in range(4)], axis=0
        )
        put_slots(value.astype(BF16), col, outs)


def weight_grad(name, args, plan, part, cols, small=None):
    specs = [vmem()] * len(args)
    scratch = []
    if small:
        specs[small] = smem()
        scratch = [pltpu.VMEM((8 * part, SMALL), F32)]
    return call(
        functools.partial(grad_kernel, plan, small),
        name,
        args,
        specs,
        slot_shapes(part, cols),
        scratch=scratch,
        limit=32,
    )


def add_kernel(x_ref, p_ref, y_ref, q_ref, x_out, y_out):
    x_out[...] = (x_ref[...].astype(F32) + p_ref[...].astype(F32)).astype(BF16)
    y_out[...] = (y_ref[...].astype(F32) + q_ref[...].astype(F32)).astype(BF16)


def add_halves(x, p, y, q):
    part, cols = x.shape
    half = p.shape[1]
    rest = cols - half
    if half != rest:
        return add_uneven(x, p, y, q)
    low = pl.BlockSpec((part, half), lambda i: (0, 0))
    high = pl.BlockSpec((part, half), lambda i: (0, 1))
    return call(
        add_kernel,
        "add_halves",
        [x, p, y, q],
        [low, low, high, low],
        (sds(x.shape), sds(y.shape)),
        out_specs=(low, high),
        grid=(1,),
        alias={0: 0, 2: 1},
        limit=16,
    )


def uneven_kernel(x_ref, p_ref, y_ref, q_ref, x_out, y_out):
    half = p_ref.shape[1]
    x_out[...] = x_ref[...]
    y_out[...] = y_ref[...]
    x_out[:, :half] = (x_ref[:, :half].astype(F32) + p_ref[...].astype(F32)).astype(BF16)
    y_out[:, half:] = (y_ref[:, half:].astype(F32) + q_ref[...].astype(F32)).astype(BF16)


def add_uneven(x, p, y, q):
    return call(
        uneven_kernel,
        "add_halves",
        [x, p, y, q],
        [vmem()] * 4,
        (sds(x.shape), sds(y.shape)),
        limit=16,
    )


def plane_sum_kernel(at_ref, a0, a1, a2, z0, z1, z2, z3, total):
    total[...] = a0[...].astype(F32) + (a1[...].astype(F32) + a2[...].astype(F32))
    rows = z0.shape[0]
    z = lax.rem(at_ref[0], 4)
    for m, out in enumerate((z0, z1, z2, z3)):
        out[...] = total[pl.ds(pl.multiple_of((z ^ m) * rows, 8), rows), :].astype(BF16)


def plane_sum(at, pieces):
    part, cols = pieces[0].shape
    return call(
        plane_sum_kernel,
        "plane_sum",
        [at] + pieces,
        [smem()] + [vmem()] * 3,
        (sds((part // 4, cols)),) * 4,
        scratch=[pltpu.VMEM((part, cols), F32)],
        limit=16,
    )


def finish_kernel(widths, tail, a0, a1, a2, a3, *outs):
    total = (a0[...].astype(F32) + a1[...].astype(F32)) + (a2[...].astype(F32) + a3[...].astype(F32))
    rows = total.shape[0]
    col = 0
    for width, out in zip(widths, outs):
        blocks = width // 128
        for c in range(blocks):
            out[pl.ds(c, rows, stride=blocks), :] = total[:, col + c * 128 : col + (c + 1) * 128]
        col += width
    if tail:
        block = jnp.concatenate([total[:, col : col + SMALL], jnp.zeros((SMALL - rows, SMALL), F32)], axis=0).T
        for i in range(8):
            outs[len(widths) + i][...] = block[i : i + 1, :rows].reshape(rows)
        outs[len(widths) + 8][...] = total[0:1, col + BIAS_AT : col + BIAS_AT + 4 * rows].reshape(4 * rows)


def finish(pieces, widths, tail=False):
    rows = pieces[0].shape[0]
    shapes = [sds((rows * w // 128, 128), F32) for w in widths]
    if tail:
        shapes += [sds((rows,), F32)] * 8 + [sds((4 * rows,), F32)]
    outs = call(
        functools.partial(finish_kernel, widths, tail),
        "finish",
        pieces,
        [vmem()] * 4,
        tuple(shapes),
        limit=16,
    )
    return [o.reshape(-1) for o in outs]


def scatter_plane(slots):
    s0, s1, s2, s3a, s3b = slots
    p, q = swap(s3a, 16), swap(s3b, 8)
    x, y = add_halves(s1, p, s2, q)
    return [s0, swap(x, 8), swap(y, 16), x]


def z_swaps_back(own):
    return [own[0]] + [swap(own[m], m) for m in (1, 2, 3)]


def blocked_layer(
    tokens,
    lengths,
    query_weight,
    query_bias,
    key_weight,
    value_weight,
    value_bias,
    output_weight,
    output_bias,
    attn_gain,
    attn_shift,
    inner_weight,
    inner_bias,
    outer_weight,
    outer_bias,
    ffn_gain,
    ffn_shift,
    cotangent,
):
    size, width = tokens.shape
    rows = query_weight.shape[0] // width
    hidden = inner_weight.shape[0] // rows
    ratio = hidden // width
    at = lax.axis_index(AXES).astype(jnp.int32).reshape(1)

    first, second, third = pack(
        [query_weight, key_weight, value_weight, output_weight, inner_weight, outer_weight],
        [query_bias, value_bias, output_bias, attn_gain, attn_shift, outer_bias, ffn_gain, ffn_shift, inner_bias],
        rows,
        width,
        hidden,
    )
    z_first = z_join(at, z_swaps(first))
    x_first, y_first = swap(z_first, 8), swap(z_first, 16)
    second_swaps = z_swaps(after(second, z_first))
    x_first, y_first, *second_swaps = lax.optimization_barrier((x_first, y_first, *second_swaps))
    f_first = forward_halves(x_first, y_first)
    first_blocks = row_blocks(z_first, x_first, y_first, f_first)
    z_second = z_join(at, second_swaps)
    x_second, y_second = swap(z_second, 8), swap(z_second, 16)
    third_swaps = z_swaps(after(third, z_second))

    tok_keep, tok_send = turn_tokens(at, tokens)
    tok_came = swap(tok_send, 4)
    queries, key_rows, value_rows, lines, bias = project(at, tokens, first_blocks)
    mixed, mixed_t, lse = attend(lengths, queries, key_rows, value_rows)
    mixed, x_second, y_second, *third_swaps = lax.optimization_barrier((mixed, x_second, y_second, *third_swaps))
    f_second = forward_halves(x_second, y_second)
    second_blocks = row_blocks(z_second, x_second, y_second, f_second)
    z_third = z_join(at, [after(third_swaps[0], *f_second)] + third_swaps[1:])
    mixed_t = after(mixed_t, z_third)
    x_third, y_third = swap(z_third, 8), swap(z_third, 16)
    unit, scale, values, activ, slope, w_second, b_keep, b_send, a_keep, a_send = inner_stage(
        at, tokens, mixed, mixed_t, lines, bias, second_blocks
    )
    a_came, b_came = swap(a_send, 4), swap(b_send, 4)
    values, x_third, y_third = lax.optimization_barrier((values, x_third, y_third))
    f_third = forward_halves(x_third, y_third)
    third_blocks = row_blocks(z_third, x_third, y_third, f_third)
    output, resid_two_grad, outer_grad, sums_two = outer_stage(at, lengths, activ, values, lines, cotangent, third_blocks)
    outer_came = swap(outer_grad, 4)
    inner_grad, bias_grad = slope_stage(at, outer_grad, slope, third_blocks)
    inner_came = swap(inner_grad, 4)
    slots_a = weight_grad(
        "grad_outer",
        [a_keep, a_came, outer_grad, outer_came],
        [(0, None, 2, 3)],
        hidden // 8,
        width,
    )
    resid_one_grad, attn_grad, mixed_grad, sums_one = normed_back(
        after(inner_grad, slots_a[0]), resid_two_grad, unit, scale, lines, w_second
    )
    attn_came = swap(attn_grad, 4)
    plane_a = scatter_plane(slots_a)
    slots_b = weight_grad(
        "grad_inner",
        [after(b_keep, plane_a[3]), b_came, attn_grad, attn_came, inner_grad, inner_came],
        [(0, 0, 2, 3), (0, 1, 4, 5)],
        width // 8,
        width + hidden,
    )
    plane_b = scatter_plane(slots_b)
    half = width // 2
    grads_low = attend_back(
        lengths, queries, key_rows, value_rows, mixed_t, after(mixed_grad, slots_b[0]), lse, 0
    )
    sums_a = plane_sum(at, plane_a[:3])
    grads_high = attend_back(
        lengths, queries, key_rows, value_rows, mixed_t, after(mixed_grad, sums_a[0], plane_b[3], grads_low[0]), lse, 1
    )
    came_low = [swap(g, 4) for g in grads_low[:3]]
    came_high = [swap(g, 4) for g in grads_high[:3]]
    (own_u,) = finish(z_swaps_back(sums_a), [width])
    small = stack_small(sums_one, sums_two, grads_low[3:], grads_high[3:], bias_grad)
    small_came = swap(small, 4)
    args, plan = [tok_keep, after(tok_came, own_u)], []
    for i in range(3):
        for mine, theirs in ((grads_low, came_low), (grads_high, came_high)):
            plan.append((0, None, len(args), len(args) + 1))
            args += [mine[i], theirs[i]]
    slots_c = weight_grad(
        "grad_first",
        args + [at, small, small_came],
        plan,
        width // 8,
        3 * width + SMALL,
        small=len(args),
    )
    plane_c = scatter_plane(slots_c)
    tokens_grad = tokens_back(
        at,
        after(resid_one_grad, slots_c[0]),
        [g for pair in zip(grads_low[:3], grads_high[:3]) for g in pair],
        first_blocks,
    )
    sums_b = plane_sum(at, plane_b[:3])
    own_o, own_i = finish(z_swaps_back(sums_b), [width, hidden])
    sums_c = plane_sum(at, plane_c[:3])
    own_q, own_k, own_v, qb, vb, ob, ag, ash, ub, fg, fs, ib = finish(
        z_swaps_back(sums_c), [width] * 3, tail=True
    )
    return (output, tokens_grad, own_q, qb, own_k, own_v, vb, own_o, ob, ag, ash, own_i, ib, own_u, ub, fg, fs)


def layer_norm(values, norm_gain, norm_shift):
    row_mean = jnp.mean(values, axis=-1, keepdims=True)
    centred = values - row_mean
    row_var = jnp.mean(centred * centred, axis=-1, keepdims=True)
    return centred * lax.rsqrt(row_var + EPSILON) * norm_gain + norm_shift


def gelu_exact(values):
    return jax.nn.gelu(values, approximate=False)


def matmul(left, right):
    return jnp.dot(left, right, preferred_element_type=jnp.float32)


def left_product(left, right):
    return jnp.einsum("rd,rf->df", left, right, preferred_element_type=jnp.float32)


def right_product(left, right):
    return jnp.einsum("rf,df->rd", left, right, preferred_element_type=jnp.float32)


def column_sums(values):
    return jnp.sum(values.astype(jnp.float32), axis=0)


def unpack(gathered, model_width):
    (
        query_weight,
        query_bias,
        key_weight,
        value_weight,
        value_bias,
        output_weight,
        output_bias,
        attn_gain,
        attn_shift,
        inner_weight,
        inner_bias,
        outer_weight,
        outer_bias,
        ffn_gain,
        ffn_shift,
    ) = gathered
    hidden_width = inner_bias.shape[0]
    return (
        query_weight.reshape(model_width, model_width),
        query_bias,
        key_weight.reshape(model_width, model_width),
        value_weight.reshape(model_width, model_width),
        value_bias,
        output_weight.reshape(model_width, model_width),
        output_bias,
        attn_gain.astype(jnp.float32),
        attn_shift.astype(jnp.float32),
        inner_weight.reshape(model_width, hidden_width),
        inner_bias,
        outer_weight.reshape(hidden_width, model_width),
        outer_bias,
        ffn_gain.astype(jnp.float32),
        ffn_shift.astype(jnp.float32),
    )


def scores_of(query_seq, key_seq, keep_row):
    scores = (
        jnp.einsum("qhd,khd->hqk", query_seq, key_seq, preferred_element_type=jnp.float32) * SCALE
    )
    return jnp.where(keep_row[None, None, :], scores, -1e30)


def attend_forward(seq_item):
    query_seq, key_seq, value_seq, keep_row = seq_item
    scores = scores_of(query_seq, key_seq, keep_row)
    top = jnp.max(scores, axis=-1, keepdims=True)
    shifted_exp = jnp.exp(scores - top)
    total = jnp.sum(shifted_exp, axis=-1, keepdims=True)
    probs = (shifted_exp / total).astype(jnp.bfloat16)
    mixed = jnp.einsum("hqk,khd->qhd", probs, value_seq, preferred_element_type=jnp.float32)
    return (mixed.astype(jnp.bfloat16), (top + jnp.log(total))[..., 0])


def attend_backward(seq_item):
    query_seq, key_seq, value_seq, keep_row, log_total, mixed_grad = seq_item
    scores = scores_of(query_seq, key_seq, keep_row)
    probs = jnp.exp(scores - log_total[..., None])
    value_grad = jnp.einsum(
        "hqk,qhd->khd", probs.astype(jnp.bfloat16), mixed_grad, preferred_element_type=jnp.float32
    )
    prob_grad = jnp.einsum(
        "qhd,khd->hqk", mixed_grad, value_seq, preferred_element_type=jnp.float32
    )
    row_delta = jnp.sum(probs * prob_grad, axis=-1, keepdims=True)
    score_grad = (probs * (prob_grad - row_delta)).astype(jnp.bfloat16)
    query_grad = (
        jnp.einsum("hqk,khd->qhd", score_grad, key_seq, preferred_element_type=jnp.float32) * SCALE
    )
    key_grad = (
        jnp.einsum("hqk,qhd->khd", score_grad, query_seq, preferred_element_type=jnp.float32)
        * SCALE
    )
    return (
        query_grad.astype(jnp.bfloat16),
        key_grad.astype(jnp.bfloat16),
        value_grad.astype(jnp.bfloat16),
    )


def plain_layer(
    tokens,
    lengths,
    query_weight,
    query_bias,
    key_weight,
    value_weight,
    value_bias,
    output_weight,
    output_bias,
    attn_gain,
    attn_shift,
    inner_weight,
    inner_bias,
    outer_weight,
    outer_bias,
    ffn_gain,
    ffn_shift,
    cotangent,
):
    row_count = tokens.shape[0]
    model_width = tokens.shape[1]
    seq_count = lengths.shape[0]
    seq_len = row_count // seq_count
    gathered = (
        lax.all_gather(query_weight, ("wide", "narrow"), axis=0, tiled=True),
        lax.all_gather(query_bias, ("wide", "narrow"), axis=0, tiled=True),
        lax.all_gather(key_weight, ("wide", "narrow"), axis=0, tiled=True),
        lax.all_gather(value_weight, ("wide", "narrow"), axis=0, tiled=True),
        lax.all_gather(value_bias, ("wide", "narrow"), axis=0, tiled=True),
        lax.all_gather(output_weight, ("wide", "narrow"), axis=0, tiled=True),
        lax.all_gather(output_bias, ("wide", "narrow"), axis=0, tiled=True),
        lax.all_gather(attn_gain, ("wide", "narrow"), axis=0, tiled=True),
        lax.all_gather(attn_shift, ("wide", "narrow"), axis=0, tiled=True),
        lax.all_gather(inner_weight, ("wide", "narrow"), axis=0, tiled=True),
        lax.all_gather(inner_bias, ("wide", "narrow"), axis=0, tiled=True),
        lax.all_gather(outer_weight, ("wide", "narrow"), axis=0, tiled=True),
        lax.all_gather(outer_bias, ("wide", "narrow"), axis=0, tiled=True),
        lax.all_gather(ffn_gain, ("wide", "narrow"), axis=0, tiled=True),
        lax.all_gather(ffn_shift, ("wide", "narrow"), axis=0, tiled=True),
    )
    (
        full_qw,
        full_qb,
        full_kw,
        full_vw,
        full_vb,
        full_ow,
        full_ob,
        full_ag,
        full_as,
        full_iw,
        full_ib,
        full_uw,
        full_ub,
        full_fg,
        full_fs,
    ) = unpack(gathered, model_width)
    positions = jnp.arange(seq_len, dtype=jnp.int32)
    keep = positions[None, :] < lengths[:, None]
    row_valid = keep.reshape(row_count, 1).astype(jnp.float32)
    shape_four = (seq_count, seq_len, HEADS, HEAD_DIM)
    queries = (matmul(tokens, full_qw) + full_qb).astype(jnp.bfloat16)
    key_rows = matmul(tokens, full_kw).astype(jnp.bfloat16)
    value_rows = (matmul(tokens, full_vw) + full_vb).astype(jnp.bfloat16)
    query_four = queries.reshape(shape_four)
    key_four = key_rows.reshape(shape_four)
    value_four = value_rows.reshape(shape_four)
    mixed, log_total = lax.map(attend_forward, (query_four, key_four, value_four, keep))
    mixed_flat = mixed.reshape(row_count, model_width)
    resid_one = tokens.astype(jnp.float32) + matmul(mixed_flat, full_ow) + full_ob
    normed_one = layer_norm(resid_one, full_ag, full_as).astype(jnp.bfloat16)
    inner = matmul(normed_one, full_iw) + full_ib
    activ = gelu_exact(inner).astype(jnp.bfloat16)
    resid_two = normed_one.astype(jnp.float32) + matmul(activ, full_uw) + full_ub
    output = (layer_norm(resid_two, full_fg, full_fs) * row_valid).astype(jnp.bfloat16)
    (
        back_qw,
        back_qb,
        back_kw,
        back_vw,
        back_vb,
        back_ow,
        back_ob,
        back_ag,
        back_as,
        back_iw,
        back_ib,
        back_uw,
        back_ub,
        back_fg,
        back_fs,
    ) = unpack(gathered, model_width)
    out_grad = cotangent.astype(jnp.float32) * row_valid
    ignored, pull_two = jax.vjp(layer_norm, resid_two, back_fg, back_fs)
    resid_two_grad, ffn_gain_grad, ffn_shift_grad = pull_two(out_grad)
    outer_grad = resid_two_grad.astype(jnp.bfloat16)
    outer_weight_grad = left_product(activ, outer_grad)
    outer_bias_grad = column_sums(outer_grad)
    activ_grad = right_product(outer_grad, back_uw)
    ignored, pull_gelu = jax.vjp(gelu_exact, inner)
    inner_grad = pull_gelu(activ_grad)[0].astype(jnp.bfloat16)
    inner_weight_grad = left_product(normed_one, inner_grad)
    inner_bias_grad = column_sums(inner_grad)
    normed_grad = resid_two_grad + right_product(inner_grad, back_iw)
    ignored, pull_one = jax.vjp(layer_norm, resid_one, back_ag, back_as)
    resid_one_grad, attn_gain_grad, attn_shift_grad = pull_one(normed_grad)
    attn_grad = resid_one_grad.astype(jnp.bfloat16)
    output_weight_grad = left_product(mixed_flat, attn_grad)
    output_bias_grad = column_sums(attn_grad)
    mixed_grad = right_product(attn_grad, back_ow).astype(jnp.bfloat16)
    query_grad, key_grad, value_grad = lax.map(
        attend_backward,
        (query_four, key_four, value_four, keep, log_total, mixed_grad.reshape(shape_four)),
    )
    query_grad = query_grad.reshape(row_count, model_width)
    key_grad = key_grad.reshape(row_count, model_width)
    value_grad = value_grad.reshape(row_count, model_width)
    query_weight_grad = left_product(tokens, query_grad)
    key_weight_grad = left_product(tokens, key_grad)
    value_weight_grad = left_product(tokens, value_grad)
    query_bias_grad = column_sums(query_grad)
    value_bias_grad = column_sums(value_grad)
    tokens_grad = (
        resid_one_grad
        + right_product(query_grad, back_qw)
        + right_product(key_grad, back_kw)
        + right_product(value_grad, back_vw)
    ).astype(jnp.bfloat16)
    (
        own_qw,
        own_qb,
        own_kw,
        own_vw,
        own_vb,
        own_ow,
        own_ob,
        own_ag,
        own_as,
        own_iw,
        own_ib,
        own_uw,
        own_ub,
        own_fg,
        own_fs,
    ) = (
        lax.psum_scatter(
            query_weight_grad.reshape(-1), ("wide", "narrow"), scatter_dimension=0, tiled=True
        ),
        lax.psum_scatter(query_bias_grad, ("wide", "narrow"), scatter_dimension=0, tiled=True),
        lax.psum_scatter(
            key_weight_grad.reshape(-1), ("wide", "narrow"), scatter_dimension=0, tiled=True
        ),
        lax.psum_scatter(
            value_weight_grad.reshape(-1), ("wide", "narrow"), scatter_dimension=0, tiled=True
        ),
        lax.psum_scatter(value_bias_grad, ("wide", "narrow"), scatter_dimension=0, tiled=True),
        lax.psum_scatter(
            output_weight_grad.reshape(-1), ("wide", "narrow"), scatter_dimension=0, tiled=True
        ),
        lax.psum_scatter(output_bias_grad, ("wide", "narrow"), scatter_dimension=0, tiled=True),
        lax.psum_scatter(attn_gain_grad, ("wide", "narrow"), scatter_dimension=0, tiled=True),
        lax.psum_scatter(attn_shift_grad, ("wide", "narrow"), scatter_dimension=0, tiled=True),
        lax.psum_scatter(
            inner_weight_grad.reshape(-1), ("wide", "narrow"), scatter_dimension=0, tiled=True
        ),
        lax.psum_scatter(inner_bias_grad, ("wide", "narrow"), scatter_dimension=0, tiled=True),
        lax.psum_scatter(
            outer_weight_grad.reshape(-1), ("wide", "narrow"), scatter_dimension=0, tiled=True
        ),
        lax.psum_scatter(outer_bias_grad, ("wide", "narrow"), scatter_dimension=0, tiled=True),
        lax.psum_scatter(ffn_gain_grad, ("wide", "narrow"), scatter_dimension=0, tiled=True),
        lax.psum_scatter(ffn_shift_grad, ("wide", "narrow"), scatter_dimension=0, tiled=True),
    )
    return (
        output,
        tokens_grad,
        own_qw,
        own_qb,
        own_kw,
        own_vw,
        own_vb,
        own_ow,
        own_ob,
        own_ag,
        own_as,
        own_iw,
        own_ib,
        own_uw,
        own_ub,
        own_fg,
        own_fs,
    )


def solution(mesh):
    split = P(AXES)
    rows = P(AXES, None)
    blocked = mesh.shape["wide"] == 8 and mesh.shape["narrow"] == 4
    return jax.shard_map(
        blocked_layer if blocked else plain_layer,
        mesh=mesh,
        in_specs=(rows,) + (split,) * 16 + (rows,),
        out_specs=(rows, rows) + (split,) * 15,
        check_vma=False,
    )
```

```python
import functools

import jax
import jax.numpy as jnp
from jax import lax
from jax.experimental import pallas as pl
from jax.experimental.pallas import tpu as pltpu
from jax.sharding import PartitionSpec as P

HEADS = 12
HEAD_DIM = 64
EPSILON = 1e-06
SCALE = 0.125
AXES = ("wide", "narrow")
SMALL = 128
BIAS_AT = 16
F32 = jnp.float32
BF16 = jnp.bfloat16
NT = (((1,), (1,)), ((), ()))
NN = (((1,), (0,)), ((), ()))
MIB = 1024 * 1024
DECLARED = 5.5e8
TIMES = {
    "pack": 1.3,
    "z_join": 0.3,
    "turn_tokens": 1.0,
    "project": 4.0,
    "attend": 8.4,
    "mix": 3.0,
    "inner": 11.0,
    "outer": 8.0,
    "slope": 6.0,
    "grad_outer": 2.6,
    "normed_back": 50.0,
    "add_halves": 0.5,
    "grad_inner": 3.2,
    "attend_back": 11.4,
    "plane_sum": 0.6,
    "pair_sum": 4.0,
    "stack_small": 0.1,
    "grad_first": 0.3,
    "tokens_back": 0.3,
    "finish": 0.8,
}


def dot(left, right, dims=NN):
    return lax.dot_general(left, right, dims, preferred_element_type=F32)


def vmem():
    return pl.BlockSpec(memory_space=pltpu.VMEM)


def smem():
    return pl.BlockSpec(memory_space=pltpu.SMEM)


def hbm():
    return pl.BlockSpec(memory_space=pltpu.HBM)


def sds(shape, dtype=BF16):
    return jax.ShapeDtypeStruct(shape, dtype)


def call(kernel, name, args, in_specs, out_shape, out_specs=None, scratch=(), limit=32, grid=None, prefetch=0, alias=None):
    many = isinstance(out_shape, (tuple, list))
    if out_specs is None:
        out_specs = tuple(vmem() for _ in out_shape) if many else vmem()
    if grid is None:
        spec = dict(in_specs=in_specs, out_specs=out_specs, scratch_shapes=list(scratch))
    else:
        spec = dict(
            grid_spec=pltpu.PrefetchScalarGridSpec(
                num_scalar_prefetch=prefetch,
                grid=grid,
                in_specs=in_specs,
                out_specs=out_specs,
                scratch_shapes=list(scratch),
            )
        )
    args = [
        pltpu.with_memory_space_constraint(a, pltpu.HBM) if i >= prefetch and in_specs[i - prefetch].memory_space is pltpu.HBM else a
        for i, a in enumerate(args)
    ]
    return pl.pallas_call(
        kernel,
        out_shape=out_shape,
        name=name,
        input_output_aliases=alias or {},
        compiler_params=pltpu.CompilerParams(vmem_limit_bytes=limit * MIB),
        cost_estimate=pl.CostEstimate(flops=int(TIMES[name] * DECLARED), bytes_accessed=0, transcendentals=0),
        **spec,
    )(*args)


def swap(value, mask):
    return lax.ppermute(value, AXES, [(i, i ^ mask) for i in range(32)])


def after(value, *others):
    return lax.optimization_barrier((value,) + others)[0]


def pack_kernel(*refs):
    given, (first, second, third), rest = refs[:15], refs[15:18], refs[18:]
    held, (scr, sems) = rest[:15], rest[15:]
    copies = [pltpu.make_async_copy(src, dst, sems.at[i]) for i, (src, dst) in enumerate(zip(given, held))]
    for copy in copies:
        copy.start()

    def spread(i, dst, col):
        copies[i].wait()
        total = held[i].shape[0]
        rows = dst.shape[0]
        blocks = total // rows
        scr[0:total] = held[i][...].astype(F32)
        for c in range(blocks):
            dst[:, col + c * 128 : col + (c + 1) * 128] = scr[pl.ds(c, rows, stride=blocks), :].astype(BF16)
        return col + blocks * 128

    col = 0
    for i in range(4):
        col = spread(i, first, col)
    for copy in copies[6:]:
        copy.wait()
    rows = first.shape[0]
    lines = [held[6 + i][...].astype(F32).reshape(1, rows) for i in range(8)]
    block = jnp.concatenate(lines, axis=0)
    block = jnp.concatenate([block, jnp.zeros((8, 128 - rows), F32)], axis=1)
    block = jnp.concatenate([block, jnp.zeros((120, 128), F32)], axis=0)
    scr[0:128] = block.T
    wide = held[14][...].astype(F32).reshape(1, 4 * rows)
    scr[0:1, BIAS_AT : BIAS_AT + 4 * rows] = wide
    first[:, col : col + SMALL] = scr[0:rows].astype(BF16)
    spread(4, second, 0)
    spread(5, third, 0)


def pack(weights, vectors, rows, width, hidden):
    flat = [w.reshape(-1, 128) for w in weights]
    ratio = hidden // width
    args = flat + vectors
    return call(
        pack_kernel,
        "pack",
        args,
        [hbm()] * len(args),
        (sds((rows, 4 * width + SMALL)), sds((rows, hidden)), sds((rows * ratio, width))),
        scratch=[pltpu.VMEM(a.shape, BF16) for a in args]
        + [pltpu.VMEM((max(f.shape[0] for f in flat), 128), F32), pltpu.SemaphoreType.DMA((15,))],
        limit=8,
    )


def z_join_kernel(at_ref, a0, a1, a2, a3, out):
    rows = a0.shape[0]
    z = lax.rem(at_ref[0], 4)
    for m, piece in enumerate((a0, a1, a2, a3)):
        out[pl.ds(pl.multiple_of((z ^ m) * rows, 8), rows), :] = piece[...]


def z_swaps(own):
    return [own] + [swap(own, m) for m in (1, 2, 3)]


def z_join(at, pieces):
    rows, cols = pieces[0].shape
    return call(z_join_kernel, "z_join", [at] + pieces, [smem()] + [vmem()] * 4, sds((4 * rows, cols)), limit=8)


def forward_halves(x, y):
    half = x.shape[1] // 256 * 128
    return [swap(x[:, :half], 16), swap(y[:, half:], 8)]


def row_blocks(own, x, y, diag):
    out = []
    for pieces in ([own], [x], [y], diag):
        out += [pieces, [swap(p, 4) for p in pieces]]
    return out


def flat_blocks(blocks):
    return [p for pieces in blocks for p in pieces]


PIECES = 10


def block_copies(at_ref, refs, scr, sems):
    group = at_ref[0] // 4
    lists, k = [], 0
    for m in range(8):
        halves = 2 if m >= 6 else 1
        col, mine = 0, []
        for _ in range(halves):
            rows, cols = refs[k].shape
            start = pl.multiple_of((group ^ m) * rows, 8)
            mine.append(pltpu.make_async_copy(refs[k], scr.at[pl.ds(start, rows), pl.ds(col, cols)], sems.at[k]))
            col += cols
            k += 1
        lists.append(mine)
    return lists


def fetch_all(at_ref, refs, scr, sems):
    lists = block_copies(at_ref, refs, scr, sems)
    for mine in lists:
        for copy in mine:
            copy.start()
    for mine in lists:
        for copy in mine:
            copy.wait()


def store_halves(group, value, keep, send, lead=()):
    part = value.shape[0] // 8
    core = lax.rem(group, 2)
    for b in range(8):
        slot = (group ^ b) // 2
        piece = value[b * part : (b + 1) * part]

        @pl.when(core == b % 2)
        def _():
            keep[lead + (pl.ds(slot, 1),)] = piece[None]

        @pl.when(core != b % 2)
        def _():
            send[lead + (pl.ds(slot, 1),)] = piece[None]


def turned(value):
    return value.astype(F32).T.astype(BF16)


def turn_kernel(at_ref, tokens, keep, send):
    store_halves(at_ref[0] // 4, turned(tokens[...]), keep, send)


def turn_tokens(at, tokens):
    size, width = tokens.shape
    out = sds((4, width // 8, size))
    return call(turn_kernel, "turn_tokens", [at, tokens], [smem(), vmem()], (out, out), limit=8)


def qkv_kernel(at_ref, tokens, *refs):
    pieces, (q, k, v, lines, bias, w_out, scr, sems) = refs[:PIECES], refs[PIECES:]
    width = tokens.shape[1]
    fetch_all(at_ref, pieces, scr, sems)
    w_out[...] = scr[:, 3 * width : 4 * width]
    tails = scr[:, 4 * width :].astype(F32)
    rows = tails.T[:16]
    lines[...] = rows
    each = width // 32
    for d in range(32):
        bias[:, 4 * each * d : 4 * each * (d + 1)] = tails[each * d : each * d + 1, BIAS_AT : BIAS_AT + 4 * each]
    x = tokens[...]
    q[...] = (dot(x, scr[:, :width]) + rows[0:1]).astype(BF16)
    k[...] = dot(x, scr[:, width : 2 * width]).astype(BF16)
    v[...] = (dot(x, scr[:, 2 * width : 3 * width]) + rows[1:2]).astype(BF16)


def project(at, tokens, blocks):
    size, width = tokens.shape
    cols = blocks[0][0].shape[1]
    args = [at, tokens] + flat_blocks(blocks)
    return call(
        qkv_kernel,
        "project",
        args,
        [smem(), vmem()] + [hbm()] * PIECES,
        (sds((size, width)),) * 3 + (sds((16, width), F32), sds((1, 4 * width), F32), sds((width, width))),
        scratch=[pltpu.VMEM((width, cols), BF16), pltpu.SemaphoreType.DMA((PIECES,))],
        limit=20,
    )


def head_lanes(h):
    lane = lax.broadcasted_iota(jnp.int32, (1, 2 * HEAD_DIM), 1)
    return (lane // HEAD_DIM) == h


def attend_kernel(len_ref, q_ref, k_ref, v_ref, mixed_ref, turned_ref, lse_ref):
    length = len_ref[0]
    q, k, v = q_ref[...], k_ref[...], v_ref[...]
    size = q.shape[0]
    keep = lax.broadcasted_iota(jnp.int32, (size, 1), 0) < length
    v_t = turned(v)
    parts = []
    for h in range(2):
        q_head = jnp.where(head_lanes(h), q.astype(F32) * SCALE, 0.0).astype(BF16)
        scores = jnp.where(keep, dot(k, q_head, NT), -1e30)
        top = jnp.max(scores, axis=0, keepdims=True)
        shifted = jnp.exp(scores - top)
        total = jnp.sum(shifted, axis=0, keepdims=True)
        mixed = dot(v_t[h * HEAD_DIM : (h + 1) * HEAD_DIM], shifted.astype(BF16)) / total
        parts.append(mixed)
        lse_ref[0, h : h + 1, :] = top + jnp.log(total)
    mixed = jnp.concatenate(parts, axis=0)
    turned_ref[...] = mixed.astype(BF16)
    mixed_ref[...] = mixed.T.astype(BF16)


def attend(lengths, q, k, v):
    size, width = q.shape
    pairs = width // 128
    tile = pl.BlockSpec((size, 128), lambda i, n: (0, i))
    return call(
        attend_kernel,
        "attend",
        [lengths, q, k, v],
        [tile] * 3,
        (sds((size, width)), sds((width, size)), sds((pairs, 2, size), F32)),
        out_specs=(
            tile,
            pl.BlockSpec((128, size), lambda i, n: (i, 0)),
            pl.BlockSpec((1, 2, size), lambda i, n: (i, 0, 0)),
        ),
        grid=(pairs,),
        prefetch=1,
        limit=16,
    )


def normed(values):
    centred = values - jnp.mean(values, axis=-1, keepdims=True)
    scale = lax.rsqrt(jnp.mean(centred * centred, axis=-1, keepdims=True) + EPSILON)
    return centred * scale, scale


def norm_back(grad, unit, scale):
    return scale * (
        grad - jnp.mean(grad, axis=-1, keepdims=True) - unit * jnp.mean(grad * unit, axis=-1, keepdims=True)
    )


def mix_kernel(at_ref, tokens, mixed, mixed_t, lines, w_out, unit_out, scale_out, normed_out, keep, send):
    group = at_ref[0] // 4
    normed_out[...] = mixed[...]
    step = 128

    def rows(i, carry):
        part = pl.ds(pl.multiple_of(i * step, step), step)
        resid = tokens[part, :].astype(F32) + dot(mixed[part, :], w_out[...]) + lines[2:3]
        unit, scale = normed(resid)
        unit_out[part, :] = unit
        scale_out[part, :] = jnp.broadcast_to(scale, (step, scale_out.shape[1]))
        normed_out[part, :] = (unit * lines[3:4] + lines[4:5]).astype(BF16)
        return carry

    lax.fori_loop(0, tokens.shape[0] // step, rows, 0)
    store_halves(group, mixed_t[...], keep, send, (0,))
    store_halves(group, turned(normed_out[...]), keep, send, (1,))


def mix_stage(at, tokens, mixed, mixed_t, lines, w_out):
    size, width = tokens.shape
    half = sds((2, 4, width // 8, size))
    return call(
        mix_kernel,
        "mix",
        [at, tokens, mixed, mixed_t, lines, w_out],
        [smem()] + [vmem()] * 5,
        (sds((size, width), F32), sds((size, 128), F32), sds((size, width)), half, half),
        limit=16,
    )


def inner_kernel(at_ref, values, bias, *refs):
    pieces = refs[:PIECES]
    (activ, slope, weights, keep, send, scr, sems, out_sem) = refs[PIECES:]
    part = activ.shape[1] // 8
    group = at_ref[0] // 4
    core = lax.rem(group, 2)
    fetch_all(at_ref, pieces, scr, sems)
    copy = pltpu.make_async_copy(scr, weights, out_sem)
    copy.start()

    def step(b, carry):
        at = pl.multiple_of(b * part, 128)
        inner = dot(values[...], scr[:, pl.ds(at, part)]) + bias[:, pl.ds(at, part)]
        share = 0.5 * (1.0 + lax.erf(inner * 0.7071067811865476))
        result = inner * share
        activ[:, pl.ds(at, part)] = result.astype(BF16)
        slope[:, pl.ds(at, part)] = (share + inner * (0.3989422804014327 * jnp.exp(-0.5 * inner * inner))).astype(BF16)
        across = result.T.astype(BF16)
        slot = (group ^ b) // 2

        @pl.when(core == lax.rem(b, 2))
        def _():
            keep[pl.ds(slot, 1)] = across[None]

        @pl.when(core != lax.rem(b, 2))
        def _():
            send[pl.ds(slot, 1)] = across[None]

        return carry

    lax.fori_loop(0, 8, step, 0)
    copy.wait()


def inner_stage(at, values, bias, blocks):
    size, width = values.shape
    hidden = bias.shape[1]
    args = [at, values, bias] + flat_blocks(blocks)
    half = sds((4, hidden // 8, size))
    return call(
        inner_kernel,
        "inner",
        args,
        [smem()] + [vmem()] * 2 + [hbm()] * PIECES,
        (sds((size, hidden)), sds((size, hidden)), sds((width, hidden)), half, half),
        out_specs=(vmem(),) * 2 + (hbm(),) + (vmem(),) * 2,
        scratch=[
            pltpu.VMEM((width, hidden), BF16),
            pltpu.SemaphoreType.DMA((PIECES,)),
            pltpu.SemaphoreType.DMA,
        ],
        limit=32,
    )


def outer_kernel(at_ref, len_ref, activ, values, lines, cot, *refs):
    pieces, (output, resid_grad, outer_grad, sums, scr, acc, sems) = refs[:PIECES], refs[PIECES:]
    size = values.shape[0]
    part = activ.shape[1] // 8
    group = at_ref[0] // 4
    lists = block_copies(at_ref, pieces, scr, sems)
    for mine in lists:
        for copy in mine:
            copy.start()
    resid = values[...].astype(F32) + lines[5:6]
    for m, mine in enumerate(lists):
        for copy in mine:
            copy.wait()
        at = pl.multiple_of((group ^ m) * part, 128)
        resid += dot(activ[:, pl.ds(at, part)], scr[pl.ds(at, part), :])
    acc[...] = resid
    gain, shift = lines[6:7], lines[7:8]
    sums[...] = jnp.zeros_like(sums)
    step = 128

    def rows(i, carry):
        part = pl.ds(pl.multiple_of(i * step, step), step)
        unit, scale = normed(acc[part, :])
        valid = lax.broadcasted_iota(jnp.int32, (step, 1), 0) + i * step < len_ref[0]
        output[part, :] = jnp.where(valid, unit * gain + shift, 0.0).astype(BF16)
        grad = jnp.where(valid, cot[part, :].astype(F32), 0.0)
        sums[6:7] += jnp.sum(grad * unit, axis=0, keepdims=True)
        sums[7:8] += jnp.sum(grad, axis=0, keepdims=True)
        grad = norm_back(grad * gain, unit, scale)
        resid_grad[part, :] = grad
        rounded = grad.astype(BF16)
        outer_grad[part, :] = rounded
        sums[5:6] += jnp.sum(rounded.astype(F32), axis=0, keepdims=True)
        return carry

    lax.fori_loop(0, size // step, rows, 0)


def outer_stage(at, lengths, activ, values, lines, cot, blocks):
    size, width = values.shape
    hidden = activ.shape[1]
    args = [at, lengths, activ, values, lines, cot] + flat_blocks(blocks)
    return call(
        outer_kernel,
        "outer",
        args,
        [smem(), smem()] + [vmem()] * 4 + [hbm()] * PIECES,
        (sds((size, width)), sds((size, width), F32), sds((size, width)), sds((8, width), F32)),
        scratch=[
            pltpu.VMEM((hidden, width), BF16),
            pltpu.VMEM((size, width), F32),
            pltpu.SemaphoreType.DMA((PIECES,)),
        ],
        limit=32,
    )


def slope_kernel(at_ref, outer_grad, slope, *refs):
    pieces, (inner_grad, sums, scr, sems) = refs[:PIECES], refs[PIECES:]
    part = slope.shape[1] // 8
    group = at_ref[0] // 4
    lists = block_copies(at_ref, pieces, scr, sems)
    for mine in lists:
        for copy in mine:
            copy.start()
    grad = outer_grad[...]
    for m, mine in enumerate(lists):
        for copy in mine:
            copy.wait()
        at = pl.multiple_of((group ^ m) * part, 128)
        back = dot(grad, scr[pl.ds(at, part), :], NT) * slope[:, pl.ds(at, part)].astype(F32)
        rounded = back.astype(BF16)
        inner_grad[:, pl.ds(at, part)] = rounded
        sums[:, pl.ds(at, part)] = jnp.sum(rounded.astype(F32), axis=0, keepdims=True)


def slope_stage(at, outer_grad, slope, blocks):
    size, width = outer_grad.shape
    hidden = slope.shape[1]
    args = [at, outer_grad, slope] + flat_blocks(blocks)
    return call(
        slope_kernel,
        "slope",
        args,
        [smem()] + [vmem()] * 2 + [hbm()] * PIECES,
        (sds((size, hidden)), sds((1, hidden), F32)),
        scratch=[pltpu.VMEM((hidden, width), BF16), pltpu.SemaphoreType.DMA((PIECES,))],
        limit=32,
    )


def normed_back_kernel(inner_grad, resid_two, unit_ref, scale_ref, lines, w_out, weights, resid_grad, attn_low, attn_high, mixed_grad, sums):
    width = unit_ref.shape[1]
    hidden = inner_grad.shape[1]
    grad = resid_two[...]
    for c in range(0, hidden, width):
        grad += dot(inner_grad[:, c : c + width], weights[:, c : c + width], NT)
    half = attn_low.shape[1]
    resid_grad[...] = grad
    sums[...] = jnp.zeros_like(sums)
    step = 128

    def rows(i, carry):
        part = pl.ds(pl.multiple_of(i * step, step), step)
        unit = unit_ref[part, :]
        grad = resid_grad[part, :]
        sums[3:4] += jnp.sum(grad * unit, axis=0, keepdims=True)
        sums[4:5] += jnp.sum(grad, axis=0, keepdims=True)
        grad = norm_back(grad * lines[3:4], unit, scale_ref[part, 0:1])
        resid_grad[part, :] = grad
        rounded = grad.astype(BF16)
        attn_low[part, :] = rounded[:, :half]
        attn_high[part, :] = rounded[:, half:]
        sums[2:3] += jnp.sum(rounded.astype(F32), axis=0, keepdims=True)
        return carry

    lax.fori_loop(0, grad.shape[0] // step, rows, 0)
    back = dot(attn_low[...], w_out[:, :half], NT) + dot(attn_high[...], w_out[:, half:], NT)
    mixed_grad[...] = back.astype(BF16)


def normed_back(inner_grad, resid_two, unit, scale, lines, w_out, weights):
    size, width = unit.shape
    hidden = inner_grad.shape[1]
    args = [inner_grad, resid_two, unit, scale, lines, w_out, weights]
    return call(
        normed_back_kernel,
        "normed_back",
        args,
        [vmem()] * 7,
        (sds((size, width), F32),)
        + (sds((size, width // 2)),) * 2
        + (sds((size, width)), sds((8, width), F32)),
        limit=32,
    )


def attend_back_kernel(len_ref, q_ref, k_ref, v_ref, mixed_ref, grad_ref, lse_ref, grads_ref, qs_ref, vs_ref):
    length = len_ref[0]
    q, k, v, grad = q_ref[...], k_ref[...], v_ref[...], grad_ref[...]
    size = q.shape[0]
    keep = lax.broadcasted_iota(jnp.int32, (size, 1), 0) < length
    k_t = turned(k)
    prod_t = turned(grad).astype(F32) * mixed_ref[...].astype(F32)
    q_grad, k_grad, v_grad = [], 0.0, 0.0
    for h in range(2):
        mine = head_lanes(h)
        q_head = jnp.where(mine, q.astype(F32) * SCALE, 0.0).astype(BF16)
        g_head = jnp.where(mine, grad, jnp.zeros_like(grad))
        scores = jnp.where(keep, dot(k, q_head, NT), -1e30)
        probs = jnp.exp(scores - lse_ref[0, h : h + 1, :])
        delta = jnp.sum(prod_t[h * HEAD_DIM : (h + 1) * HEAD_DIM], axis=0, keepdims=True)
        prob_grad = dot(v, g_head, NT)
        score_grad = (probs * (prob_grad - delta)).astype(BF16)
        v_grad += dot(probs.astype(BF16), g_head)
        k_grad += dot(score_grad, q_head)
        q_grad.append(dot(k_t[h * HEAD_DIM : (h + 1) * HEAD_DIM], score_grad))
    q_rounded = (jnp.concatenate(q_grad, axis=0) * SCALE).T.astype(BF16)
    v_rounded = v_grad.astype(BF16)
    grads_ref[0] = q_rounded
    grads_ref[1] = k_grad.astype(BF16)
    grads_ref[2] = v_rounded
    qs_ref[...] = jnp.sum(q_rounded.astype(F32), axis=0, keepdims=True)
    vs_ref[...] = jnp.sum(v_rounded.astype(F32), axis=0, keepdims=True)


def attend_back(lengths, q, k, v, mixed_t, grad, lse):
    size, width = q.shape
    pairs = width // 128
    tile = pl.BlockSpec((size, 128), lambda i, n: (0, i))
    out = pl.BlockSpec((3, size, 128), lambda i, n: (0, 0, i))
    line = pl.BlockSpec((1, 128), lambda i, n: (0, i))
    return call(
        attend_back_kernel,
        "attend_back",
        [lengths, q, k, v, mixed_t, grad, lse],
        [tile] * 3
        + [
            pl.BlockSpec((128, size), lambda i, n: (i, 0)),
            tile,
            pl.BlockSpec((1, 2, size), lambda i, n: (i, 0, 0)),
        ],
        (sds((3, size, width)),) + (sds((1, width), F32),) * 2,
        out_specs=(out,) + (line,) * 2,
        grid=(pairs,),
        prefetch=1,
        limit=16,
    )


def tokens_kernel(at_ref, resid_grad, *refs):
    grads, pieces, (out, scr, sems) = refs[0], refs[1 : 1 + PIECES], refs[1 + PIECES :]
    width = resid_grad.shape[1]
    fetch_all(at_ref, pieces, scr, sems)
    total = resid_grad[...]
    for i in range(3):
        total += dot(grads[i], scr[:, i * width : (i + 1) * width], NT)
    out[...] = total.astype(BF16)


def tokens_back(at, resid_grad, grads, blocks):
    size, width = resid_grad.shape
    cols = blocks[0][0].shape[1]
    args = [at, resid_grad, grads] + flat_blocks(blocks)
    return call(
        tokens_kernel,
        "tokens_back",
        args,
        [smem()] + [vmem()] * 2 + [hbm()] * PIECES,
        sds((size, width)),
        scratch=[pltpu.VMEM((width, cols), BF16), pltpu.SemaphoreType.DMA((PIECES,))],
        limit=24,
    )


def small_kernel(one, two, q_sum, v_sum, bias, out):
    width = one.shape[1]
    out[0:8] = one[...] + two[...]
    out[8:16] = jnp.zeros((8, width), F32)
    out[0:1], out[1:2] = q_sum[...], v_sum[...]
    for r in range(4):
        out[12 + r : 13 + r] = bias[:, r * width : (r + 1) * width]


def stack_small(*args):
    one = args[0]
    return call(small_kernel, "stack_small", list(args), [vmem()] * 5, sds((16, one.shape[1]), F32), limit=4)


def put_slots(value, col, outs):
    s0, s1, s2, s3a, s3b = outs
    part, cols = s0.shape
    half = s3a.shape[1]
    width = value.shape[1]
    for s, out in enumerate((s0, s1, s2)):
        out[:, col : col + width] = value[s * part : (s + 1) * part]
    last = value[3 * part : 4 * part]
    cut = min(max(half - col, 0), width)
    if cut > 0:
        s3a[:, col : col + cut] = last[:, :cut]
    if cut < width:
        s3b[:, col + cut - half : col + width - half] = last[:, cut:]


def slot_shapes(part, cols):
    half = cols // 256 * 128
    return (sds((part, cols)),) * 3 + (sds((part, half)), sds((part, cols - half)))


def grad_kernel(plan, small, *refs):
    outs = refs[-5:]
    if small:
        outs, scr = refs[-6:-1], refs[-1]
    part = outs[0].shape[0]
    col = 0
    for left, lead, mine, came, which in plan:
        rows = 4 * part
        size = refs[left].shape[-1]
        a = refs[left][lead] if lead is not None else refs[left][...]
        b = refs[left + 1][lead] if lead is not None else refs[left + 1][...]
        a, b = a.reshape(rows, size), b.reshape(rows, size)
        total = refs[mine].shape[-1]
        step = min(total, 768)
        for start in range(0, total, step):
            at = which + (slice(None), slice(start, start + step))
            value = dot(a, refs[mine][at]) + dot(b, refs[came][at])
            put_slots(value.astype(BF16), col, outs)
            col += step
    if small:
        at_ref, own, came = refs[small], refs[small + 1], refs[small + 2]
        both = own[...] + came[...]
        padded = jnp.concatenate([both, jnp.zeros((SMALL - both.shape[0], both.shape[1]), F32)], axis=0)
        scr[...] = padded.T
        each = 4 * scr.shape[0] // 32
        wide = scr.shape[0]
        for d in range(32):
            row, lane = 12 + each * d // wide, each * d % wide
            scr[wide // 32 * d : wide // 32 * d + 1, BIAS_AT : BIAS_AT + each] = both[row : row + 1, lane : lane + each]
        group = at_ref[0] // 4
        value = jnp.concatenate(
            [scr[pl.ds(pl.multiple_of((group ^ (2 * s)) * part, 8), part), :] for s in range(4)], axis=0
        )
        put_slots(value.astype(BF16), col, outs)


def weight_grad(name, args, plan, part, cols, small=None):
    specs = [vmem()] * len(args)
    scratch = []
    if small:
        specs[small] = smem()
        scratch = [pltpu.VMEM((8 * part, SMALL), F32)]
    return call(
        functools.partial(grad_kernel, plan, small),
        name,
        args,
        specs,
        slot_shapes(part, cols),
        scratch=scratch,
        limit=32,
    )


def add_kernel(x_ref, p_ref, y_ref, q_ref, x_out, y_out):
    x_out[...] = (x_ref[...].astype(F32) + p_ref[...].astype(F32)).astype(BF16)
    y_out[...] = (y_ref[...].astype(F32) + q_ref[...].astype(F32)).astype(BF16)


def add_halves(x, p, y, q):
    part, cols = x.shape
    half = p.shape[1]
    rest = cols - half
    if half != rest:
        return add_uneven(x, p, y, q)
    low = pl.BlockSpec((part, half), lambda i: (0, 0))
    high = pl.BlockSpec((part, half), lambda i: (0, 1))
    return call(
        add_kernel,
        "add_halves",
        [x, p, y, q],
        [low, low, high, low],
        (sds(x.shape), sds(y.shape)),
        out_specs=(low, high),
        grid=(1,),
        alias={0: 0, 2: 1},
        limit=16,
    )


def uneven_kernel(x_ref, p_ref, y_ref, q_ref, x_out, y_out):
    half = p_ref.shape[1]
    x_out[...] = x_ref[...]
    y_out[...] = y_ref[...]
    x_out[:, :half] = (x_ref[:, :half].astype(F32) + p_ref[...].astype(F32)).astype(BF16)
    y_out[:, half:] = (y_ref[:, half:].astype(F32) + q_ref[...].astype(F32)).astype(BF16)


def add_uneven(x, p, y, q):
    return call(
        uneven_kernel,
        "add_halves",
        [x, p, y, q],
        [vmem()] * 4,
        (sds(x.shape), sds(y.shape)),
        limit=16,
    )


def plane_sum_kernel(at_ref, a0, a1, a2, keep, send, total):
    total[...] = a0[...].astype(F32) + (a1[...].astype(F32) + a2[...].astype(F32))
    rows = keep.shape[0] // 2
    z = lax.rem(at_ref[0], 4)
    for m in range(4):
        out = (keep, send)[m // 2]
        part = total[pl.ds(pl.multiple_of((z ^ m) * rows, 8), rows), :]
        out[m % 2 * rows : (m % 2 + 1) * rows] = part.astype(BF16)


def plane_sum(at, pieces):
    part, cols = pieces[0].shape
    return call(
        plane_sum_kernel,
        "plane_sum",
        [at] + pieces,
        [smem()] + [vmem()] * 3,
        (sds((part // 2, cols)),) * 2,
        scratch=[pltpu.VMEM((part, cols), F32)],
        limit=16,
    )


def pair_sum_kernel(keep, came, own, send):
    rows = own.shape[0]
    total = keep[...].astype(F32) + came[...].astype(F32)
    own[...] = total[:rows]
    send[...] = total[rows:].astype(BF16)


def pair_sum(keep, came):
    rows, cols = keep.shape[0] // 2, keep.shape[1]
    return call(
        pair_sum_kernel,
        "pair_sum",
        [keep, came],
        [vmem()] * 2,
        (sds((rows, cols), F32), sds((rows, cols))),
        limit=8,
    )


def finish_kernel(widths, tail, own, came, *outs):
    total = own[...] + came[...].astype(F32)
    rows = total.shape[0]
    col = 0
    for width, out in zip(widths, outs):
        blocks = width // 128
        for c in range(blocks):
            out[pl.ds(c, rows, stride=blocks), :] = total[:, col + c * 128 : col + (c + 1) * 128]
        col += width
    if tail:
        block = jnp.concatenate([total[:, col : col + SMALL], jnp.zeros((SMALL - rows, SMALL), F32)], axis=0).T
        for i in range(8):
            outs[len(widths) + i][...] = block[i : i + 1, :rows].reshape(rows)
        outs[len(widths) + 8][...] = total[0:1, col + BIAS_AT : col + BIAS_AT + 4 * rows].reshape(4 * rows)


def finish(pieces, widths, tail=False):
    rows = pieces[0].shape[0]
    shapes = [sds((rows * w // 128, 128), F32) for w in widths]
    if tail:
        shapes += [sds((rows,), F32)] * 8 + [sds((4 * rows,), F32)]
    outs = call(
        functools.partial(finish_kernel, widths, tail),
        "finish",
        pieces,
        [vmem()] * 2,
        tuple(shapes),
        limit=16,
    )
    return [o.reshape(-1) for o in outs]


def scatter_plane(slots, *done):
    s0, s1, s2, s3a, s3b = slots
    p, q = swap(s3a, 16), swap(s3b, 8)
    s1 = after(s1, *done)
    x, y = add_halves(s1, p, s2, q)
    return [s0, swap(x, 8), swap(y, 16), x]


def first_z(sums, *done):
    keep, send = sums
    return pair_sum(after(keep, *done), swap(send, 2))


def blocked_layer(
    tokens,
    lengths,
    query_weight,
    query_bias,
    key_weight,
    value_weight,
    value_bias,
    output_weight,
    output_bias,
    attn_gain,
    attn_shift,
    inner_weight,
    inner_bias,
    outer_weight,
    outer_bias,
    ffn_gain,
    ffn_shift,
    cotangent,
):
    size, width = tokens.shape
    rows = query_weight.shape[0] // width
    hidden = inner_weight.shape[0] // rows
    ratio = hidden // width
    at = lax.axis_index(AXES).astype(jnp.int32).reshape(1)

    first, second, third = pack(
        [query_weight, key_weight, value_weight, output_weight, inner_weight, outer_weight],
        [query_bias, value_bias, output_bias, attn_gain, attn_shift, outer_bias, ffn_gain, ffn_shift, inner_bias],
        rows,
        width,
        hidden,
    )
    z_first = z_join(at, z_swaps(first))
    x_first, y_first = swap(z_first, 8), swap(z_first, 16)
    second_swaps = z_swaps(after(second, z_first))
    f_first = forward_halves(x_first, y_first)
    first_blocks = row_blocks(z_first, x_first, y_first, f_first)
    z_second = z_join(at, second_swaps)
    x_second, y_second = swap(z_second, 8), swap(z_second, 16)
    third_swaps = z_swaps(after(third, z_second))
    tok_keep, tok_send = turn_tokens(at, tokens)
    tok_came = swap(tok_send, 4)
    queries, key_rows, value_rows, lines, bias, w_out = project(at, tokens, first_blocks)
    mixed, mixed_t, lse = attend(lengths, queries, key_rows, value_rows)
    mixed, x_second, y_second, *third_swaps = lax.optimization_barrier((mixed, x_second, y_second, *third_swaps))
    f_second = forward_halves(x_second, y_second)
    unit, scale, values, b_keep, b_send = mix_stage(at, tokens, after(mixed, tok_came), mixed_t, lines, w_out)
    b_came = swap(b_send, 4)
    second_blocks = row_blocks(z_second, x_second, y_second, [after(f, values) for f in f_second])
    z_third = z_join(at, [after(third_swaps[0], *f_second)] + third_swaps[1:])
    x_third, y_third = swap(z_third, 8), swap(z_third, 16)
    activ, slope, w_inner, a_keep, a_send = inner_stage(at, after(values, z_third), bias, second_blocks)
    activ, x_third, y_third = lax.optimization_barrier((activ, x_third, y_third))
    f_third = forward_halves(x_third, y_third)
    third_blocks = row_blocks(z_third, x_third, y_third, f_third)
    a_came = swap(after(a_send, x_third), 4)
    activ = after(activ, a_came)
    output, resid_two_grad, outer_grad, sums_two = outer_stage(at, lengths, activ, values, lines, cotangent, third_blocks)

    outer_came = swap(outer_grad, 4)
    slots_a = weight_grad(
        "grad_outer",
        [a_keep, a_came, outer_grad, outer_came],
        [(0, None, 2, 3, ())],
        hidden // 8,
        width,
    )
    inner_grad, bias_grad = slope_stage(at, after(outer_grad, slots_a[0]), slope, third_blocks)
    plane_a = scatter_plane(slots_a, inner_grad)
    inner_came = swap(after(inner_grad, plane_a[3]), 4)
    resid_one_grad, attn_low, attn_high, mixed_grad, sums_one = normed_back(
        after(inner_grad, plane_a[3]), resid_two_grad, unit, scale, lines, w_out, w_inner
    )
    low_came, high_came = swap(attn_low, 4), swap(attn_high, 4)
    slots_b = weight_grad(
        "grad_inner",
        [b_keep, b_came, attn_low, low_came, attn_high, high_came, inner_grad, inner_came],
        [(0, 0, 2, 3, ()), (0, 0, 4, 5, ()), (0, 1, 6, 7, ())],
        width // 8,
        width + hidden,
    )
    sums_a = plane_sum(at, [after(plane_a[0], slots_b[0])] + plane_a[1:3])
    grads, q_sum, v_sum = attend_back(
        lengths, queries, key_rows, value_rows, mixed_t, after(mixed_grad, sums_a[0]), lse
    )
    own_a, last_a = first_z(sums_a, grads)
    plane_b = scatter_plane(slots_b, own_a)
    grads_came = swap(after(grads, plane_b[3]), 4)
    (own_u,) = finish([own_a, swap(last_a, 1)], [width])
    small = stack_small(sums_one, sums_two, q_sum, v_sum, bias_grad)
    small_came = swap(small, 4)
    args = [tok_keep, tok_came, grads, grads_came]
    plan = [(0, None, 2, 3, (i,)) for i in range(3)]
    slots_c = weight_grad(
        "grad_first",
        args + [at, small, small_came],
        plan,
        width // 8,
        3 * width + SMALL,
        small=len(args),
    )
    slots_c = list(slots_c)
    slots_c[3], slots_c[4], _ = lax.optimization_barrier((slots_c[3], slots_c[4], own_u))
    tokens_grad = tokens_back(at, after(resid_one_grad, slots_c[3]), grads, first_blocks)
    sums_b = plane_sum(at, [after(plane_b[0], tokens_grad)] + plane_b[1:3])
    plane_c = scatter_plane(slots_c, sums_b[0])
    own_b, last_b = first_z(sums_b)
    sums_c = plane_sum(at, [after(plane_c[0], own_b)] + plane_c[1:3])
    own_o, own_i = finish([own_b, swap(last_b, 1)], [width, hidden])
    own_c, last_c = first_z(sums_c)
    own_q, own_k, own_v, qb, vb, ob, ag, ash, ub, fg, fs, ib = finish(
        [own_c, swap(last_c, 1)], [width] * 3, tail=True
    )
    return (output, tokens_grad, own_q, qb, own_k, own_v, vb, own_o, ob, ag, ash, own_i, ib, own_u, ub, fg, fs)


def layer_norm(values, norm_gain, norm_shift):
    row_mean = jnp.mean(values, axis=-1, keepdims=True)
    centred = values - row_mean
    row_var = jnp.mean(centred * centred, axis=-1, keepdims=True)
    return centred * lax.rsqrt(row_var + EPSILON) * norm_gain + norm_shift


def gelu_exact(values):
    return jax.nn.gelu(values, approximate=False)


def matmul(left, right):
    return jnp.dot(left, right, preferred_element_type=jnp.float32)


def left_product(left, right):
    return jnp.einsum("rd,rf->df", left, right, preferred_element_type=jnp.float32)


def right_product(left, right):
    return jnp.einsum("rf,df->rd", left, right, preferred_element_type=jnp.float32)


def column_sums(values):
    return jnp.sum(values.astype(jnp.float32), axis=0)


def unpack(gathered, model_width):
    (
        query_weight,
        query_bias,
        key_weight,
        value_weight,
        value_bias,
        output_weight,
        output_bias,
        attn_gain,
        attn_shift,
        inner_weight,
        inner_bias,
        outer_weight,
        outer_bias,
        ffn_gain,
        ffn_shift,
    ) = gathered
    hidden_width = inner_bias.shape[0]
    return (
        query_weight.reshape(model_width, model_width),
        query_bias,
        key_weight.reshape(model_width, model_width),
        value_weight.reshape(model_width, model_width),
        value_bias,
        output_weight.reshape(model_width, model_width),
        output_bias,
        attn_gain.astype(jnp.float32),
        attn_shift.astype(jnp.float32),
        inner_weight.reshape(model_width, hidden_width),
        inner_bias,
        outer_weight.reshape(hidden_width, model_width),
        outer_bias,
        ffn_gain.astype(jnp.float32),
        ffn_shift.astype(jnp.float32),
    )


def scores_of(query_seq, key_seq, keep_row):
    scores = (
        jnp.einsum("qhd,khd->hqk", query_seq, key_seq, preferred_element_type=jnp.float32) * SCALE
    )
    return jnp.where(keep_row[None, None, :], scores, -1e30)


def attend_forward(seq_item):
    query_seq, key_seq, value_seq, keep_row = seq_item
    scores = scores_of(query_seq, key_seq, keep_row)
    top = jnp.max(scores, axis=-1, keepdims=True)
    shifted_exp = jnp.exp(scores - top)
    total = jnp.sum(shifted_exp, axis=-1, keepdims=True)
    probs = (shifted_exp / total).astype(jnp.bfloat16)
    mixed = jnp.einsum("hqk,khd->qhd", probs, value_seq, preferred_element_type=jnp.float32)
    return (mixed.astype(jnp.bfloat16), (top + jnp.log(total))[..., 0])


def attend_backward(seq_item):
    query_seq, key_seq, value_seq, keep_row, log_total, mixed_grad = seq_item
    scores = scores_of(query_seq, key_seq, keep_row)
    probs = jnp.exp(scores - log_total[..., None])
    value_grad = jnp.einsum(
        "hqk,qhd->khd", probs.astype(jnp.bfloat16), mixed_grad, preferred_element_type=jnp.float32
    )
    prob_grad = jnp.einsum(
        "qhd,khd->hqk", mixed_grad, value_seq, preferred_element_type=jnp.float32
    )
    row_delta = jnp.sum(probs * prob_grad, axis=-1, keepdims=True)
    score_grad = (probs * (prob_grad - row_delta)).astype(jnp.bfloat16)
    query_grad = (
        jnp.einsum("hqk,khd->qhd", score_grad, key_seq, preferred_element_type=jnp.float32) * SCALE
    )
    key_grad = (
        jnp.einsum("hqk,qhd->khd", score_grad, query_seq, preferred_element_type=jnp.float32)
        * SCALE
    )
    return (
        query_grad.astype(jnp.bfloat16),
        key_grad.astype(jnp.bfloat16),
        value_grad.astype(jnp.bfloat16),
    )


def plain_layer(
    tokens,
    lengths,
    query_weight,
    query_bias,
    key_weight,
    value_weight,
    value_bias,
    output_weight,
    output_bias,
    attn_gain,
    attn_shift,
    inner_weight,
    inner_bias,
    outer_weight,
    outer_bias,
    ffn_gain,
    ffn_shift,
    cotangent,
):
    row_count = tokens.shape[0]
    model_width = tokens.shape[1]
    seq_count = lengths.shape[0]
    seq_len = row_count // seq_count
    gathered = (
        lax.all_gather(query_weight, ("wide", "narrow"), axis=0, tiled=True),
        lax.all_gather(query_bias, ("wide", "narrow"), axis=0, tiled=True),
        lax.all_gather(key_weight, ("wide", "narrow"), axis=0, tiled=True),
        lax.all_gather(value_weight, ("wide", "narrow"), axis=0, tiled=True),
        lax.all_gather(value_bias, ("wide", "narrow"), axis=0, tiled=True),
        lax.all_gather(output_weight, ("wide", "narrow"), axis=0, tiled=True),
        lax.all_gather(output_bias, ("wide", "narrow"), axis=0, tiled=True),
        lax.all_gather(attn_gain, ("wide", "narrow"), axis=0, tiled=True),
        lax.all_gather(attn_shift, ("wide", "narrow"), axis=0, tiled=True),
        lax.all_gather(inner_weight, ("wide", "narrow"), axis=0, tiled=True),
        lax.all_gather(inner_bias, ("wide", "narrow"), axis=0, tiled=True),
        lax.all_gather(outer_weight, ("wide", "narrow"), axis=0, tiled=True),
        lax.all_gather(outer_bias, ("wide", "narrow"), axis=0, tiled=True),
        lax.all_gather(ffn_gain, ("wide", "narrow"), axis=0, tiled=True),
        lax.all_gather(ffn_shift, ("wide", "narrow"), axis=0, tiled=True),
    )
    (
        full_qw,
        full_qb,
        full_kw,
        full_vw,
        full_vb,
        full_ow,
        full_ob,
        full_ag,
        full_as,
        full_iw,
        full_ib,
        full_uw,
        full_ub,
        full_fg,
        full_fs,
    ) = unpack(gathered, model_width)
    positions = jnp.arange(seq_len, dtype=jnp.int32)
    keep = positions[None, :] < lengths[:, None]
    row_valid = keep.reshape(row_count, 1).astype(jnp.float32)
    shape_four = (seq_count, seq_len, HEADS, HEAD_DIM)
    queries = (matmul(tokens, full_qw) + full_qb).astype(jnp.bfloat16)
    key_rows = matmul(tokens, full_kw).astype(jnp.bfloat16)
    value_rows = (matmul(tokens, full_vw) + full_vb).astype(jnp.bfloat16)
    query_four = queries.reshape(shape_four)
    key_four = key_rows.reshape(shape_four)
    value_four = value_rows.reshape(shape_four)
    mixed, log_total = lax.map(attend_forward, (query_four, key_four, value_four, keep))
    mixed_flat = mixed.reshape(row_count, model_width)
    resid_one = tokens.astype(jnp.float32) + matmul(mixed_flat, full_ow) + full_ob
    normed_one = layer_norm(resid_one, full_ag, full_as).astype(jnp.bfloat16)
    inner = matmul(normed_one, full_iw) + full_ib
    activ = gelu_exact(inner).astype(jnp.bfloat16)
    resid_two = normed_one.astype(jnp.float32) + matmul(activ, full_uw) + full_ub
    output = (layer_norm(resid_two, full_fg, full_fs) * row_valid).astype(jnp.bfloat16)
    (
        back_qw,
        back_qb,
        back_kw,
        back_vw,
        back_vb,
        back_ow,
        back_ob,
        back_ag,
        back_as,
        back_iw,
        back_ib,
        back_uw,
        back_ub,
        back_fg,
        back_fs,
    ) = unpack(gathered, model_width)
    out_grad = cotangent.astype(jnp.float32) * row_valid
    ignored, pull_two = jax.vjp(layer_norm, resid_two, back_fg, back_fs)
    resid_two_grad, ffn_gain_grad, ffn_shift_grad = pull_two(out_grad)
    outer_grad = resid_two_grad.astype(jnp.bfloat16)
    outer_weight_grad = left_product(activ, outer_grad)
    outer_bias_grad = column_sums(outer_grad)
    activ_grad = right_product(outer_grad, back_uw)
    ignored, pull_gelu = jax.vjp(gelu_exact, inner)
    inner_grad = pull_gelu(activ_grad)[0].astype(jnp.bfloat16)
    inner_weight_grad = left_product(normed_one, inner_grad)
    inner_bias_grad = column_sums(inner_grad)
    normed_grad = resid_two_grad + right_product(inner_grad, back_iw)
    ignored, pull_one = jax.vjp(layer_norm, resid_one, back_ag, back_as)
    resid_one_grad, attn_gain_grad, attn_shift_grad = pull_one(normed_grad)
    attn_grad = resid_one_grad.astype(jnp.bfloat16)
    output_weight_grad = left_product(mixed_flat, attn_grad)
    output_bias_grad = column_sums(attn_grad)
    mixed_grad = right_product(attn_grad, back_ow).astype(jnp.bfloat16)
    query_grad, key_grad, value_grad = lax.map(
        attend_backward,
        (query_four, key_four, value_four, keep, log_total, mixed_grad.reshape(shape_four)),
    )
    query_grad = query_grad.reshape(row_count, model_width)
    key_grad = key_grad.reshape(row_count, model_width)
    value_grad = value_grad.reshape(row_count, model_width)
    query_weight_grad = left_product(tokens, query_grad)
    key_weight_grad = left_product(tokens, key_grad)
    value_weight_grad = left_product(tokens, value_grad)
    query_bias_grad = column_sums(query_grad)
    value_bias_grad = column_sums(value_grad)
    tokens_grad = (
        resid_one_grad
        + right_product(query_grad, back_qw)
        + right_product(key_grad, back_kw)
        + right_product(value_grad, back_vw)
    ).astype(jnp.bfloat16)
    (
        own_qw,
        own_qb,
        own_kw,
        own_vw,
        own_vb,
        own_ow,
        own_ob,
        own_ag,
        own_as,
        own_iw,
        own_ib,
        own_uw,
        own_ub,
        own_fg,
        own_fs,
    ) = (
        lax.psum_scatter(
            query_weight_grad.reshape(-1), ("wide", "narrow"), scatter_dimension=0, tiled=True
        ),
        lax.psum_scatter(query_bias_grad, ("wide", "narrow"), scatter_dimension=0, tiled=True),
        lax.psum_scatter(
            key_weight_grad.reshape(-1), ("wide", "narrow"), scatter_dimension=0, tiled=True
        ),
        lax.psum_scatter(
            value_weight_grad.reshape(-1), ("wide", "narrow"), scatter_dimension=0, tiled=True
        ),
        lax.psum_scatter(value_bias_grad, ("wide", "narrow"), scatter_dimension=0, tiled=True),
        lax.psum_scatter(
            output_weight_grad.reshape(-1), ("wide", "narrow"), scatter_dimension=0, tiled=True
        ),
        lax.psum_scatter(output_bias_grad, ("wide", "narrow"), scatter_dimension=0, tiled=True),
        lax.psum_scatter(attn_gain_grad, ("wide", "narrow"), scatter_dimension=0, tiled=True),
        lax.psum_scatter(attn_shift_grad, ("wide", "narrow"), scatter_dimension=0, tiled=True),
        lax.psum_scatter(
            inner_weight_grad.reshape(-1), ("wide", "narrow"), scatter_dimension=0, tiled=True
        ),
        lax.psum_scatter(inner_bias_grad, ("wide", "narrow"), scatter_dimension=0, tiled=True),
        lax.psum_scatter(
            outer_weight_grad.reshape(-1), ("wide", "narrow"), scatter_dimension=0, tiled=True
        ),
        lax.psum_scatter(outer_bias_grad, ("wide", "narrow"), scatter_dimension=0, tiled=True),
        lax.psum_scatter(ffn_gain_grad, ("wide", "narrow"), scatter_dimension=0, tiled=True),
        lax.psum_scatter(ffn_shift_grad, ("wide", "narrow"), scatter_dimension=0, tiled=True),
    )
    return (
        output,
        tokens_grad,
        own_qw,
        own_qb,
        own_kw,
        own_vw,
        own_vb,
        own_ow,
        own_ob,
        own_ag,
        own_as,
        own_iw,
        own_ib,
        own_uw,
        own_ub,
        own_fg,
        own_fs,
    )


def solution(mesh):
    split = P(AXES)
    rows = P(AXES, None)
    blocked = mesh.shape["wide"] == 8 and mesh.shape["narrow"] == 4
    return jax.shard_map(
        blocked_layer if blocked else plain_layer,
        mesh=mesh,
        in_specs=(rows,) + (split,) * 16 + (rows,),
        out_specs=(rows, rows) + (split,) * 15,
        check_vma=False,
    )
```

```python
import functools

import jax
import jax.numpy as jnp
from jax import lax
from jax.experimental import pallas as pl
from jax.experimental.pallas import tpu as pltpu
from jax.sharding import PartitionSpec as P

HEADS = 12
HEAD_DIM = 64
EPSILON = 1e-06
SCALE = 0.125
AXES = ("wide", "narrow")
SMALL = 128
BIAS_AT = 16
F32 = jnp.float32
BF16 = jnp.bfloat16
NT = (((1,), (1,)), ((), ()))
NN = (((1,), (0,)), ((), ()))
MIB = 1024 * 1024
DECLARED = 5.5e8
TIMES = {
    "pack": 1.3,
    "z_join": 0.3,
    "turn_tokens": 1.0,
    "project": 1.5,
    "attend": 2.0,
    "mix": 3.0,
    "inner": 11.0,
    "outer": 6.0,
    "slope": 3.7,
    "grad_outer": 2.6,
    "normed_back": 5.0,
    "add_halves": 0.5,
    "grad_inner": 3.2,
    "attend_back": 11.4,
    "plane_sum": 0.6,
    "pair_sum": 4.0,
    "stack_small": 0.1,
    "grad_first": 2.0,
    "tokens_back": 5.6,
    "finish": 0.8,
}


def dot(left, right, dims=NN):
    return lax.dot_general(left, right, dims, preferred_element_type=F32)


def vmem():
    return pl.BlockSpec(memory_space=pltpu.VMEM)


def smem():
    return pl.BlockSpec(memory_space=pltpu.SMEM)


def hbm():
    return pl.BlockSpec(memory_space=pltpu.HBM)


def sds(shape, dtype=BF16):
    return jax.ShapeDtypeStruct(shape, dtype)


def call(kernel, name, args, in_specs, out_shape, out_specs=None, scratch=(), limit=32, grid=None, prefetch=0, alias=None):
    many = isinstance(out_shape, (tuple, list))
    if out_specs is None:
        out_specs = tuple(vmem() for _ in out_shape) if many else vmem()
    if grid is None:
        spec = dict(in_specs=in_specs, out_specs=out_specs, scratch_shapes=list(scratch))
    else:
        spec = dict(
            grid_spec=pltpu.PrefetchScalarGridSpec(
                num_scalar_prefetch=prefetch,
                grid=grid,
                in_specs=in_specs,
                out_specs=out_specs,
                scratch_shapes=list(scratch),
            )
        )
    args = [
        pltpu.with_memory_space_constraint(a, pltpu.HBM) if i >= prefetch and in_specs[i - prefetch].memory_space is pltpu.HBM else a
        for i, a in enumerate(args)
    ]
    return pl.pallas_call(
        kernel,
        out_shape=out_shape,
        name=name,
        input_output_aliases=alias or {},
        compiler_params=pltpu.CompilerParams(vmem_limit_bytes=limit * MIB),
        cost_estimate=pl.CostEstimate(flops=int(TIMES[name] * DECLARED), bytes_accessed=0, transcendentals=0),
        **spec,
    )(*args)


def swap(value, mask):
    return lax.ppermute(value, AXES, [(i, i ^ mask) for i in range(32)])


def after(value, *others):
    return lax.optimization_barrier((value,) + others)[0]


def pack_kernel(*refs):
    given, (first, second, third), rest = refs[:15], refs[15:18], refs[18:]
    held, (scr, sems) = rest[:15], rest[15:]
    copies = [pltpu.make_async_copy(src, dst, sems.at[i]) for i, (src, dst) in enumerate(zip(given, held))]
    for copy in copies:
        copy.start()

    def spread(i, dst, col):
        copies[i].wait()
        total = held[i].shape[0]
        rows = dst.shape[0]
        blocks = total // rows
        scr[0:total] = held[i][...].astype(F32)
        for c in range(blocks):
            dst[:, col + c * 128 : col + (c + 1) * 128] = scr[pl.ds(c, rows, stride=blocks), :].astype(BF16)
        return col + blocks * 128

    col = 0
    for i in range(4):
        col = spread(i, first, col)
    for copy in copies[6:]:
        copy.wait()
    rows = first.shape[0]
    lines = [held[6 + i][...].astype(F32).reshape(1, rows) for i in range(8)]
    block = jnp.concatenate(lines, axis=0)
    block = jnp.concatenate([block, jnp.zeros((8, 128 - rows), F32)], axis=1)
    block = jnp.concatenate([block, jnp.zeros((120, 128), F32)], axis=0)
    scr[0:128] = block.T
    wide = held[14][...].astype(F32).reshape(1, 4 * rows)
    scr[0:1, BIAS_AT : BIAS_AT + 4 * rows] = wide
    first[:, col : col + SMALL] = scr[0:rows].astype(BF16)
    spread(4, second, 0)
    spread(5, third, 0)


def pack(weights, vectors, rows, width, hidden):
    flat = [w.reshape(-1, 128) for w in weights]
    ratio = hidden // width
    args = flat + vectors
    return call(
        pack_kernel,
        "pack",
        args,
        [hbm()] * len(args),
        (sds((rows, 4 * width + SMALL)), sds((rows, hidden)), sds((rows * ratio, width))),
        scratch=[pltpu.VMEM(a.shape, BF16) for a in args]
        + [pltpu.VMEM((max(f.shape[0] for f in flat), 128), F32), pltpu.SemaphoreType.DMA((15,))],
        limit=8,
    )


def z_join_kernel(at_ref, a0, a1, a2, a3, out):
    rows = a0.shape[0]
    z = lax.rem(at_ref[0], 4)
    for m, piece in enumerate((a0, a1, a2, a3)):
        out[pl.ds(pl.multiple_of((z ^ m) * rows, 8), rows), :] = piece[...]


def z_swaps(own):
    return [own] + [swap(own, m) for m in (1, 2, 3)]


def z_join(at, pieces):
    rows, cols = pieces[0].shape
    return call(z_join_kernel, "z_join", [at] + pieces, [smem()] + [vmem()] * 4, sds((4 * rows, cols)), limit=8)


def pair_join_kernel(a0, a1, out):
    rows = a0.shape[0]
    out[:rows] = a0[...]
    out[rows:] = a1[...]


def pair_join(own, came):
    rows, cols = own.shape
    return call(pair_join_kernel, "z_join", [own, came], [vmem()] * 2, sds((2 * rows, cols)), limit=4)


def z_join_pairs_kernel(at_ref, a, b, out):
    rows = a.shape[0] // 2
    z = lax.rem(at_ref[0], 4)
    for m in range(4):
        piece = (a, b)[m % 2]
        start = pl.multiple_of((z ^ m) * rows, 8)
        out[pl.ds(start, rows), :] = piece[m // 2 * rows : (m // 2 + 1) * rows]


def z_join_pairs(at, pair, came):
    rows, cols = pair.shape
    return call(z_join_pairs_kernel, "z_join", [at, pair, came], [smem()] + [vmem()] * 2, sds((2 * rows, cols)), limit=8)


def forward_halves(x, y):
    half = x.shape[1] // 256 * 128
    return [swap(x[:, :half], 16), swap(y[:, half:], 8)]


def row_blocks(own, x, y, diag):
    out = []
    for pieces in ([own], [x], [y], diag):
        out += [pieces, [swap(p, 4) for p in pieces]]
    return out


def flat_blocks(blocks):
    return [p for pieces in blocks for p in pieces]


PIECES = 10


def grouped(refs):
    return [[r] for r in refs[:6]] + [list(refs[6:8]), list(refs[8:10])]


def block_copies(at_ref, refs, scr, sems):
    group = at_ref[0] // 4
    lists, k = [], 0
    for m in range(8):
        halves = 2 if m >= 6 else 1
        col, mine = 0, []
        for _ in range(halves):
            rows, cols = refs[k].shape
            start = pl.multiple_of((group ^ m) * rows, 8)
            mine.append(pltpu.make_async_copy(refs[k], scr.at[pl.ds(start, rows), pl.ds(col, cols)], sems.at[k]))
            col += cols
            k += 1
        lists.append(mine)
    return lists


def fetch_all(at_ref, refs, scr, sems):
    lists = block_copies(at_ref, refs, scr, sems)
    for mine in lists:
        for copy in mine:
            copy.start()
    for mine in lists:
        for copy in mine:
            copy.wait()


def store_halves(group, value, keep, send, lead=()):
    part = value.shape[0] // 8
    core = lax.rem(group, 2)
    for b in range(8):
        slot = (group ^ b) // 2
        piece = value[b * part : (b + 1) * part]

        @pl.when(core == b % 2)
        def _():
            keep[lead + (pl.ds(slot, 1),)] = piece[None]

        @pl.when(core != b % 2)
        def _():
            send[lead + (pl.ds(slot, 1),)] = piece[None]


def turned(value):
    return value.astype(F32).T.astype(BF16)


def turn_kernel(at_ref, tokens, keep, send):
    store_halves(at_ref[0] // 4, turned(tokens[...]), keep, send)


def turn_tokens(at, tokens):
    size, width = tokens.shape
    out = sds((4, width // 8, size))
    return call(turn_kernel, "turn_tokens", [at, tokens], [smem(), vmem()], (out, out), limit=8)


def qkv_kernel(at_ref, tokens, *refs):
    pieces, (q, k, v, lines, bias, w_out, scr, sems) = refs[:PIECES], refs[PIECES:]
    width = tokens.shape[1]
    fetch_all(at_ref, pieces, scr, sems)
    w_out[...] = scr[:, 3 * width : 4 * width]
    tails = scr[:, 4 * width :].astype(F32)
    rows = tails.T[:16]
    lines[...] = rows
    each = width // 32
    for d in range(32):
        bias[:, 4 * each * d : 4 * each * (d + 1)] = tails[each * d : each * d + 1, BIAS_AT : BIAS_AT + 4 * each]
    x = tokens[...]
    q[...] = (dot(x, scr[:, :width]) + rows[0:1]).astype(BF16)
    k[...] = dot(x, scr[:, width : 2 * width]).astype(BF16)
    v[...] = (dot(x, scr[:, 2 * width : 3 * width]) + rows[1:2]).astype(BF16)


def project(at, tokens, blocks):
    size, width = tokens.shape
    cols = blocks[0][0].shape[1]
    args = [at, tokens] + flat_blocks(blocks)
    return call(
        qkv_kernel,
        "project",
        args,
        [smem(), vmem()] + [hbm()] * PIECES,
        (sds((size, width)),) * 3 + (sds((16, width), F32), sds((1, 4 * width), F32), sds((width, width))),
        scratch=[pltpu.VMEM((width, cols), BF16), pltpu.SemaphoreType.DMA((PIECES,))],
        limit=14,
    )


def head_lanes(h):
    lane = lax.broadcasted_iota(jnp.int32, (1, 2 * HEAD_DIM), 1)
    return (lane // HEAD_DIM) == h


def attend_kernel(len_ref, q_ref, k_ref, v_ref, mixed_ref, turned_ref, lse_ref):
    length = len_ref[0]
    q, k, v = q_ref[...], k_ref[...], v_ref[...]
    size = q.shape[0]
    keep = lax.broadcasted_iota(jnp.int32, (size, 1), 0) < length
    v_t = turned(v)
    parts = []
    for h in range(2):
        q_head = jnp.where(head_lanes(h), q.astype(F32) * SCALE, 0.0).astype(BF16)
        scores = jnp.where(keep, dot(k, q_head, NT), -1e30)
        top = jnp.max(scores, axis=0, keepdims=True)
        shifted = jnp.exp(scores - top)
        total = jnp.sum(shifted, axis=0, keepdims=True)
        mixed = dot(v_t[h * HEAD_DIM : (h + 1) * HEAD_DIM], shifted.astype(BF16)) / total
        parts.append(mixed)
        lse_ref[0, h : h + 1, :] = top + jnp.log(total)
    mixed = jnp.concatenate(parts, axis=0)
    turned_ref[...] = mixed.astype(BF16)
    mixed_ref[...] = mixed.T.astype(BF16)


def attend(lengths, q, k, v):
    size, width = q.shape
    pairs = width // 128
    tile = pl.BlockSpec((size, 128), lambda i, n: (0, i))
    return call(
        attend_kernel,
        "attend",
        [lengths, q, k, v],
        [tile] * 3,
        (sds((size, width)), sds((width, size)), sds((pairs, 2, size), F32)),
        out_specs=(
            tile,
            pl.BlockSpec((128, size), lambda i, n: (i, 0)),
            pl.BlockSpec((1, 2, size), lambda i, n: (i, 0, 0)),
        ),
        grid=(pairs,),
        prefetch=1,
        limit=12,
    )


def normed(values):
    centred = values - jnp.mean(values, axis=-1, keepdims=True)
    scale = lax.rsqrt(jnp.mean(centred * centred, axis=-1, keepdims=True) + EPSILON)
    return centred * scale, scale


def norm_back(grad, unit, scale):
    return scale * (
        grad - jnp.mean(grad, axis=-1, keepdims=True) - unit * jnp.mean(grad * unit, axis=-1, keepdims=True)
    )


def mix_kernel(at_ref, tokens, mixed, mixed_t, lines, w_out, unit_out, scale_out, normed_out, keep, send):
    group = at_ref[0] // 4
    normed_out[...] = mixed[...]
    step = 128

    def rows(i, carry):
        part = pl.ds(pl.multiple_of(i * step, step), step)
        resid = tokens[part, :].astype(F32) + dot(mixed[part, :], w_out[...]) + lines[2:3]
        unit, scale = normed(resid)
        unit_out[part, :] = unit
        scale_out[part, :] = jnp.broadcast_to(scale, (step, scale_out.shape[1]))
        normed_out[part, :] = (unit * lines[3:4] + lines[4:5]).astype(BF16)
        return carry

    lax.fori_loop(0, tokens.shape[0] // step, rows, 0)
    store_halves(group, mixed_t[...], keep, send, (0,))
    store_halves(group, turned(normed_out[...]), keep, send, (1,))


def mix_stage(at, tokens, mixed, mixed_t, lines, w_out):
    size, width = tokens.shape
    half = sds((2, 4, width // 8, size))
    return call(
        mix_kernel,
        "mix",
        [at, tokens, mixed, mixed_t, lines, w_out],
        [smem()] + [vmem()] * 5,
        (sds((size, width), F32), sds((size, 128), F32), sds((size, width)), half, half),
        limit=10,
    )


def inner_kernel(at_ref, values, bias, *refs):
    pieces = refs[:PIECES]
    (activ, slope, scr, keep, send, sems) = refs[PIECES:]
    part = activ.shape[1] // 8
    group = at_ref[0] // 4
    core = lax.rem(group, 2)
    fetch_all(at_ref, pieces, scr, sems)

    def step(b, carry):
        at = pl.multiple_of(b * part, 128)
        inner = dot(values[...], scr[:, pl.ds(at, part)]) + bias[:, pl.ds(at, part)]
        share = 0.5 * (1.0 + lax.erf(inner * 0.7071067811865476))
        result = inner * share
        activ[:, pl.ds(at, part)] = result.astype(BF16)
        slope[:, pl.ds(at, part)] = (share + inner * (0.3989422804014327 * jnp.exp(-0.5 * inner * inner))).astype(BF16)
        across = result.T.astype(BF16)
        slot = (group ^ b) // 2

        @pl.when(core == lax.rem(b, 2))
        def _():
            keep[pl.ds(slot, 1)] = across[None]

        @pl.when(core != lax.rem(b, 2))
        def _():
            send[pl.ds(slot, 1)] = across[None]

        return carry

    lax.fori_loop(0, 8, step, 0)


def inner_stage(at, values, bias, blocks):
    size, width = values.shape
    hidden = bias.shape[1]
    args = [at, values, bias] + flat_blocks(blocks)
    half = sds((4, hidden // 8, size))
    return call(
        inner_kernel,
        "inner",
        args,
        [smem()] + [vmem()] * 2 + [hbm()] * PIECES,
        (sds((size, hidden)), sds((size, hidden)), sds((width, hidden)), half, half),
        scratch=[pltpu.SemaphoreType.DMA((PIECES,))],
        limit=14,
    )


def outer_kernel(at_ref, len_ref, activ, values, lines, cot, *refs):
    pieces, (output, resid_grad, outer_grad, sums, acc) = refs[:PIECES], refs[PIECES:]
    size = values.shape[0]
    part = activ.shape[1] // 8
    group = at_ref[0] // 4
    resid = values[...].astype(F32) + lines[5:6]
    for m, mine in enumerate(grouped(pieces)):
        given = activ[:, pl.ds(pl.multiple_of((group ^ m) * part, 128), part)]
        products = [dot(given, piece[...]) for piece in mine]
        resid += products[0] if len(products) == 1 else jnp.concatenate(products, axis=1)
    acc[...] = resid
    gain, shift = lines[6:7], lines[7:8]
    sums[...] = jnp.zeros_like(sums)
    step = 128

    def rows(i, carry):
        part = pl.ds(pl.multiple_of(i * step, step), step)
        unit, scale = normed(acc[part, :])
        valid = lax.broadcasted_iota(jnp.int32, (step, 1), 0) + i * step < len_ref[0]
        output[part, :] = jnp.where(valid, unit * gain + shift, 0.0).astype(BF16)
        grad = jnp.where(valid, cot[part, :].astype(F32), 0.0)
        sums[6:7] += jnp.sum(grad * unit, axis=0, keepdims=True)
        sums[7:8] += jnp.sum(grad, axis=0, keepdims=True)
        grad = norm_back(grad * gain, unit, scale)
        resid_grad[part, :] = grad
        rounded = grad.astype(BF16)
        outer_grad[part, :] = rounded
        sums[5:6] += jnp.sum(rounded.astype(F32), axis=0, keepdims=True)
        return carry

    lax.fori_loop(0, size // step, rows, 0)


def outer_stage(at, lengths, activ, values, lines, cot, blocks):
    size, width = values.shape
    hidden = activ.shape[1]
    args = [at, lengths, activ, values, lines, cot] + flat_blocks(blocks)
    return call(
        outer_kernel,
        "outer",
        args,
        [smem(), smem()] + [vmem()] * (4 + PIECES),
        (sds((size, width)), sds((size, width), F32), sds((size, width)), sds((8, width), F32)),
        scratch=[pltpu.VMEM((size, width), F32)],
        limit=10,
    )


def slope_kernel(at_ref, outer_grad, slope, *refs):
    pieces, (inner_grad, sums) = refs[:PIECES], refs[PIECES:]
    part = slope.shape[1] // 8
    group = at_ref[0] // 4
    grad = outer_grad[...]
    for m, mine in enumerate(grouped(pieces)):
        at = pl.multiple_of((group ^ m) * part, 128)
        back, col = 0.0, 0
        for piece in mine:
            cols = piece.shape[1]
            back += dot(grad[:, col : col + cols], piece[...], NT)
            col += cols
        rounded = (back * slope[:, pl.ds(at, part)].astype(F32)).astype(BF16)
        inner_grad[:, pl.ds(at, part)] = rounded
        sums[:, pl.ds(at, part)] = jnp.sum(rounded.astype(F32), axis=0, keepdims=True)


def slope_stage(at, outer_grad, slope, blocks):
    size, width = outer_grad.shape
    hidden = slope.shape[1]
    args = [at, outer_grad, slope] + flat_blocks(blocks)
    return call(
        slope_kernel,
        "slope",
        args,
        [smem()] + [vmem()] * (2 + PIECES),
        (sds((size, hidden)), sds((1, hidden), F32)),
        limit=10,
    )


def normed_back_kernel(inner_grad, resid_two, unit_ref, scale_ref, lines, w_out, weights, resid_grad, attn_low, attn_high, mixed_grad, sums):
    width = unit_ref.shape[1]
    hidden = inner_grad.shape[1]
    grad = resid_two[...]
    for c in range(0, hidden, width):
        grad += dot(inner_grad[:, c : c + width], weights[:, c : c + width], NT)
    half = attn_low.shape[1]
    resid_grad[...] = grad
    sums[...] = jnp.zeros_like(sums)
    step = 128

    def rows(i, carry):
        part = pl.ds(pl.multiple_of(i * step, step), step)
        unit = unit_ref[part, :]
        grad = resid_grad[part, :]
        sums[3:4] += jnp.sum(grad * unit, axis=0, keepdims=True)
        sums[4:5] += jnp.sum(grad, axis=0, keepdims=True)
        grad = norm_back(grad * lines[3:4], unit, scale_ref[part, 0:1])
        resid_grad[part, :] = grad
        rounded = grad.astype(BF16)
        attn_low[part, :] = rounded[:, :half]
        attn_high[part, :] = rounded[:, half:]
        sums[2:3] += jnp.sum(rounded.astype(F32), axis=0, keepdims=True)
        return carry

    lax.fori_loop(0, grad.shape[0] // step, rows, 0)
    back = dot(attn_low[...], w_out[:, :half], NT) + dot(attn_high[...], w_out[:, half:], NT)
    mixed_grad[...] = back.astype(BF16)


def normed_back(inner_grad, resid_two, unit, scale, lines, w_out, weights):
    size, width = unit.shape
    hidden = inner_grad.shape[1]
    args = [inner_grad, resid_two, unit, scale, lines, w_out, weights]
    return call(
        normed_back_kernel,
        "normed_back",
        args,
        [vmem()] * 7,
        (sds((size, width), F32),)
        + (sds((size, width // 2)),) * 2
        + (sds((size, width)), sds((8, width), F32)),
        limit=12,
    )


def attend_back_kernel(len_ref, q_ref, k_ref, v_ref, mixed_ref, grad_ref, lse_ref, grads_ref, qs_ref, vs_ref):
    length = len_ref[0]
    q, k, v, grad = q_ref[...], k_ref[...], v_ref[...], grad_ref[...]
    size = q.shape[0]
    keep = lax.broadcasted_iota(jnp.int32, (size, 1), 0) < length
    k_t = turned(k)
    prod_t = turned(grad).astype(F32) * mixed_ref[...].astype(F32)
    q_grad, k_grad, v_grad = [], 0.0, 0.0
    for h in range(2):
        mine = head_lanes(h)
        q_head = jnp.where(mine, q.astype(F32) * SCALE, 0.0).astype(BF16)
        g_head = jnp.where(mine, grad, jnp.zeros_like(grad))
        scores = jnp.where(keep, dot(k, q_head, NT), -1e30)
        probs = jnp.exp(scores - lse_ref[0, h : h + 1, :])
        delta = jnp.sum(prod_t[h * HEAD_DIM : (h + 1) * HEAD_DIM], axis=0, keepdims=True)
        prob_grad = dot(v, g_head, NT)
        score_grad = (probs * (prob_grad - delta)).astype(BF16)
        v_grad += dot(probs.astype(BF16), g_head)
        k_grad += dot(score_grad, q_head)
        q_grad.append(dot(k_t[h * HEAD_DIM : (h + 1) * HEAD_DIM], score_grad))
    q_rounded = (jnp.concatenate(q_grad, axis=0) * SCALE).T.astype(BF16)
    v_rounded = v_grad.astype(BF16)
    grads_ref[0] = q_rounded
    grads_ref[1] = k_grad.astype(BF16)
    grads_ref[2] = v_rounded
    qs_ref[...] = jnp.sum(q_rounded.astype(F32), axis=0, keepdims=True)
    vs_ref[...] = jnp.sum(v_rounded.astype(F32), axis=0, keepdims=True)


def attend_back(lengths, q, k, v, mixed_t, grad, lse):
    size, width = q.shape
    pairs = width // 128
    tile = pl.BlockSpec((size, 128), lambda i, n: (0, i))
    out = pl.BlockSpec((3, size, 128), lambda i, n: (0, 0, i))
    line = pl.BlockSpec((1, 128), lambda i, n: (0, i))
    return call(
        attend_back_kernel,
        "attend_back",
        [lengths, q, k, v, mixed_t, grad, lse],
        [tile] * 3
        + [
            pl.BlockSpec((128, size), lambda i, n: (i, 0)),
            tile,
            pl.BlockSpec((1, 2, size), lambda i, n: (i, 0, 0)),
        ],
        (sds((3, size, width)),) + (sds((1, width), F32),) * 2,
        out_specs=(out,) + (line,) * 2,
        grid=(pairs,),
        prefetch=1,
        limit=12,
    )


def tokens_kernel(at_ref, resid_grad, *refs):
    grads, pieces, (out, scr, sems) = refs[0], refs[1 : 1 + PIECES], refs[1 + PIECES :]
    width = resid_grad.shape[1]
    fetch_all(at_ref, pieces, scr, sems)
    total = resid_grad[...]
    for i in range(3):
        total += dot(grads[i], scr[:, i * width : (i + 1) * width], NT)
    out[...] = total.astype(BF16)


def tokens_back(at, resid_grad, grads, blocks):
    size, width = resid_grad.shape
    cols = blocks[0][0].shape[1]
    args = [at, resid_grad, grads] + flat_blocks(blocks)
    return call(
        tokens_kernel,
        "tokens_back",
        args,
        [smem()] + [vmem()] * 2 + [hbm()] * PIECES,
        sds((size, width)),
        scratch=[pltpu.VMEM((width, cols), BF16), pltpu.SemaphoreType.DMA((PIECES,))],
        limit=14,
    )


def small_kernel(one, two, q_sum, v_sum, bias, out):
    width = one.shape[1]
    out[0:8] = one[...] + two[...]
    out[8:16] = jnp.zeros((8, width), F32)
    out[0:1], out[1:2] = q_sum[...], v_sum[...]
    for r in range(4):
        out[12 + r : 13 + r] = bias[:, r * width : (r + 1) * width]


def stack_small(*args):
    one = args[0]
    return call(small_kernel, "stack_small", list(args), [vmem()] * 5, sds((16, one.shape[1]), F32), limit=4)


def put_slots(value, col, outs):
    s0, s1, s2, s3a, s3b = outs
    part, cols = s0.shape
    half = s3a.shape[1]
    width = value.shape[1]
    for s, out in enumerate((s0, s1, s2)):
        out[:, col : col + width] = value[s * part : (s + 1) * part]
    last = value[3 * part : 4 * part]
    cut = min(max(half - col, 0), width)
    if cut > 0:
        s3a[:, col : col + cut] = last[:, :cut]
    if cut < width:
        s3b[:, col + cut - half : col + width - half] = last[:, cut:]


def slot_shapes(part, cols):
    half = cols // 256 * 128
    return (sds((part, cols)),) * 3 + (sds((part, half)), sds((part, cols - half)))


def grad_kernel(plan, small, *refs):
    outs = refs[-5:]
    if small:
        outs, scr = refs[-6:-1], refs[-1]
    part = outs[0].shape[0]
    col = 0
    for left, lead, mine, came, which in plan:
        rows = 4 * part
        size = refs[left].shape[-1]
        a = refs[left][lead] if lead is not None else refs[left][...]
        b = refs[left + 1][lead] if lead is not None else refs[left + 1][...]
        a, b = a.reshape(rows, size), b.reshape(rows, size)
        total = refs[mine].shape[-1]
        step = min(total, 768)
        for start in range(0, total, step):
            at = which + (slice(None), slice(start, start + step))
            value = dot(a, refs[mine][at]) + dot(b, refs[came][at])
            put_slots(value.astype(BF16), col, outs)
            col += step
    if small:
        at_ref, own, came = refs[small], refs[small + 1], refs[small + 2]
        both = own[...] + came[...]
        padded = jnp.concatenate([both, jnp.zeros((SMALL - both.shape[0], both.shape[1]), F32)], axis=0)
        scr[...] = padded.T
        each = 4 * scr.shape[0] // 32
        wide = scr.shape[0]
        for d in range(32):
            row, lane = 12 + each * d // wide, each * d % wide
            scr[wide // 32 * d : wide // 32 * d + 1, BIAS_AT : BIAS_AT + each] = both[row : row + 1, lane : lane + each]
        group = at_ref[0] // 4
        value = jnp.concatenate(
            [scr[pl.ds(pl.multiple_of((group ^ (2 * s)) * part, 8), part), :] for s in range(4)], axis=0
        )
        put_slots(value.astype(BF16), col, outs)


def weight_grad(name, args, plan, part, cols, small=None):
    specs = [vmem()] * len(args)
    scratch = []
    if small:
        specs[small] = smem()
        scratch = [pltpu.VMEM((8 * part, SMALL), F32)]
    return call(
        functools.partial(grad_kernel, plan, small),
        name,
        args,
        specs,
        slot_shapes(part, cols),
        scratch=scratch,
        limit=14,
    )


def add_kernel(x_ref, p_ref, y_ref, q_ref, x_out, y_out):
    x_out[...] = (x_ref[...].astype(F32) + p_ref[...].astype(F32)).astype(BF16)
    y_out[...] = (y_ref[...].astype(F32) + q_ref[...].astype(F32)).astype(BF16)


def add_halves(x, p, y, q):
    part, cols = x.shape
    half = p.shape[1]
    rest = cols - half
    if half != rest:
        return add_uneven(x, p, y, q)
    low = pl.BlockSpec((part, half), lambda i: (0, 0))
    high = pl.BlockSpec((part, half), lambda i: (0, 1))
    return call(
        add_kernel,
        "add_halves",
        [x, p, y, q],
        [low, low, high, low],
        (sds(x.shape), sds(y.shape)),
        out_specs=(low, high),
        grid=(1,),
        alias={0: 0, 2: 1},
        limit=16,
    )


def uneven_kernel(x_ref, p_ref, y_ref, q_ref, x_out, y_out):
    half = p_ref.shape[1]
    x_out[...] = x_ref[...]
    y_out[...] = y_ref[...]
    x_out[:, :half] = (x_ref[:, :half].astype(F32) + p_ref[...].astype(F32)).astype(BF16)
    y_out[:, half:] = (y_ref[:, half:].astype(F32) + q_ref[...].astype(F32)).astype(BF16)


def add_uneven(x, p, y, q):
    return call(
        uneven_kernel,
        "add_halves",
        [x, p, y, q],
        [vmem()] * 4,
        (sds(x.shape), sds(y.shape)),
        limit=16,
    )


def plane_sum_kernel(at_ref, a0, a1, a2, keep, send, total):
    total[...] = a0[...].astype(F32) + (a1[...].astype(F32) + a2[...].astype(F32))
    rows = keep.shape[0] // 2
    z = lax.rem(at_ref[0], 4)
    for m in range(4):
        out = (keep, send)[m // 2]
        part = total[pl.ds(pl.multiple_of((z ^ m) * rows, 8), rows), :]
        out[m % 2 * rows : (m % 2 + 1) * rows] = part.astype(BF16)


def plane_sum(at, pieces):
    part, cols = pieces[0].shape
    return call(
        plane_sum_kernel,
        "plane_sum",
        [at] + pieces,
        [smem()] + [vmem()] * 3,
        (sds((part // 2, cols)),) * 2,
        scratch=[pltpu.VMEM((part, cols), F32)],
        limit=6,
    )


def pair_sum_kernel(keep, came, own, send):
    rows = own.shape[0]
    total = keep[...].astype(F32) + came[...].astype(F32)
    own[...] = total[:rows]
    send[...] = total[rows:].astype(BF16)


def pair_sum(keep, came):
    rows, cols = keep.shape[0] // 2, keep.shape[1]
    return call(
        pair_sum_kernel,
        "pair_sum",
        [keep, came],
        [vmem()] * 2,
        (sds((rows, cols), F32), sds((rows, cols))),
        limit=8,
    )


def finish_kernel(widths, tail, own, came, *outs):
    total = own[...] + came[...].astype(F32)
    rows = total.shape[0]
    col = 0
    for width, out in zip(widths, outs):
        blocks = width // 128
        for c in range(blocks):
            out[pl.ds(c, rows, stride=blocks), :] = total[:, col + c * 128 : col + (c + 1) * 128]
        col += width
    if tail:
        block = jnp.concatenate([total[:, col : col + SMALL], jnp.zeros((SMALL - rows, SMALL), F32)], axis=0).T
        for i in range(8):
            outs[len(widths) + i][...] = block[i : i + 1, :rows].reshape(rows)
        outs[len(widths) + 8][...] = total[0:1, col + BIAS_AT : col + BIAS_AT + 4 * rows].reshape(4 * rows)


def finish(pieces, widths, tail=False):
    rows = pieces[0].shape[0]
    shapes = [sds((rows * w // 128, 128), F32) for w in widths]
    if tail:
        shapes += [sds((rows,), F32)] * 8 + [sds((4 * rows,), F32)]
    outs = call(
        functools.partial(finish_kernel, widths, tail),
        "finish",
        pieces,
        [vmem()] * 2,
        tuple(shapes),
        limit=6,
    )
    return [o.reshape(-1) for o in outs]


def scatter_plane(slots, *done):
    s0, s1, s2, s3a, s3b = slots
    p, q = swap(s3a, 16), swap(s3b, 8)
    s1 = after(s1, *done)
    x, y = add_halves(s1, p, s2, q)
    return [s0, swap(x, 8), swap(y, 16), x]


def first_z(sums, *done):
    keep, send = sums
    return pair_sum(after(keep, *done), swap(send, 2))


def blocked_layer(
    tokens,
    lengths,
    query_weight,
    query_bias,
    key_weight,
    value_weight,
    value_bias,
    output_weight,
    output_bias,
    attn_gain,
    attn_shift,
    inner_weight,
    inner_bias,
    outer_weight,
    outer_bias,
    ffn_gain,
    ffn_shift,
    cotangent,
):
    size, width = tokens.shape
    rows = query_weight.shape[0] // width
    hidden = inner_weight.shape[0] // rows
    ratio = hidden // width
    at = lax.axis_index(AXES).astype(jnp.int32).reshape(1)

    first, second, third = pack(
        [query_weight, key_weight, value_weight, output_weight, inner_weight, outer_weight],
        [query_bias, value_bias, output_bias, attn_gain, attn_shift, outer_bias, ffn_gain, ffn_shift, inner_bias],
        rows,
        width,
        hidden,
    )
    z_first = z_join(at, z_swaps(first))
    x_first, y_first = swap(z_first, 8), swap(z_first, 16)
    second = after(second, z_first)
    second = pair_join(second, swap(second, 2))
    x_first, second = lax.optimization_barrier((x_first, second))
    f_first = forward_halves(x_first, y_first)
    first_blocks = row_blocks(z_first, x_first, y_first, f_first)
    z_second = z_join_pairs(at, second, swap(second, 1))
    x_second, y_second = swap(z_second, 8), swap(z_second, 16)
    third = after(third, z_second)
    third_came = swap(third, 2)

    tok_keep, tok_send = turn_tokens(at, tokens)
    tok_came = swap(tok_send, 4)
    queries, key_rows, value_rows, lines, bias, w_out = project(at, tokens, first_blocks)
    third = pair_join(third, after(third_came, queries))
    queries = after(queries, third)
    mixed, mixed_t, lse = attend(lengths, queries, key_rows, value_rows)
    mixed, x_second, y_second = lax.optimization_barrier((mixed, x_second, y_second))
    f_second = forward_halves(x_second, y_second)
    unit, scale, values, b_keep, b_send = mix_stage(at, tokens, after(mixed, tok_came), mixed_t, lines, w_out)
    b_came = swap(b_send, 4)
    second_blocks = row_blocks(z_second, x_second, y_second, [after(f, values) for f in f_second])
    z_third = z_join_pairs(at, third, after(swap(third, 1), *f_second))
    x_third, y_third = swap(z_third, 8), swap(z_third, 16)
    activ, slope, w_inner, a_keep, a_send = inner_stage(at, after(values, z_third), bias, second_blocks)
    activ, x_third, y_third = lax.optimization_barrier((activ, x_third, y_third))
    f_third = forward_halves(x_third, y_third)
    third_blocks = row_blocks(z_third, x_third, y_third, f_third)
    a_came = swap(after(a_send, x_third), 4)
    activ = after(activ, a_came)
    output, resid_two_grad, outer_grad, sums_two = outer_stage(at, lengths, activ, values, lines, cotangent, third_blocks)

    outer_came = swap(outer_grad, 4)
    inner_grad, bias_grad = slope_stage(at, outer_grad, slope, third_blocks)
    inner_came = swap(after(inner_grad, outer_came), 4)
    slots_a = weight_grad(
        "grad_outer",
        [a_keep, a_came, outer_grad, after(outer_came, inner_grad)],
        [(0, None, 2, 3, ())],
        hidden // 8,
        width,
    )
    resid_one_grad, attn_low, attn_high, mixed_grad, sums_one = normed_back(
        after(inner_grad, slots_a[0]), resid_two_grad, unit, scale, lines, w_out, w_inner
    )
    plane_a = scatter_plane(slots_a, attn_low)
    low_came, high_came = (swap(after(g, plane_a[3]), 4) for g in (attn_low, attn_high))
    slots_b = weight_grad(
        "grad_inner",
        [b_keep, b_came, attn_low, low_came, attn_high, high_came, inner_grad, inner_came],
        [(0, 0, 2, 3, ()), (0, 0, 4, 5, ()), (0, 1, 6, 7, ())],
        width // 8,
        width + hidden,
    )
    grads, q_sum, v_sum = attend_back(
        lengths, queries, key_rows, value_rows, mixed_t, after(mixed_grad, slots_b[0]), lse
    )
    plane_b = scatter_plane(slots_b, grads)
    sums_a = plane_sum(at, [after(plane_a[0], plane_b[3])] + plane_a[1:3])
    grads_came = swap(after(grads, sums_a[0]), 4)
    small = stack_small(sums_one, sums_two, q_sum, v_sum, bias_grad)
    small_came = swap(small, 4)
    args = [tok_keep, tok_came, grads, grads_came]
    plan = [(0, None, 2, 3, (i,)) for i in range(3)]
    slots_c = weight_grad(
        "grad_first",
        args + [at, small, small_came],
        plan,
        width // 8,
        3 * width + SMALL,
        small=len(args),
    )
    tokens_grad = tokens_back(at, after(resid_one_grad, slots_c[0]), grads, first_blocks)
    own_a, last_a = first_z(sums_a, tokens_grad)
    slots_c = list(slots_c)
    slots_c[3], slots_c[4], _ = lax.optimization_barrier((slots_c[3], slots_c[4], own_a))
    sums_b = plane_sum(at, [after(plane_b[0], own_a)] + plane_b[1:3])
    plane_c = scatter_plane(slots_c, sums_b[0])
    (own_u,) = finish([own_a, swap(after(last_a, sums_b[0]), 1)], [width])
    own_b, last_b = first_z(sums_b)
    sums_c = plane_sum(at, [after(plane_c[0], own_b)] + plane_c[1:3])
    own_o, own_i = finish([own_b, swap(last_b, 1)], [width, hidden])
    own_c, last_c = first_z(sums_c)
    own_q, own_k, own_v, qb, vb, ob, ag, ash, ub, fg, fs, ib = finish(
        [own_c, swap(last_c, 1)], [width] * 3, tail=True
    )
    return (output, tokens_grad, own_q, qb, own_k, own_v, vb, own_o, ob, ag, ash, own_i, ib, own_u, ub, fg, fs)


def layer_norm(values, norm_gain, norm_shift):
    row_mean = jnp.mean(values, axis=-1, keepdims=True)
    centred = values - row_mean
    row_var = jnp.mean(centred * centred, axis=-1, keepdims=True)
    return centred * lax.rsqrt(row_var + EPSILON) * norm_gain + norm_shift


def gelu_exact(values):
    return jax.nn.gelu(values, approximate=False)


def matmul(left, right):
    return jnp.dot(left, right, preferred_element_type=jnp.float32)


def left_product(left, right):
    return jnp.einsum("rd,rf->df", left, right, preferred_element_type=jnp.float32)


def right_product(left, right):
    return jnp.einsum("rf,df->rd", left, right, preferred_element_type=jnp.float32)


def column_sums(values):
    return jnp.sum(values.astype(jnp.float32), axis=0)


def unpack(gathered, model_width):
    (
        query_weight,
        query_bias,
        key_weight,
        value_weight,
        value_bias,
        output_weight,
        output_bias,
        attn_gain,
        attn_shift,
        inner_weight,
        inner_bias,
        outer_weight,
        outer_bias,
        ffn_gain,
        ffn_shift,
    ) = gathered
    hidden_width = inner_bias.shape[0]
    return (
        query_weight.reshape(model_width, model_width),
        query_bias,
        key_weight.reshape(model_width, model_width),
        value_weight.reshape(model_width, model_width),
        value_bias,
        output_weight.reshape(model_width, model_width),
        output_bias,
        attn_gain.astype(jnp.float32),
        attn_shift.astype(jnp.float32),
        inner_weight.reshape(model_width, hidden_width),
        inner_bias,
        outer_weight.reshape(hidden_width, model_width),
        outer_bias,
        ffn_gain.astype(jnp.float32),
        ffn_shift.astype(jnp.float32),
    )


def scores_of(query_seq, key_seq, keep_row):
    scores = (
        jnp.einsum("qhd,khd->hqk", query_seq, key_seq, preferred_element_type=jnp.float32) * SCALE
    )
    return jnp.where(keep_row[None, None, :], scores, -1e30)


def attend_forward(seq_item):
    query_seq, key_seq, value_seq, keep_row = seq_item
    scores = scores_of(query_seq, key_seq, keep_row)
    top = jnp.max(scores, axis=-1, keepdims=True)
    shifted_exp = jnp.exp(scores - top)
    total = jnp.sum(shifted_exp, axis=-1, keepdims=True)
    probs = (shifted_exp / total).astype(jnp.bfloat16)
    mixed = jnp.einsum("hqk,khd->qhd", probs, value_seq, preferred_element_type=jnp.float32)
    return (mixed.astype(jnp.bfloat16), (top + jnp.log(total))[..., 0])


def attend_backward(seq_item):
    query_seq, key_seq, value_seq, keep_row, log_total, mixed_grad = seq_item
    scores = scores_of(query_seq, key_seq, keep_row)
    probs = jnp.exp(scores - log_total[..., None])
    value_grad = jnp.einsum(
        "hqk,qhd->khd", probs.astype(jnp.bfloat16), mixed_grad, preferred_element_type=jnp.float32
    )
    prob_grad = jnp.einsum(
        "qhd,khd->hqk", mixed_grad, value_seq, preferred_element_type=jnp.float32
    )
    row_delta = jnp.sum(probs * prob_grad, axis=-1, keepdims=True)
    score_grad = (probs * (prob_grad - row_delta)).astype(jnp.bfloat16)
    query_grad = (
        jnp.einsum("hqk,khd->qhd", score_grad, key_seq, preferred_element_type=jnp.float32) * SCALE
    )
    key_grad = (
        jnp.einsum("hqk,qhd->khd", score_grad, query_seq, preferred_element_type=jnp.float32)
        * SCALE
    )
    return (
        query_grad.astype(jnp.bfloat16),
        key_grad.astype(jnp.bfloat16),
        value_grad.astype(jnp.bfloat16),
    )


def plain_layer(
    tokens,
    lengths,
    query_weight,
    query_bias,
    key_weight,
    value_weight,
    value_bias,
    output_weight,
    output_bias,
    attn_gain,
    attn_shift,
    inner_weight,
    inner_bias,
    outer_weight,
    outer_bias,
    ffn_gain,
    ffn_shift,
    cotangent,
):
    row_count = tokens.shape[0]
    model_width = tokens.shape[1]
    seq_count = lengths.shape[0]
    seq_len = row_count // seq_count
    gathered = (
        lax.all_gather(query_weight, ("wide", "narrow"), axis=0, tiled=True),
        lax.all_gather(query_bias, ("wide", "narrow"), axis=0, tiled=True),
        lax.all_gather(key_weight, ("wide", "narrow"), axis=0, tiled=True),
        lax.all_gather(value_weight, ("wide", "narrow"), axis=0, tiled=True),
        lax.all_gather(value_bias, ("wide", "narrow"), axis=0, tiled=True),
        lax.all_gather(output_weight, ("wide", "narrow"), axis=0, tiled=True),
        lax.all_gather(output_bias, ("wide", "narrow"), axis=0, tiled=True),
        lax.all_gather(attn_gain, ("wide", "narrow"), axis=0, tiled=True),
        lax.all_gather(attn_shift, ("wide", "narrow"), axis=0, tiled=True),
        lax.all_gather(inner_weight, ("wide", "narrow"), axis=0, tiled=True),
        lax.all_gather(inner_bias, ("wide", "narrow"), axis=0, tiled=True),
        lax.all_gather(outer_weight, ("wide", "narrow"), axis=0, tiled=True),
        lax.all_gather(outer_bias, ("wide", "narrow"), axis=0, tiled=True),
        lax.all_gather(ffn_gain, ("wide", "narrow"), axis=0, tiled=True),
        lax.all_gather(ffn_shift, ("wide", "narrow"), axis=0, tiled=True),
    )
    (
        full_qw,
        full_qb,
        full_kw,
        full_vw,
        full_vb,
        full_ow,
        full_ob,
        full_ag,
        full_as,
        full_iw,
        full_ib,
        full_uw,
        full_ub,
        full_fg,
        full_fs,
    ) = unpack(gathered, model_width)
    positions = jnp.arange(seq_len, dtype=jnp.int32)
    keep = positions[None, :] < lengths[:, None]
    row_valid = keep.reshape(row_count, 1).astype(jnp.float32)
    shape_four = (seq_count, seq_len, HEADS, HEAD_DIM)
    queries = (matmul(tokens, full_qw) + full_qb).astype(jnp.bfloat16)
    key_rows = matmul(tokens, full_kw).astype(jnp.bfloat16)
    value_rows = (matmul(tokens, full_vw) + full_vb).astype(jnp.bfloat16)
    query_four = queries.reshape(shape_four)
    key_four = key_rows.reshape(shape_four)
    value_four = value_rows.reshape(shape_four)
    mixed, log_total = lax.map(attend_forward, (query_four, key_four, value_four, keep))
    mixed_flat = mixed.reshape(row_count, model_width)
    resid_one = tokens.astype(jnp.float32) + matmul(mixed_flat, full_ow) + full_ob
    normed_one = layer_norm(resid_one, full_ag, full_as).astype(jnp.bfloat16)
    inner = matmul(normed_one, full_iw) + full_ib
    activ = gelu_exact(inner).astype(jnp.bfloat16)
    resid_two = normed_one.astype(jnp.float32) + matmul(activ, full_uw) + full_ub
    output = (layer_norm(resid_two, full_fg, full_fs) * row_valid).astype(jnp.bfloat16)
    (
        back_qw,
        back_qb,
        back_kw,
        back_vw,
        back_vb,
        back_ow,
        back_ob,
        back_ag,
        back_as,
        back_iw,
        back_ib,
        back_uw,
        back_ub,
        back_fg,
        back_fs,
    ) = unpack(gathered, model_width)
    out_grad = cotangent.astype(jnp.float32) * row_valid
    ignored, pull_two = jax.vjp(layer_norm, resid_two, back_fg, back_fs)
    resid_two_grad, ffn_gain_grad, ffn_shift_grad = pull_two(out_grad)
    outer_grad = resid_two_grad.astype(jnp.bfloat16)
    outer_weight_grad = left_product(activ, outer_grad)
    outer_bias_grad = column_sums(outer_grad)
    activ_grad = right_product(outer_grad, back_uw)
    ignored, pull_gelu = jax.vjp(gelu_exact, inner)
    inner_grad = pull_gelu(activ_grad)[0].astype(jnp.bfloat16)
    inner_weight_grad = left_product(normed_one, inner_grad)
    inner_bias_grad = column_sums(inner_grad)
    normed_grad = resid_two_grad + right_product(inner_grad, back_iw)
    ignored, pull_one = jax.vjp(layer_norm, resid_one, back_ag, back_as)
    resid_one_grad, attn_gain_grad, attn_shift_grad = pull_one(normed_grad)
    attn_grad = resid_one_grad.astype(jnp.bfloat16)
    output_weight_grad = left_product(mixed_flat, attn_grad)
    output_bias_grad = column_sums(attn_grad)
    mixed_grad = right_product(attn_grad, back_ow).astype(jnp.bfloat16)
    query_grad, key_grad, value_grad = lax.map(
        attend_backward,
        (query_four, key_four, value_four, keep, log_total, mixed_grad.reshape(shape_four)),
    )
    query_grad = query_grad.reshape(row_count, model_width)
    key_grad = key_grad.reshape(row_count, model_width)
    value_grad = value_grad.reshape(row_count, model_width)
    query_weight_grad = left_product(tokens, query_grad)
    key_weight_grad = left_product(tokens, key_grad)
    value_weight_grad = left_product(tokens, value_grad)
    query_bias_grad = column_sums(query_grad)
    value_bias_grad = column_sums(value_grad)
    tokens_grad = (
        resid_one_grad
        + right_product(query_grad, back_qw)
        + right_product(key_grad, back_kw)
        + right_product(value_grad, back_vw)
    ).astype(jnp.bfloat16)
    (
        own_qw,
        own_qb,
        own_kw,
        own_vw,
        own_vb,
        own_ow,
        own_ob,
        own_ag,
        own_as,
        own_iw,
        own_ib,
        own_uw,
        own_ub,
        own_fg,
        own_fs,
    ) = (
        lax.psum_scatter(
            query_weight_grad.reshape(-1), ("wide", "narrow"), scatter_dimension=0, tiled=True
        ),
        lax.psum_scatter(query_bias_grad, ("wide", "narrow"), scatter_dimension=0, tiled=True),
        lax.psum_scatter(
            key_weight_grad.reshape(-1), ("wide", "narrow"), scatter_dimension=0, tiled=True
        ),
        lax.psum_scatter(
            value_weight_grad.reshape(-1), ("wide", "narrow"), scatter_dimension=0, tiled=True
        ),
        lax.psum_scatter(value_bias_grad, ("wide", "narrow"), scatter_dimension=0, tiled=True),
        lax.psum_scatter(
            output_weight_grad.reshape(-1), ("wide", "narrow"), scatter_dimension=0, tiled=True
        ),
        lax.psum_scatter(output_bias_grad, ("wide", "narrow"), scatter_dimension=0, tiled=True),
        lax.psum_scatter(attn_gain_grad, ("wide", "narrow"), scatter_dimension=0, tiled=True),
        lax.psum_scatter(attn_shift_grad, ("wide", "narrow"), scatter_dimension=0, tiled=True),
        lax.psum_scatter(
            inner_weight_grad.reshape(-1), ("wide", "narrow"), scatter_dimension=0, tiled=True
        ),
        lax.psum_scatter(inner_bias_grad, ("wide", "narrow"), scatter_dimension=0, tiled=True),
        lax.psum_scatter(
            outer_weight_grad.reshape(-1), ("wide", "narrow"), scatter_dimension=0, tiled=True
        ),
        lax.psum_scatter(outer_bias_grad, ("wide", "narrow"), scatter_dimension=0, tiled=True),
        lax.psum_scatter(ffn_gain_grad, ("wide", "narrow"), scatter_dimension=0, tiled=True),
        lax.psum_scatter(ffn_shift_grad, ("wide", "narrow"), scatter_dimension=0, tiled=True),
    )
    return (
        output,
        tokens_grad,
        own_qw,
        own_qb,
        own_kw,
        own_vw,
        own_vb,
        own_ow,
        own_ob,
        own_ag,
        own_as,
        own_iw,
        own_ib,
        own_uw,
        own_ub,
        own_fg,
        own_fs,
    )


def solution(mesh):
    split = P(AXES)
    rows = P(AXES, None)
    blocked = mesh.shape["wide"] == 8 and mesh.shape["narrow"] == 4
    return jax.shard_map(
        blocked_layer if blocked else plain_layer,
        mesh=mesh,
        in_specs=(rows,) + (split,) * 16 + (rows,),
        out_specs=(rows, rows) + (split,) * 15,
        check_vma=False,
    )
```

```python
import functools

import jax
import jax.numpy as jnp
from jax import lax
from jax.experimental import pallas as pl
from jax.experimental.pallas import tpu as pltpu
from jax.sharding import PartitionSpec as P

HEADS = 12
HEAD_DIM = 64
EPSILON = 1e-06
SCALE = 0.125
AXES = ("wide", "narrow")
SMALL = 128
BIAS_AT = 16
F32 = jnp.float32
BF16 = jnp.bfloat16
NT = (((1,), (1,)), ((), ()))
NN = (((1,), (0,)), ((), ()))
MIB = 1024 * 1024
DECLARED = 5.5e8
TIMES = {
    "pack": 1.3,
    "z_join": 0.3,
    "turn_tokens": 1.0,
    "project": 1.5,
    "attend": 2.0,
    "mix": 3.0,
    "inner": 9.0,
    "outer": 6.0,
    "slope": 3.7,
    "grad_outer": 2.6,
    "normed_back": 5.0,
    "add_halves": 0.5,
    "grad_inner": 3.2,
    "attend_back": 11.4,
    "plane_sum": 0.6,
    "pair_sum": 4.0,
    "stack_small": 0.1,
    "grad_first": 2.0,
    "tokens_back": 5.6,
    "finish": 0.8,
}


def dot(left, right, dims=NN):
    return lax.dot_general(left, right, dims, preferred_element_type=F32)


def vmem():
    return pl.BlockSpec(memory_space=pltpu.VMEM)


def smem():
    return pl.BlockSpec(memory_space=pltpu.SMEM)


def hbm():
    return pl.BlockSpec(memory_space=pltpu.HBM)


def sds(shape, dtype=BF16):
    return jax.ShapeDtypeStruct(shape, dtype)


def call(kernel, name, args, in_specs, out_shape, out_specs=None, scratch=(), limit=32, grid=None, prefetch=0, alias=None):
    many = isinstance(out_shape, (tuple, list))
    if out_specs is None:
        out_specs = tuple(vmem() for _ in out_shape) if many else vmem()
    if grid is None:
        spec = dict(in_specs=in_specs, out_specs=out_specs, scratch_shapes=list(scratch))
    else:
        spec = dict(
            grid_spec=pltpu.PrefetchScalarGridSpec(
                num_scalar_prefetch=prefetch,
                grid=grid,
                in_specs=in_specs,
                out_specs=out_specs,
                scratch_shapes=list(scratch),
            )
        )
    args = [
        pltpu.with_memory_space_constraint(a, pltpu.HBM) if i >= prefetch and in_specs[i - prefetch].memory_space is pltpu.HBM else a
        for i, a in enumerate(args)
    ]
    return pl.pallas_call(
        kernel,
        out_shape=out_shape,
        name=name,
        input_output_aliases=alias or {},
        compiler_params=pltpu.CompilerParams(vmem_limit_bytes=limit * MIB),
        cost_estimate=pl.CostEstimate(flops=int(TIMES[name] * DECLARED), bytes_accessed=0, transcendentals=0),
        **spec,
    )(*args)


def swap(value, mask):
    return lax.ppermute(value, AXES, [(i, i ^ mask) for i in range(32)])


def after(value, *others):
    return lax.optimization_barrier((value,) + others)[0]


def pack_kernel(*refs):
    given, (first, second, third), rest = refs[:15], refs[15:18], refs[18:]
    held, (scr, sems) = rest[:15], rest[15:]
    copies = [pltpu.make_async_copy(src, dst, sems.at[i]) for i, (src, dst) in enumerate(zip(given, held))]
    for copy in copies:
        copy.start()

    def spread(i, dst, col):
        copies[i].wait()
        total = held[i].shape[0]
        rows = dst.shape[0]
        blocks = total // rows
        scr[0:total] = held[i][...].astype(F32)
        for c in range(blocks):
            dst[:, col + c * 128 : col + (c + 1) * 128] = scr[pl.ds(c, rows, stride=blocks), :].astype(BF16)
        return col + blocks * 128

    col = 0
    for i in range(4):
        col = spread(i, first, col)
    for copy in copies[6:]:
        copy.wait()
    rows = first.shape[0]
    lines = [held[6 + i][...].astype(F32).reshape(1, rows) for i in range(8)]
    block = jnp.concatenate(lines, axis=0)
    block = jnp.concatenate([block, jnp.zeros((8, 128 - rows), F32)], axis=1)
    block = jnp.concatenate([block, jnp.zeros((120, 128), F32)], axis=0)
    scr[0:128] = block.T
    wide = held[14][...].astype(F32).reshape(1, 4 * rows)
    scr[0:1, BIAS_AT : BIAS_AT + 4 * rows] = wide
    first[:, col : col + SMALL] = scr[0:rows].astype(BF16)
    spread(4, second, 0)
    spread(5, third, 0)


def pack(weights, vectors, rows, width, hidden):
    flat = [w.reshape(-1, 128) for w in weights]
    ratio = hidden // width
    args = flat + vectors
    return call(
        pack_kernel,
        "pack",
        args,
        [hbm()] * len(args),
        (sds((rows, 4 * width + SMALL)), sds((rows, hidden)), sds((rows * ratio, width))),
        scratch=[pltpu.VMEM(a.shape, BF16) for a in args]
        + [pltpu.VMEM((max(f.shape[0] for f in flat), 128), F32), pltpu.SemaphoreType.DMA((15,))],
        limit=8,
    )


def z_join_kernel(at_ref, a0, a1, a2, a3, out):
    rows = a0.shape[0]
    z = lax.rem(at_ref[0], 4)
    for m, piece in enumerate((a0, a1, a2, a3)):
        out[pl.ds(pl.multiple_of((z ^ m) * rows, 8), rows), :] = piece[...]


def z_swaps(own):
    return [own] + [swap(own, m) for m in (1, 2, 3)]


def z_join(at, pieces):
    rows, cols = pieces[0].shape
    return call(z_join_kernel, "z_join", [at] + pieces, [smem()] + [vmem()] * 4, sds((4 * rows, cols)), limit=8)


def pair_join_kernel(a0, a1, out):
    rows = a0.shape[0]
    out[:rows] = a0[...]
    out[rows:] = a1[...]


def pair_join(own, came):
    rows, cols = own.shape
    return call(pair_join_kernel, "z_join", [own, came], [vmem()] * 2, sds((2 * rows, cols)), limit=4)


def z_join_pairs_kernel(at_ref, a, b, out):
    rows = a.shape[0] // 2
    z = lax.rem(at_ref[0], 4)
    for m in range(4):
        piece = (a, b)[m % 2]
        start = pl.multiple_of((z ^ m) * rows, 8)
        out[pl.ds(start, rows), :] = piece[m // 2 * rows : (m // 2 + 1) * rows]


def z_join_pairs(at, pair, came):
    rows, cols = pair.shape
    return call(z_join_pairs_kernel, "z_join", [at, pair, came], [smem()] + [vmem()] * 2, sds((2 * rows, cols)), limit=8)


def forward_halves(x, y):
    half = x.shape[1] // 256 * 128
    return [swap(x[:, :half], 16), swap(y[:, half:], 8)]


def row_blocks(own, x, y, diag):
    out = []
    for pieces in ([own], [x], [y], diag):
        out += [pieces, [swap(p, 4) for p in pieces]]
    return out


def flat_blocks(blocks):
    return [p for pieces in blocks for p in pieces]


PIECES = 10


def grouped(refs):
    return [[r] for r in refs[:6]] + [list(refs[6:8]), list(refs[8:10])]


def block_copies(at_ref, refs, scr, sems):
    group = at_ref[0] // 4
    lists, k = [], 0
    for m in range(8):
        halves = 2 if m >= 6 else 1
        col, mine = 0, []
        for _ in range(halves):
            rows, cols = refs[k].shape
            start = pl.multiple_of((group ^ m) * rows, 8)
            mine.append(pltpu.make_async_copy(refs[k], scr.at[pl.ds(start, rows), pl.ds(col, cols)], sems.at[k]))
            col += cols
            k += 1
        lists.append(mine)
    return lists


def fetch_all(at_ref, refs, scr, sems):
    lists = block_copies(at_ref, refs, scr, sems)
    for mine in lists:
        for copy in mine:
            copy.start()
    for mine in lists:
        for copy in mine:
            copy.wait()


def store_halves(group, value, keep, send, lead=()):
    part = value.shape[0] // 8
    core = lax.rem(group, 2)
    for b in range(8):
        slot = (group ^ b) // 2
        piece = value[b * part : (b + 1) * part]

        @pl.when(core == b % 2)
        def _():
            keep[lead + (pl.ds(slot, 1),)] = piece[None]

        @pl.when(core != b % 2)
        def _():
            send[lead + (pl.ds(slot, 1),)] = piece[None]


def turned(value):
    return value.astype(F32).T.astype(BF16)


def turn_kernel(at_ref, tokens, keep, send):
    store_halves(at_ref[0] // 4, turned(tokens[...]), keep, send)


def turn_tokens(at, tokens):
    size, width = tokens.shape
    out = sds((4, width // 8, size))
    return call(turn_kernel, "turn_tokens", [at, tokens], [smem(), vmem()], (out, out), limit=8)


def qkv_kernel(at_ref, tokens, *refs):
    pieces, (q, k, v, lines, bias, w_out, scr, sems) = refs[:PIECES], refs[PIECES:]
    width = tokens.shape[1]
    fetch_all(at_ref, pieces, scr, sems)
    w_out[...] = scr[:, 3 * width : 4 * width]
    tails = scr[:, 4 * width :].astype(F32)
    rows = tails.T[:16]
    lines[...] = rows
    each = width // 32
    for d in range(32):
        bias[:, 4 * each * d : 4 * each * (d + 1)] = tails[each * d : each * d + 1, BIAS_AT : BIAS_AT + 4 * each]
    x = tokens[...]
    q[...] = (dot(x, scr[:, :width]) + rows[0:1]).astype(BF16)
    k[...] = dot(x, scr[:, width : 2 * width]).astype(BF16)
    v[...] = (dot(x, scr[:, 2 * width : 3 * width]) + rows[1:2]).astype(BF16)


def project(at, tokens, blocks):
    size, width = tokens.shape
    cols = blocks[0][0].shape[1]
    args = [at, tokens] + flat_blocks(blocks)
    return call(
        qkv_kernel,
        "project",
        args,
        [smem(), vmem()] + [vmem()] * PIECES,
        (sds((size, width)),) * 3 + (sds((16, width), F32), sds((1, 4 * width), F32), sds((width, width))),
        scratch=[pltpu.VMEM((width, cols), BF16), pltpu.SemaphoreType.DMA((PIECES,))],
        limit=14,
    )


def head_lanes(h):
    lane = lax.broadcasted_iota(jnp.int32, (1, 2 * HEAD_DIM), 1)
    return (lane // HEAD_DIM) == h


def attend_kernel(len_ref, q_ref, k_ref, v_ref, mixed_ref, turned_ref, lse_ref):
    length = len_ref[0]
    q, k, v = q_ref[...], k_ref[...], v_ref[...]
    size = q.shape[0]
    keep = lax.broadcasted_iota(jnp.int32, (size, 1), 0) < length
    v_t = turned(v)
    parts = []
    for h in range(2):
        q_head = jnp.where(head_lanes(h), q.astype(F32) * SCALE, 0.0).astype(BF16)
        scores = jnp.where(keep, dot(k, q_head, NT), -1e30)
        top = jnp.max(scores, axis=0, keepdims=True)
        shifted = jnp.exp(scores - top)
        total = jnp.sum(shifted, axis=0, keepdims=True)
        mixed = dot(v_t[h * HEAD_DIM : (h + 1) * HEAD_DIM], shifted.astype(BF16)) / total
        parts.append(mixed)
        lse_ref[0, h : h + 1, :] = top + jnp.log(total)
    mixed = jnp.concatenate(parts, axis=0)
    turned_ref[...] = mixed.astype(BF16)
    mixed_ref[...] = mixed.T.astype(BF16)


def attend(lengths, q, k, v):
    size, width = q.shape
    pairs = width // 128
    tile = pl.BlockSpec((size, 128), lambda i, n: (0, i))
    return call(
        attend_kernel,
        "attend",
        [lengths, q, k, v],
        [tile] * 3,
        (sds((size, width)), sds((width, size)), sds((pairs, 2, size), F32)),
        out_specs=(
            tile,
            pl.BlockSpec((128, size), lambda i, n: (i, 0)),
            pl.BlockSpec((1, 2, size), lambda i, n: (i, 0, 0)),
        ),
        grid=(pairs,),
        prefetch=1,
        limit=12,
    )


def normed(values):
    centred = values - jnp.mean(values, axis=-1, keepdims=True)
    scale = lax.rsqrt(jnp.mean(centred * centred, axis=-1, keepdims=True) + EPSILON)
    return centred * scale, scale


def norm_back(grad, unit, scale):
    return scale * (
        grad - jnp.mean(grad, axis=-1, keepdims=True) - unit * jnp.mean(grad * unit, axis=-1, keepdims=True)
    )


def mix_kernel(at_ref, tokens, mixed, mixed_t, lines, w_out, unit_out, scale_out, normed_out, keep, send):
    group = at_ref[0] // 4
    normed_out[...] = mixed[...]
    step = 128

    def rows(i, carry):
        part = pl.ds(pl.multiple_of(i * step, step), step)
        resid = tokens[part, :].astype(F32) + dot(mixed[part, :], w_out[...]) + lines[2:3]
        unit, scale = normed(resid)
        unit_out[part, :] = unit
        scale_out[part, :] = jnp.broadcast_to(scale, (step, scale_out.shape[1]))
        normed_out[part, :] = (unit * lines[3:4] + lines[4:5]).astype(BF16)
        return carry

    lax.fori_loop(0, tokens.shape[0] // step, rows, 0)
    store_halves(group, mixed_t[...], keep, send, (0,))
    store_halves(group, turned(normed_out[...]), keep, send, (1,))


def mix_stage(at, tokens, mixed, mixed_t, lines, w_out):
    size, width = tokens.shape
    half = sds((2, 4, width // 8, size))
    return call(
        mix_kernel,
        "mix",
        [at, tokens, mixed, mixed_t, lines, w_out],
        [smem()] + [vmem()] * 5,
        (sds((size, width), F32), sds((size, 128), F32), sds((size, width)), half, half),
        limit=10,
    )


def inner_kernel(at_ref, values, bias, *refs):
    pieces = refs[:PIECES]
    (activ, slope, scr, keep, send, sems) = refs[PIECES:]
    part = activ.shape[1] // 8
    group = at_ref[0] // 4
    core = lax.rem(group, 2)
    fetch_all(at_ref, pieces, scr, sems)

    def step(b, carry):
        at = pl.multiple_of(b * part, 128)
        inner = dot(values[...], scr[:, pl.ds(at, part)]) + bias[:, pl.ds(at, part)]
        share = 0.5 * (1.0 + lax.erf(inner * 0.7071067811865476))
        result = inner * share
        activ[:, pl.ds(at, part)] = result.astype(BF16)
        slope[:, pl.ds(at, part)] = (share + inner * (0.3989422804014327 * jnp.exp(-0.5 * inner * inner))).astype(BF16)
        across = result.T.astype(BF16)
        slot = (group ^ b) // 2

        @pl.when(core == lax.rem(b, 2))
        def _():
            keep[pl.ds(slot, 1)] = across[None]

        @pl.when(core != lax.rem(b, 2))
        def _():
            send[pl.ds(slot, 1)] = across[None]

        return carry

    lax.fori_loop(0, 8, step, 0)


def inner_stage(at, values, bias, blocks):
    size, width = values.shape
    hidden = bias.shape[1]
    args = [at, values, bias] + flat_blocks(blocks)
    half = sds((4, hidden // 8, size))
    return call(
        inner_kernel,
        "inner",
        args,
        [smem()] + [vmem()] * (2 + PIECES),
        (sds((size, hidden)), sds((size, hidden)), sds((width, hidden)), half, half),
        scratch=[pltpu.SemaphoreType.DMA((PIECES,))],
        limit=14,
    )


def outer_kernel(at_ref, len_ref, activ, values, lines, cot, *refs):
    pieces, (output, resid_grad, outer_grad, sums, acc) = refs[:PIECES], refs[PIECES:]
    size = values.shape[0]
    part = activ.shape[1] // 8
    group = at_ref[0] // 4
    resid = values[...].astype(F32) + lines[5:6]
    for m, mine in enumerate(grouped(pieces)):
        given = activ[:, pl.ds(pl.multiple_of((group ^ m) * part, 128), part)]
        products = [dot(given, piece[...]) for piece in mine]
        resid += products[0] if len(products) == 1 else jnp.concatenate(products, axis=1)
    acc[...] = resid
    gain, shift = lines[6:7], lines[7:8]
    sums[...] = jnp.zeros_like(sums)
    step = 128

    def rows(i, carry):
        part = pl.ds(pl.multiple_of(i * step, step), step)
        unit, scale = normed(acc[part, :])
        valid = lax.broadcasted_iota(jnp.int32, (step, 1), 0) + i * step < len_ref[0]
        output[part, :] = jnp.where(valid, unit * gain + shift, 0.0).astype(BF16)
        grad = jnp.where(valid, cot[part, :].astype(F32), 0.0)
        sums[6:7] += jnp.sum(grad * unit, axis=0, keepdims=True)
        sums[7:8] += jnp.sum(grad, axis=0, keepdims=True)
        grad = norm_back(grad * gain, unit, scale)
        resid_grad[part, :] = grad
        rounded = grad.astype(BF16)
        outer_grad[part, :] = rounded
        sums[5:6] += jnp.sum(rounded.astype(F32), axis=0, keepdims=True)
        return carry

    lax.fori_loop(0, size // step, rows, 0)


def outer_stage(at, lengths, activ, values, lines, cot, blocks):
    size, width = values.shape
    hidden = activ.shape[1]
    args = [at, lengths, activ, values, lines, cot] + flat_blocks(blocks)
    return call(
        outer_kernel,
        "outer",
        args,
        [smem(), smem()] + [vmem()] * (4 + PIECES),
        (sds((size, width)), sds((size, width), F32), sds((size, width)), sds((8, width), F32)),
        scratch=[pltpu.VMEM((size, width), F32)],
        limit=10,
    )


def slope_kernel(at_ref, outer_grad, slope, *refs):
    pieces, (inner_grad, sums) = refs[:PIECES], refs[PIECES:]
    part = slope.shape[1] // 8
    group = at_ref[0] // 4
    grad = outer_grad[...]
    for m, mine in enumerate(grouped(pieces)):
        at = pl.multiple_of((group ^ m) * part, 128)
        back, col = 0.0, 0
        for piece in mine:
            cols = piece.shape[1]
            back += dot(grad[:, col : col + cols], piece[...], NT)
            col += cols
        rounded = (back * slope[:, pl.ds(at, part)].astype(F32)).astype(BF16)
        inner_grad[:, pl.ds(at, part)] = rounded
        sums[:, pl.ds(at, part)] = jnp.sum(rounded.astype(F32), axis=0, keepdims=True)


def slope_stage(at, outer_grad, slope, blocks):
    size, width = outer_grad.shape
    hidden = slope.shape[1]
    args = [at, outer_grad, slope] + flat_blocks(blocks)
    return call(
        slope_kernel,
        "slope",
        args,
        [smem()] + [vmem()] * (2 + PIECES),
        (sds((size, hidden)), sds((1, hidden), F32)),
        limit=10,
    )


def normed_back_kernel(inner_grad, resid_two, unit_ref, scale_ref, lines, w_out, weights, resid_grad, attn_low, attn_high, mixed_grad, sums):
    width = unit_ref.shape[1]
    hidden = inner_grad.shape[1]
    grad = resid_two[...]
    for c in range(0, hidden, width):
        grad += dot(inner_grad[:, c : c + width], weights[:, c : c + width], NT)
    half = attn_low.shape[1]
    resid_grad[...] = grad
    sums[...] = jnp.zeros_like(sums)
    step = 128

    def rows(i, carry):
        part = pl.ds(pl.multiple_of(i * step, step), step)
        unit = unit_ref[part, :]
        grad = resid_grad[part, :]
        sums[3:4] += jnp.sum(grad * unit, axis=0, keepdims=True)
        sums[4:5] += jnp.sum(grad, axis=0, keepdims=True)
        grad = norm_back(grad * lines[3:4], unit, scale_ref[part, 0:1])
        resid_grad[part, :] = grad
        rounded = grad.astype(BF16)
        attn_low[part, :] = rounded[:, :half]
        attn_high[part, :] = rounded[:, half:]
        sums[2:3] += jnp.sum(rounded.astype(F32), axis=0, keepdims=True)
        return carry

    lax.fori_loop(0, grad.shape[0] // step, rows, 0)
    back = dot(attn_low[...], w_out[:, :half], NT) + dot(attn_high[...], w_out[:, half:], NT)
    mixed_grad[...] = back.astype(BF16)


def normed_back(inner_grad, resid_two, unit, scale, lines, w_out, weights):
    size, width = unit.shape
    hidden = inner_grad.shape[1]
    args = [inner_grad, resid_two, unit, scale, lines, w_out, weights]
    return call(
        normed_back_kernel,
        "normed_back",
        args,
        [vmem()] * 7,
        (sds((size, width), F32),)
        + (sds((size, width // 2)),) * 2
        + (sds((size, width)), sds((8, width), F32)),
        limit=12,
    )


def attend_back_kernel(len_ref, q_ref, k_ref, v_ref, mixed_ref, grad_ref, lse_ref, grads_ref, qs_ref, vs_ref):
    length = len_ref[0]
    q, k, v, grad = q_ref[...], k_ref[...], v_ref[...], grad_ref[...]
    size = q.shape[0]
    keep = lax.broadcasted_iota(jnp.int32, (size, 1), 0) < length
    k_t = turned(k)
    prod_t = turned(grad).astype(F32) * mixed_ref[...].astype(F32)
    q_grad, k_grad, v_grad = [], 0.0, 0.0
    for h in range(2):
        mine = head_lanes(h)
        q_head = jnp.where(mine, q.astype(F32) * SCALE, 0.0).astype(BF16)
        g_head = jnp.where(mine, grad, jnp.zeros_like(grad))
        scores = jnp.where(keep, dot(k, q_head, NT), -1e30)
        probs = jnp.exp(scores - lse_ref[0, h : h + 1, :])
        delta = jnp.sum(prod_t[h * HEAD_DIM : (h + 1) * HEAD_DIM], axis=0, keepdims=True)
        prob_grad = dot(v, g_head, NT)
        score_grad = (probs * (prob_grad - delta)).astype(BF16)
        v_grad += dot(probs.astype(BF16), g_head)
        k_grad += dot(score_grad, q_head)
        q_grad.append(dot(k_t[h * HEAD_DIM : (h + 1) * HEAD_DIM], score_grad))
    q_rounded = (jnp.concatenate(q_grad, axis=0) * SCALE).T.astype(BF16)
    v_rounded = v_grad.astype(BF16)
    grads_ref[0] = q_rounded
    grads_ref[1] = k_grad.astype(BF16)
    grads_ref[2] = v_rounded
    qs_ref[...] = jnp.sum(q_rounded.astype(F32), axis=0, keepdims=True)
    vs_ref[...] = jnp.sum(v_rounded.astype(F32), axis=0, keepdims=True)


def attend_back(lengths, q, k, v, mixed_t, grad, lse):
    size, width = q.shape
    pairs = width // 128
    tile = pl.BlockSpec((size, 128), lambda i, n: (0, i))
    out = pl.BlockSpec((3, size, 128), lambda i, n: (0, 0, i))
    line = pl.BlockSpec((1, 128), lambda i, n: (0, i))
    return call(
        attend_back_kernel,
        "attend_back",
        [lengths, q, k, v, mixed_t, grad, lse],
        [tile] * 3
        + [
            pl.BlockSpec((128, size), lambda i, n: (i, 0)),
            tile,
            pl.BlockSpec((1, 2, size), lambda i, n: (i, 0, 0)),
        ],
        (sds((3, size, width)),) + (sds((1, width), F32),) * 2,
        out_specs=(out,) + (line,) * 2,
        grid=(pairs,),
        prefetch=1,
        limit=12,
    )


def tokens_kernel(at_ref, resid_grad, *refs):
    grads, pieces, (out, scr, sems) = refs[0], refs[1 : 1 + PIECES], refs[1 + PIECES :]
    width = resid_grad.shape[1]
    fetch_all(at_ref, pieces, scr, sems)
    total = resid_grad[...]
    for i in range(3):
        total += dot(grads[i], scr[:, i * width : (i + 1) * width], NT)
    out[...] = total.astype(BF16)


def tokens_back(at, resid_grad, grads, blocks):
    size, width = resid_grad.shape
    cols = blocks[0][0].shape[1]
    args = [at, resid_grad, grads] + flat_blocks(blocks)
    return call(
        tokens_kernel,
        "tokens_back",
        args,
        [smem()] + [vmem()] * 2 + [hbm()] * PIECES,
        sds((size, width)),
        scratch=[pltpu.VMEM((width, cols), BF16), pltpu.SemaphoreType.DMA((PIECES,))],
        limit=14,
    )


def small_kernel(one, two, q_sum, v_sum, bias, out):
    width = one.shape[1]
    out[0:8] = one[...] + two[...]
    out[8:16] = jnp.zeros((8, width), F32)
    out[0:1], out[1:2] = q_sum[...], v_sum[...]
    for r in range(4):
        out[12 + r : 13 + r] = bias[:, r * width : (r + 1) * width]


def stack_small(*args):
    one = args[0]
    return call(small_kernel, "stack_small", list(args), [vmem()] * 5, sds((16, one.shape[1]), F32), limit=4)


def put_slots(value, col, outs):
    s0, s1, s2, s3a, s3b = outs
    part, cols = s0.shape
    half = s3a.shape[1]
    width = value.shape[1]
    for s, out in enumerate((s0, s1, s2)):
        out[:, col : col + width] = value[s * part : (s + 1) * part]
    last = value[3 * part : 4 * part]
    cut = min(max(half - col, 0), width)
    if cut > 0:
        s3a[:, col : col + cut] = last[:, :cut]
    if cut < width:
        s3b[:, col + cut - half : col + width - half] = last[:, cut:]


def slot_shapes(part, cols):
    half = cols // 256 * 128
    return (sds((part, cols)),) * 3 + (sds((part, half)), sds((part, cols - half)))


def grad_kernel(plan, small, *refs):
    outs = refs[-5:]
    if small:
        outs, scr = refs[-6:-1], refs[-1]
    part = outs[0].shape[0]
    col = 0
    for left, lead, mine, came, which in plan:
        rows = 4 * part
        size = refs[left].shape[-1]
        a = refs[left][lead] if lead is not None else refs[left][...]
        b = refs[left + 1][lead] if lead is not None else refs[left + 1][...]
        a, b = a.reshape(rows, size), b.reshape(rows, size)
        total = refs[mine].shape[-1]
        step = min(total, 768)
        for start in range(0, total, step):
            at = which + (slice(None), slice(start, start + step))
            value = dot(a, refs[mine][at]) + dot(b, refs[came][at])
            put_slots(value.astype(BF16), col, outs)
            col += step
    if small:
        at_ref, own, came = refs[small], refs[small + 1], refs[small + 2]
        both = own[...] + came[...]
        padded = jnp.concatenate([both, jnp.zeros((SMALL - both.shape[0], both.shape[1]), F32)], axis=0)
        scr[...] = padded.T
        each = 4 * scr.shape[0] // 32
        wide = scr.shape[0]
        for d in range(32):
            row, lane = 12 + each * d // wide, each * d % wide
            scr[wide // 32 * d : wide // 32 * d + 1, BIAS_AT : BIAS_AT + each] = both[row : row + 1, lane : lane + each]
        group = at_ref[0] // 4
        value = jnp.concatenate(
            [scr[pl.ds(pl.multiple_of((group ^ (2 * s)) * part, 8), part), :] for s in range(4)], axis=0
        )
        put_slots(value.astype(BF16), col, outs)


def weight_grad(name, args, plan, part, cols, small=None):
    specs = [vmem()] * len(args)
    scratch = []
    if small:
        specs[small] = smem()
        scratch = [pltpu.VMEM((8 * part, SMALL), F32)]
    return call(
        functools.partial(grad_kernel, plan, small),
        name,
        args,
        specs,
        slot_shapes(part, cols),
        scratch=scratch,
        limit=14,
    )


def add_kernel(x_ref, p_ref, y_ref, q_ref, x_out, y_out):
    x_out[...] = (x_ref[...].astype(F32) + p_ref[...].astype(F32)).astype(BF16)
    y_out[...] = (y_ref[...].astype(F32) + q_ref[...].astype(F32)).astype(BF16)


def add_halves(x, p, y, q):
    part, cols = x.shape
    half = p.shape[1]
    rest = cols - half
    if half != rest:
        return add_uneven(x, p, y, q)
    low = pl.BlockSpec((part, half), lambda i: (0, 0))
    high = pl.BlockSpec((part, half), lambda i: (0, 1))
    return call(
        add_kernel,
        "add_halves",
        [x, p, y, q],
        [low, low, high, low],
        (sds(x.shape), sds(y.shape)),
        out_specs=(low, high),
        grid=(1,),
        alias={0: 0, 2: 1},
        limit=16,
    )


def uneven_kernel(x_ref, p_ref, y_ref, q_ref, x_out, y_out):
    half = p_ref.shape[1]
    x_out[...] = x_ref[...]
    y_out[...] = y_ref[...]
    x_out[:, :half] = (x_ref[:, :half].astype(F32) + p_ref[...].astype(F32)).astype(BF16)
    y_out[:, half:] = (y_ref[:, half:].astype(F32) + q_ref[...].astype(F32)).astype(BF16)


def add_uneven(x, p, y, q):
    return call(
        uneven_kernel,
        "add_halves",
        [x, p, y, q],
        [vmem()] * 4,
        (sds(x.shape), sds(y.shape)),
        limit=16,
    )


def plane_sum_kernel(at_ref, a0, a1, a2, keep, send, total):
    total[...] = a0[...].astype(F32) + (a1[...].astype(F32) + a2[...].astype(F32))
    rows = keep.shape[0] // 2
    z = lax.rem(at_ref[0], 4)
    for m in range(4):
        out = (keep, send)[m // 2]
        part = total[pl.ds(pl.multiple_of((z ^ m) * rows, 8), rows), :]
        out[m % 2 * rows : (m % 2 + 1) * rows] = part.astype(BF16)


def plane_sum(at, pieces):
    part, cols = pieces[0].shape
    return call(
        plane_sum_kernel,
        "plane_sum",
        [at] + pieces,
        [smem()] + [vmem()] * 3,
        (sds((part // 2, cols)),) * 2,
        scratch=[pltpu.VMEM((part, cols), F32)],
        limit=6,
    )


def pair_sum_kernel(keep, came, own, send):
    rows = own.shape[0]
    total = keep[...].astype(F32) + came[...].astype(F32)
    own[...] = total[:rows]
    send[...] = total[rows:].astype(BF16)


def pair_sum(keep, came):
    rows, cols = keep.shape[0] // 2, keep.shape[1]
    return call(
        pair_sum_kernel,
        "pair_sum",
        [keep, came],
        [vmem()] * 2,
        (sds((rows, cols), F32), sds((rows, cols))),
        limit=8,
    )


def finish_kernel(widths, tail, own, came, *outs):
    total = own[...] + came[...].astype(F32)
    rows = total.shape[0]
    col = 0
    for width, out in zip(widths, outs):
        blocks = width // 128
        for c in range(blocks):
            out[pl.ds(c, rows, stride=blocks), :] = total[:, col + c * 128 : col + (c + 1) * 128]
        col += width
    if tail:
        block = jnp.concatenate([total[:, col : col + SMALL], jnp.zeros((SMALL - rows, SMALL), F32)], axis=0).T
        for i in range(8):
            outs[len(widths) + i][...] = block[i : i + 1, :rows].reshape(rows)
        outs[len(widths) + 8][...] = total[0:1, col + BIAS_AT : col + BIAS_AT + 4 * rows].reshape(4 * rows)


def finish(pieces, widths, tail=False):
    rows = pieces[0].shape[0]
    shapes = [sds((rows * w // 128, 128), F32) for w in widths]
    if tail:
        shapes += [sds((rows,), F32)] * 8 + [sds((4 * rows,), F32)]
    outs = call(
        functools.partial(finish_kernel, widths, tail),
        "finish",
        pieces,
        [vmem()] * 2,
        tuple(shapes),
        limit=6,
    )
    return [o.reshape(-1) for o in outs]


def scatter_plane(slots, *done):
    s0, s1, s2, s3a, s3b = slots
    p, q = swap(s3a, 16), swap(s3b, 8)
    s1 = after(s1, *done)
    x, y = add_halves(s1, p, s2, q)
    return [s0, swap(x, 8), swap(y, 16), x]


def first_z(sums, *done):
    keep, send = sums
    return pair_sum(after(keep, *done), swap(send, 2))


def blocked_layer(
    tokens,
    lengths,
    query_weight,
    query_bias,
    key_weight,
    value_weight,
    value_bias,
    output_weight,
    output_bias,
    attn_gain,
    attn_shift,
    inner_weight,
    inner_bias,
    outer_weight,
    outer_bias,
    ffn_gain,
    ffn_shift,
    cotangent,
):
    size, width = tokens.shape
    rows = query_weight.shape[0] // width
    hidden = inner_weight.shape[0] // rows
    ratio = hidden // width
    at = lax.axis_index(AXES).astype(jnp.int32).reshape(1)

    first, second, third = pack(
        [query_weight, key_weight, value_weight, output_weight, inner_weight, outer_weight],
        [query_bias, value_bias, output_bias, attn_gain, attn_shift, outer_bias, ffn_gain, ffn_shift, inner_bias],
        rows,
        width,
        hidden,
    )
    z_first = z_join(at, z_swaps(first))
    x_first, y_first = swap(z_first, 8), swap(z_first, 16)
    second = after(second, z_first)
    second = pair_join(second, swap(second, 2))
    x_first, second = lax.optimization_barrier((x_first, second))
    f_first = forward_halves(x_first, y_first)
    first_blocks = row_blocks(z_first, x_first, y_first, f_first)
    z_second = z_join_pairs(at, second, swap(second, 1))
    x_second, y_second = swap(z_second, 8), swap(z_second, 16)
    third = after(third, z_second, first_blocks[7][0], first_blocks[7][1])
    third_came = swap(third, 2)

    tok_keep, tok_send = turn_tokens(at, tokens)
    tok_came = swap(tok_send, 4)
    queries, key_rows, value_rows, lines, bias, w_out = project(at, tokens, first_blocks)
    mixed, mixed_t, lse = attend(lengths, queries, key_rows, value_rows)
    third = pair_join(third, after(third_came, mixed))
    mixed, x_second, y_second, third = lax.optimization_barrier((mixed, x_second, y_second, third))
    f_second = forward_halves(x_second, y_second)
    unit, scale, values, b_keep, b_send = mix_stage(at, tokens, after(mixed, tok_came), mixed_t, lines, w_out)
    b_came = swap(b_send, 4)
    second_blocks = row_blocks(z_second, x_second, y_second, f_second)
    z_third = z_join_pairs(at, third, after(swap(third, 1), *f_second))
    x_third, y_third = swap(z_third, 8), swap(z_third, 16)
    activ, slope, w_inner, a_keep, a_send = inner_stage(at, after(values, z_third), bias, second_blocks)
    activ, x_third, y_third = lax.optimization_barrier((activ, x_third, y_third))
    f_third = forward_halves(x_third, y_third)
    third_blocks = row_blocks(z_third, x_third, y_third, f_third)
    a_came = swap(after(a_send, x_third), 4)
    activ = after(activ, a_came)
    output, resid_two_grad, outer_grad, sums_two = outer_stage(at, lengths, activ, values, lines, cotangent, third_blocks)

    outer_came = swap(outer_grad, 4)
    inner_grad, bias_grad = slope_stage(at, outer_grad, slope, third_blocks)
    inner_came = swap(after(inner_grad, outer_came), 4)
    slots_a = weight_grad(
        "grad_outer",
        [a_keep, a_came, outer_grad, after(outer_came, inner_grad)],
        [(0, None, 2, 3, ())],
        hidden // 8,
        width,
    )
    resid_one_grad, attn_low, attn_high, mixed_grad, sums_one = normed_back(
        after(inner_grad, slots_a[0]), resid_two_grad, unit, scale, lines, w_out, w_inner
    )
    plane_a = scatter_plane(slots_a, attn_low)
    low_came, high_came = (swap(after(g, plane_a[3]), 4) for g in (attn_low, attn_high))
    slots_b = weight_grad(
        "grad_inner",
        [b_keep, b_came, attn_low, low_came, attn_high, high_came, inner_grad, inner_came],
        [(0, 0, 2, 3, ()), (0, 0, 4, 5, ()), (0, 1, 6, 7, ())],
        width // 8,
        width + hidden,
    )
    grads, q_sum, v_sum = attend_back(
        lengths, queries, key_rows, value_rows, mixed_t, after(mixed_grad, slots_b[0]), lse
    )
    plane_b = scatter_plane(slots_b, grads)
    sums_a = plane_sum(at, [after(plane_a[0], plane_b[3])] + plane_a[1:3])
    grads_came = swap(after(grads, sums_a[0]), 4)
    small = stack_small(sums_one, sums_two, q_sum, v_sum, bias_grad)
    small_came = swap(small, 4)
    args = [tok_keep, tok_came, grads, grads_came]
    plan = [(0, None, 2, 3, (i,)) for i in range(3)]
    slots_c = weight_grad(
        "grad_first",
        args + [at, small, small_came],
        plan,
        width // 8,
        3 * width + SMALL,
        small=len(args),
    )
    tokens_grad = tokens_back(at, after(resid_one_grad, slots_c[0]), grads, first_blocks)
    own_a, last_a = first_z(sums_a, tokens_grad)
    slots_c = list(slots_c)
    slots_c[3], slots_c[4], _ = lax.optimization_barrier((slots_c[3], slots_c[4], own_a))
    sums_b = plane_sum(at, [after(plane_b[0], own_a)] + plane_b[1:3])
    plane_c = scatter_plane(slots_c, sums_b[0])
    (own_u,) = finish([own_a, swap(after(last_a, sums_b[0]), 1)], [width])
    own_b, last_b = first_z(sums_b)
    sums_c = plane_sum(at, [after(plane_c[0], own_b)] + plane_c[1:3])
    own_o, own_i = finish([own_b, swap(last_b, 1)], [width, hidden])
    own_c, last_c = first_z(sums_c)
    own_q, own_k, own_v, qb, vb, ob, ag, ash, ub, fg, fs, ib = finish(
        [own_c, swap(last_c, 1)], [width] * 3, tail=True
    )
    return (output, tokens_grad, own_q, qb, own_k, own_v, vb, own_o, ob, ag, ash, own_i, ib, own_u, ub, fg, fs)


def layer_norm(values, norm_gain, norm_shift):
    row_mean = jnp.mean(values, axis=-1, keepdims=True)
    centred = values - row_mean
    row_var = jnp.mean(centred * centred, axis=-1, keepdims=True)
    return centred * lax.rsqrt(row_var + EPSILON) * norm_gain + norm_shift


def gelu_exact(values):
    return jax.nn.gelu(values, approximate=False)


def matmul(left, right):
    return jnp.dot(left, right, preferred_element_type=jnp.float32)


def left_product(left, right):
    return jnp.einsum("rd,rf->df", left, right, preferred_element_type=jnp.float32)


def right_product(left, right):
    return jnp.einsum("rf,df->rd", left, right, preferred_element_type=jnp.float32)


def column_sums(values):
    return jnp.sum(values.astype(jnp.float32), axis=0)


def unpack(gathered, model_width):
    (
        query_weight,
        query_bias,
        key_weight,
        value_weight,
        value_bias,
        output_weight,
        output_bias,
        attn_gain,
        attn_shift,
        inner_weight,
        inner_bias,
        outer_weight,
        outer_bias,
        ffn_gain,
        ffn_shift,
    ) = gathered
    hidden_width = inner_bias.shape[0]
    return (
        query_weight.reshape(model_width, model_width),
        query_bias,
        key_weight.reshape(model_width, model_width),
        value_weight.reshape(model_width, model_width),
        value_bias,
        output_weight.reshape(model_width, model_width),
        output_bias,
        attn_gain.astype(jnp.float32),
        attn_shift.astype(jnp.float32),
        inner_weight.reshape(model_width, hidden_width),
        inner_bias,
        outer_weight.reshape(hidden_width, model_width),
        outer_bias,
        ffn_gain.astype(jnp.float32),
        ffn_shift.astype(jnp.float32),
    )


def scores_of(query_seq, key_seq, keep_row):
    scores = (
        jnp.einsum("qhd,khd->hqk", query_seq, key_seq, preferred_element_type=jnp.float32) * SCALE
    )
    return jnp.where(keep_row[None, None, :], scores, -1e30)


def attend_forward(seq_item):
    query_seq, key_seq, value_seq, keep_row = seq_item
    scores = scores_of(query_seq, key_seq, keep_row)
    top = jnp.max(scores, axis=-1, keepdims=True)
    shifted_exp = jnp.exp(scores - top)
    total = jnp.sum(shifted_exp, axis=-1, keepdims=True)
    probs = (shifted_exp / total).astype(jnp.bfloat16)
    mixed = jnp.einsum("hqk,khd->qhd", probs, value_seq, preferred_element_type=jnp.float32)
    return (mixed.astype(jnp.bfloat16), (top + jnp.log(total))[..., 0])


def attend_backward(seq_item):
    query_seq, key_seq, value_seq, keep_row, log_total, mixed_grad = seq_item
    scores = scores_of(query_seq, key_seq, keep_row)
    probs = jnp.exp(scores - log_total[..., None])
    value_grad = jnp.einsum(
        "hqk,qhd->khd", probs.astype(jnp.bfloat16), mixed_grad, preferred_element_type=jnp.float32
    )
    prob_grad = jnp.einsum(
        "qhd,khd->hqk", mixed_grad, value_seq, preferred_element_type=jnp.float32
    )
    row_delta = jnp.sum(probs * prob_grad, axis=-1, keepdims=True)
    score_grad = (probs * (prob_grad - row_delta)).astype(jnp.bfloat16)
    query_grad = (
        jnp.einsum("hqk,khd->qhd", score_grad, key_seq, preferred_element_type=jnp.float32) * SCALE
    )
    key_grad = (
        jnp.einsum("hqk,qhd->khd", score_grad, query_seq, preferred_element_type=jnp.float32)
        * SCALE
    )
    return (
        query_grad.astype(jnp.bfloat16),
        key_grad.astype(jnp.bfloat16),
        value_grad.astype(jnp.bfloat16),
    )


def plain_layer(
    tokens,
    lengths,
    query_weight,
    query_bias,
    key_weight,
    value_weight,
    value_bias,
    output_weight,
    output_bias,
    attn_gain,
    attn_shift,
    inner_weight,
    inner_bias,
    outer_weight,
    outer_bias,
    ffn_gain,
    ffn_shift,
    cotangent,
):
    row_count = tokens.shape[0]
    model_width = tokens.shape[1]
    seq_count = lengths.shape[0]
    seq_len = row_count // seq_count
    gathered = (
        lax.all_gather(query_weight, ("wide", "narrow"), axis=0, tiled=True),
        lax.all_gather(query_bias, ("wide", "narrow"), axis=0, tiled=True),
        lax.all_gather(key_weight, ("wide", "narrow"), axis=0, tiled=True),
        lax.all_gather(value_weight, ("wide", "narrow"), axis=0, tiled=True),
        lax.all_gather(value_bias, ("wide", "narrow"), axis=0, tiled=True),
        lax.all_gather(output_weight, ("wide", "narrow"), axis=0, tiled=True),
        lax.all_gather(output_bias, ("wide", "narrow"), axis=0, tiled=True),
        lax.all_gather(attn_gain, ("wide", "narrow"), axis=0, tiled=True),
        lax.all_gather(attn_shift, ("wide", "narrow"), axis=0, tiled=True),
        lax.all_gather(inner_weight, ("wide", "narrow"), axis=0, tiled=True),
        lax.all_gather(inner_bias, ("wide", "narrow"), axis=0, tiled=True),
        lax.all_gather(outer_weight, ("wide", "narrow"), axis=0, tiled=True),
        lax.all_gather(outer_bias, ("wide", "narrow"), axis=0, tiled=True),
        lax.all_gather(ffn_gain, ("wide", "narrow"), axis=0, tiled=True),
        lax.all_gather(ffn_shift, ("wide", "narrow"), axis=0, tiled=True),
    )
    (
        full_qw,
        full_qb,
        full_kw,
        full_vw,
        full_vb,
        full_ow,
        full_ob,
        full_ag,
        full_as,
        full_iw,
        full_ib,
        full_uw,
        full_ub,
        full_fg,
        full_fs,
    ) = unpack(gathered, model_width)
    positions = jnp.arange(seq_len, dtype=jnp.int32)
    keep = positions[None, :] < lengths[:, None]
    row_valid = keep.reshape(row_count, 1).astype(jnp.float32)
    shape_four = (seq_count, seq_len, HEADS, HEAD_DIM)
    queries = (matmul(tokens, full_qw) + full_qb).astype(jnp.bfloat16)
    key_rows = matmul(tokens, full_kw).astype(jnp.bfloat16)
    value_rows = (matmul(tokens, full_vw) + full_vb).astype(jnp.bfloat16)
    query_four = queries.reshape(shape_four)
    key_four = key_rows.reshape(shape_four)
    value_four = value_rows.reshape(shape_four)
    mixed, log_total = lax.map(attend_forward, (query_four, key_four, value_four, keep))
    mixed_flat = mixed.reshape(row_count, model_width)
    resid_one = tokens.astype(jnp.float32) + matmul(mixed_flat, full_ow) + full_ob
    normed_one = layer_norm(resid_one, full_ag, full_as).astype(jnp.bfloat16)
    inner = matmul(normed_one, full_iw) + full_ib
    activ = gelu_exact(inner).astype(jnp.bfloat16)
    resid_two = normed_one.astype(jnp.float32) + matmul(activ, full_uw) + full_ub
    output = (layer_norm(resid_two, full_fg, full_fs) * row_valid).astype(jnp.bfloat16)
    (
        back_qw,
        back_qb,
        back_kw,
        back_vw,
        back_vb,
        back_ow,
        back_ob,
        back_ag,
        back_as,
        back_iw,
        back_ib,
        back_uw,
        back_ub,
        back_fg,
        back_fs,
    ) = unpack(gathered, model_width)
    out_grad = cotangent.astype(jnp.float32) * row_valid
    ignored, pull_two = jax.vjp(layer_norm, resid_two, back_fg, back_fs)
    resid_two_grad, ffn_gain_grad, ffn_shift_grad = pull_two(out_grad)
    outer_grad = resid_two_grad.astype(jnp.bfloat16)
    outer_weight_grad = left_product(activ, outer_grad)
    outer_bias_grad = column_sums(outer_grad)
    activ_grad = right_product(outer_grad, back_uw)
    ignored, pull_gelu = jax.vjp(gelu_exact, inner)
    inner_grad = pull_gelu(activ_grad)[0].astype(jnp.bfloat16)
    inner_weight_grad = left_product(normed_one, inner_grad)
    inner_bias_grad = column_sums(inner_grad)
    normed_grad = resid_two_grad + right_product(inner_grad, back_iw)
    ignored, pull_one = jax.vjp(layer_norm, resid_one, back_ag, back_as)
    resid_one_grad, attn_gain_grad, attn_shift_grad = pull_one(normed_grad)
    attn_grad = resid_one_grad.astype(jnp.bfloat16)
    output_weight_grad = left_product(mixed_flat, attn_grad)
    output_bias_grad = column_sums(attn_grad)
    mixed_grad = right_product(attn_grad, back_ow).astype(jnp.bfloat16)
    query_grad, key_grad, value_grad = lax.map(
        attend_backward,
        (query_four, key_four, value_four, keep, log_total, mixed_grad.reshape(shape_four)),
    )
    query_grad = query_grad.reshape(row_count, model_width)
    key_grad = key_grad.reshape(row_count, model_width)
    value_grad = value_grad.reshape(row_count, model_width)
    query_weight_grad = left_product(tokens, query_grad)
    key_weight_grad = left_product(tokens, key_grad)
    value_weight_grad = left_product(tokens, value_grad)
    query_bias_grad = column_sums(query_grad)
    value_bias_grad = column_sums(value_grad)
    tokens_grad = (
        resid_one_grad
        + right_product(query_grad, back_qw)
        + right_product(key_grad, back_kw)
        + right_product(value_grad, back_vw)
    ).astype(jnp.bfloat16)
    (
        own_qw,
        own_qb,
        own_kw,
        own_vw,
        own_vb,
        own_ow,
        own_ob,
        own_ag,
        own_as,
        own_iw,
        own_ib,
        own_uw,
        own_ub,
        own_fg,
        own_fs,
    ) = (
        lax.psum_scatter(
            query_weight_grad.reshape(-1), ("wide", "narrow"), scatter_dimension=0, tiled=True
        ),
        lax.psum_scatter(query_bias_grad, ("wide", "narrow"), scatter_dimension=0, tiled=True),
        lax.psum_scatter(
            key_weight_grad.reshape(-1), ("wide", "narrow"), scatter_dimension=0, tiled=True
        ),
        lax.psum_scatter(
            value_weight_grad.reshape(-1), ("wide", "narrow"), scatter_dimension=0, tiled=True
        ),
        lax.psum_scatter(value_bias_grad, ("wide", "narrow"), scatter_dimension=0, tiled=True),
        lax.psum_scatter(
            output_weight_grad.reshape(-1), ("wide", "narrow"), scatter_dimension=0, tiled=True
        ),
        lax.psum_scatter(output_bias_grad, ("wide", "narrow"), scatter_dimension=0, tiled=True),
        lax.psum_scatter(attn_gain_grad, ("wide", "narrow"), scatter_dimension=0, tiled=True),
        lax.psum_scatter(attn_shift_grad, ("wide", "narrow"), scatter_dimension=0, tiled=True),
        lax.psum_scatter(
            inner_weight_grad.reshape(-1), ("wide", "narrow"), scatter_dimension=0, tiled=True
        ),
        lax.psum_scatter(inner_bias_grad, ("wide", "narrow"), scatter_dimension=0, tiled=True),
        lax.psum_scatter(
            outer_weight_grad.reshape(-1), ("wide", "narrow"), scatter_dimension=0, tiled=True
        ),
        lax.psum_scatter(outer_bias_grad, ("wide", "narrow"), scatter_dimension=0, tiled=True),
        lax.psum_scatter(ffn_gain_grad, ("wide", "narrow"), scatter_dimension=0, tiled=True),
        lax.psum_scatter(ffn_shift_grad, ("wide", "narrow"), scatter_dimension=0, tiled=True),
    )
    return (
        output,
        tokens_grad,
        own_qw,
        own_qb,
        own_kw,
        own_vw,
        own_vb,
        own_ow,
        own_ob,
        own_ag,
        own_as,
        own_iw,
        own_ib,
        own_uw,
        own_ub,
        own_fg,
        own_fs,
    )


def solution(mesh):
    split = P(AXES)
    rows = P(AXES, None)
    blocked = mesh.shape["wide"] == 8 and mesh.shape["narrow"] == 4
    return jax.shard_map(
        blocked_layer if blocked else plain_layer,
        mesh=mesh,
        in_specs=(rows,) + (split,) * 16 + (rows,),
        out_specs=(rows, rows) + (split,) * 15,
        check_vma=False,
    )
```

```python
import functools

import jax
import jax.numpy as jnp
from jax import lax
from jax.experimental import pallas as pl
from jax.experimental.pallas import tpu as pltpu
from jax.sharding import PartitionSpec as P

HEADS = 12
HEAD_DIM = 64
EPSILON = 1e-06
SCALE = 0.125
AXES = ("wide", "narrow")
SMALL = 128
BIAS_AT = 16
F32 = jnp.float32
BF16 = jnp.bfloat16
NT = (((1,), (1,)), ((), ()))
NN = (((1,), (0,)), ((), ()))
MIB = 1024 * 1024
DECLARED = 5.5e8
TIMES = {
    "pack": 1.3,
    "z_join": 0.3,
    "turn_tokens": 1.0,
    "project": 1.5,
    "attend": 2.0,
    "mix": 3.0,
    "inner": 9.0,
    "outer": 6.0,
    "slope": 3.7,
    "grad_outer": 2.6,
    "normed_back": 5.0,
    "add_halves": 0.5,
    "grad_inner": 3.2,
    "attend_back": 11.4,
    "plane_sum": 0.6,
    "pair_sum": 0.1,
    "stack_small": 0.1,
    "grad_first": 2.0,
    "tokens_back": 5.6,
    "finish": 0.8,
}


def dot(left, right, dims=NN):
    return lax.dot_general(left, right, dims, preferred_element_type=F32)


def vmem():
    return pl.BlockSpec(memory_space=pltpu.VMEM)


def smem():
    return pl.BlockSpec(memory_space=pltpu.SMEM)


def hbm():
    return pl.BlockSpec(memory_space=pltpu.HBM)


def sds(shape, dtype=BF16):
    return jax.ShapeDtypeStruct(shape, dtype)


def call(kernel, name, args, in_specs, out_shape, out_specs=None, scratch=(), limit=32, grid=None, prefetch=0, alias=None):
    many = isinstance(out_shape, (tuple, list))
    if out_specs is None:
        out_specs = tuple(vmem() for _ in out_shape) if many else vmem()
    if grid is None:
        spec = dict(in_specs=in_specs, out_specs=out_specs, scratch_shapes=list(scratch))
    else:
        spec = dict(
            grid_spec=pltpu.PrefetchScalarGridSpec(
                num_scalar_prefetch=prefetch,
                grid=grid,
                in_specs=in_specs,
                out_specs=out_specs,
                scratch_shapes=list(scratch),
            )
        )
    args = [
        pltpu.with_memory_space_constraint(a, pltpu.HBM) if i >= prefetch and in_specs[i - prefetch].memory_space is pltpu.HBM else a
        for i, a in enumerate(args)
    ]
    return pl.pallas_call(
        kernel,
        out_shape=out_shape,
        name=name,
        input_output_aliases=alias or {},
        compiler_params=pltpu.CompilerParams(vmem_limit_bytes=limit * MIB),
        cost_estimate=pl.CostEstimate(flops=int(TIMES[name] * DECLARED), bytes_accessed=0, transcendentals=0),
        **spec,
    )(*args)


def swap(value, mask):
    return lax.ppermute(value, AXES, [(i, i ^ mask) for i in range(32)])


def after(value, *others):
    return lax.optimization_barrier((value,) + others)[0]


def pack_kernel(*refs):
    given, (first, second, third), rest = refs[:15], refs[15:18], refs[18:]
    held, (scr, sems) = rest[:15], rest[15:]
    copies = [pltpu.make_async_copy(src, dst, sems.at[i]) for i, (src, dst) in enumerate(zip(given, held))]
    for copy in copies:
        copy.start()

    def spread(i, dst, col):
        copies[i].wait()
        total = held[i].shape[0]
        rows = dst.shape[0]
        blocks = total // rows
        scr[0:total] = held[i][...].astype(F32)
        for c in range(blocks):
            dst[:, col + c * 128 : col + (c + 1) * 128] = scr[pl.ds(c, rows, stride=blocks), :].astype(BF16)
        return col + blocks * 128

    col = 0
    for i in range(4):
        col = spread(i, first, col)
    for copy in copies[6:]:
        copy.wait()
    rows = first.shape[0]
    lines = [held[6 + i][...].astype(F32).reshape(1, rows) for i in range(8)]
    block = jnp.concatenate(lines, axis=0)
    block = jnp.concatenate([block, jnp.zeros((8, 128 - rows), F32)], axis=1)
    block = jnp.concatenate([block, jnp.zeros((120, 128), F32)], axis=0)
    scr[0:128] = block.T
    wide = held[14][...].astype(F32).reshape(1, 4 * rows)
    scr[0:1, BIAS_AT : BIAS_AT + 4 * rows] = wide
    first[:, col : col + SMALL] = scr[0:rows].astype(BF16)
    spread(4, second, 0)
    spread(5, third, 0)


def pack(weights, vectors, rows, width, hidden):
    flat = [w.reshape(-1, 128) for w in weights]
    ratio = hidden // width
    args = flat + vectors
    return call(
        pack_kernel,
        "pack",
        args,
        [hbm()] * len(args),
        (sds((rows, 4 * width + SMALL)), sds((rows, hidden)), sds((rows * ratio, width))),
        scratch=[pltpu.VMEM(a.shape, BF16) for a in args]
        + [pltpu.VMEM((max(f.shape[0] for f in flat), 128), F32), pltpu.SemaphoreType.DMA((15,))],
        limit=8,
    )


def z_join_kernel(at_ref, a0, a1, a2, a3, out):
    rows = a0.shape[0]
    z = lax.rem(at_ref[0], 4)
    for m, piece in enumerate((a0, a1, a2, a3)):
        out[pl.ds(pl.multiple_of((z ^ m) * rows, 8), rows), :] = piece[...]


def z_swaps(own):
    return [own] + [swap(own, m) for m in (1, 2, 3)]


def z_join(at, pieces):
    rows, cols = pieces[0].shape
    return call(z_join_kernel, "z_join", [at] + pieces, [smem()] + [vmem()] * 4, sds((4 * rows, cols)), limit=8)


def pair_join_kernel(a0, a1, out):
    rows = a0.shape[0]
    out[:rows] = a0[...]
    out[rows:] = a1[...]


def pair_join(own, came):
    rows, cols = own.shape
    return call(pair_join_kernel, "z_join", [own, came], [vmem()] * 2, sds((2 * rows, cols)), limit=4)


def z_join_pairs_kernel(at_ref, a, b, out):
    rows = a.shape[0] // 2
    z = lax.rem(at_ref[0], 4)
    for m in range(4):
        piece = (a, b)[m % 2]
        start = pl.multiple_of((z ^ m) * rows, 8)
        out[pl.ds(start, rows), :] = piece[m // 2 * rows : (m // 2 + 1) * rows]


def z_join_pairs(at, pair, came):
    rows, cols = pair.shape
    return call(z_join_pairs_kernel, "z_join", [at, pair, came], [smem()] + [vmem()] * 2, sds((2 * rows, cols)), limit=8)


def forward_halves(x, y):
    half = x.shape[1] // 256 * 128
    return [swap(x[:, :half], 16), swap(y[:, half:], 8)]


def row_blocks(own, x, y, diag):
    out = []
    for pieces in ([own], [x], [y], diag):
        out += [pieces, [swap(p, 4) for p in pieces]]
    return out


def flat_blocks(blocks):
    return [p for pieces in blocks for p in pieces]


PIECES = 10


def grouped(refs):
    return [[r] for r in refs[:6]] + [list(refs[6:8]), list(refs[8:10])]


def block_copies(at_ref, refs, scr, sems):
    group = at_ref[0] // 4
    lists, k = [], 0
    for m in range(8):
        halves = 2 if m >= 6 else 1
        col, mine = 0, []
        for _ in range(halves):
            rows, cols = refs[k].shape
            start = pl.multiple_of((group ^ m) * rows, 8)
            mine.append(pltpu.make_async_copy(refs[k], scr.at[pl.ds(start, rows), pl.ds(col, cols)], sems.at[k]))
            col += cols
            k += 1
        lists.append(mine)
    return lists


def fetch_all(at_ref, refs, scr, sems):
    lists = block_copies(at_ref, refs, scr, sems)
    for mine in lists:
        for copy in mine:
            copy.start()
    for mine in lists:
        for copy in mine:
            copy.wait()


def store_halves(group, value, keep, send, lead=()):
    part = value.shape[0] // 8
    core = lax.rem(group, 2)
    for b in range(8):
        slot = (group ^ b) // 2
        piece = value[b * part : (b + 1) * part]

        @pl.when(core == b % 2)
        def _():
            keep[lead + (pl.ds(slot, 1),)] = piece[None]

        @pl.when(core != b % 2)
        def _():
            send[lead + (pl.ds(slot, 1),)] = piece[None]


def turned(value):
    return value.astype(F32).T.astype(BF16)


def turn_kernel(at_ref, tokens, keep, send):
    store_halves(at_ref[0] // 4, turned(tokens[...]), keep, send)


def turn_tokens(at, tokens):
    size, width = tokens.shape
    out = sds((4, width // 8, size))
    return call(turn_kernel, "turn_tokens", [at, tokens], [smem(), vmem()], (out, out), limit=8)


def qkv_kernel(at_ref, tokens, *refs):
    pieces, (q, k, v, lines, bias, w_out, scr, sems) = refs[:PIECES], refs[PIECES:]
    width = tokens.shape[1]
    fetch_all(at_ref, pieces, scr, sems)
    w_out[...] = scr[:, 3 * width : 4 * width]
    tails = scr[:, 4 * width :].astype(F32)
    rows = tails.T[:16]
    lines[...] = rows
    each = width // 32
    for d in range(32):
        bias[:, 4 * each * d : 4 * each * (d + 1)] = tails[each * d : each * d + 1, BIAS_AT : BIAS_AT + 4 * each]
    x = tokens[...]
    q[...] = (dot(x, scr[:, :width]) + rows[0:1]).astype(BF16)
    k[...] = dot(x, scr[:, width : 2 * width]).astype(BF16)
    v[...] = (dot(x, scr[:, 2 * width : 3 * width]) + rows[1:2]).astype(BF16)


def project(at, tokens, blocks):
    size, width = tokens.shape
    cols = blocks[0][0].shape[1]
    args = [at, tokens] + flat_blocks(blocks)
    return call(
        qkv_kernel,
        "project",
        args,
        [smem(), vmem()] + [vmem()] * PIECES,
        (sds((size, width)),) * 3 + (sds((16, width), F32), sds((1, 4 * width), F32), sds((width, width))),
        scratch=[pltpu.VMEM((width, cols), BF16), pltpu.SemaphoreType.DMA((PIECES,))],
        limit=14,
    )


def head_lanes(h):
    lane = lax.broadcasted_iota(jnp.int32, (1, 2 * HEAD_DIM), 1)
    return (lane // HEAD_DIM) == h


def attend_kernel(len_ref, q_ref, k_ref, v_ref, mixed_ref, turned_ref, lse_ref):
    length = len_ref[0]
    q, k, v = q_ref[...], k_ref[...], v_ref[...]
    size = q.shape[0]
    keep = lax.broadcasted_iota(jnp.int32, (size, 1), 0) < length
    v_t = turned(v)
    parts = []
    for h in range(2):
        q_head = jnp.where(head_lanes(h), q.astype(F32) * SCALE, 0.0).astype(BF16)
        scores = jnp.where(keep, dot(k, q_head, NT), -1e30)
        top = jnp.max(scores, axis=0, keepdims=True)
        shifted = jnp.exp(scores - top)
        total = jnp.sum(shifted, axis=0, keepdims=True)
        mixed = dot(v_t[h * HEAD_DIM : (h + 1) * HEAD_DIM], shifted.astype(BF16)) / total
        parts.append(mixed)
        lse_ref[0, h : h + 1, :] = top + jnp.log(total)
    mixed = jnp.concatenate(parts, axis=0)
    turned_ref[...] = mixed.astype(BF16)
    mixed_ref[...] = mixed.T.astype(BF16)


def attend(lengths, q, k, v):
    size, width = q.shape
    pairs = width // 128
    tile = pl.BlockSpec((size, 128), lambda i, n: (0, i))
    return call(
        attend_kernel,
        "attend",
        [lengths, q, k, v],
        [tile] * 3,
        (sds((size, width)), sds((width, size)), sds((pairs, 2, size), F32)),
        out_specs=(
            tile,
            pl.BlockSpec((128, size), lambda i, n: (i, 0)),
            pl.BlockSpec((1, 2, size), lambda i, n: (i, 0, 0)),
        ),
        grid=(pairs,),
        prefetch=1,
        limit=12,
    )


def normed(values):
    centred = values - jnp.mean(values, axis=-1, keepdims=True)
    scale = lax.rsqrt(jnp.mean(centred * centred, axis=-1, keepdims=True) + EPSILON)
    return centred * scale, scale


def norm_back(grad, unit, scale):
    return scale * (
        grad - jnp.mean(grad, axis=-1, keepdims=True) - unit * jnp.mean(grad * unit, axis=-1, keepdims=True)
    )


def mix_kernel(at_ref, tokens, mixed, mixed_t, lines, w_out, unit_out, scale_out, normed_out, keep, send):
    group = at_ref[0] // 4
    normed_out[...] = mixed[...]
    step = 128

    def rows(i, carry):
        part = pl.ds(pl.multiple_of(i * step, step), step)
        resid = tokens[part, :].astype(F32) + dot(mixed[part, :], w_out[...]) + lines[2:3]
        unit, scale = normed(resid)
        unit_out[part, :] = unit
        scale_out[part, :] = jnp.broadcast_to(scale, (step, scale_out.shape[1]))
        normed_out[part, :] = (unit * lines[3:4] + lines[4:5]).astype(BF16)
        return carry

    lax.fori_loop(0, tokens.shape[0] // step, rows, 0)
    store_halves(group, mixed_t[...], keep, send, (0,))
    store_halves(group, turned(normed_out[...]), keep, send, (1,))


def mix_stage(at, tokens, mixed, mixed_t, lines, w_out):
    size, width = tokens.shape
    half = sds((2, 4, width // 8, size))
    return call(
        mix_kernel,
        "mix",
        [at, tokens, mixed, mixed_t, lines, w_out],
        [smem()] + [vmem()] * 5,
        (sds((size, width), F32), sds((size, 128), F32), sds((size, width)), half, half),
        limit=10,
    )


def inner_kernel(at_ref, values, bias, *refs):
    pieces = refs[:PIECES]
    (activ, slope, scr, keep, send, sems) = refs[PIECES:]
    part = activ.shape[1] // 8
    group = at_ref[0] // 4
    core = lax.rem(group, 2)
    fetch_all(at_ref, pieces, scr, sems)

    def step(b, carry):
        at = pl.multiple_of(b * part, 128)
        inner = dot(values[...], scr[:, pl.ds(at, part)]) + bias[:, pl.ds(at, part)]
        share = 0.5 * (1.0 + lax.erf(inner * 0.7071067811865476))
        result = inner * share
        activ[:, pl.ds(at, part)] = result.astype(BF16)
        slope[:, pl.ds(at, part)] = (share + inner * (0.3989422804014327 * jnp.exp(-0.5 * inner * inner))).astype(BF16)
        across = result.T.astype(BF16)
        slot = (group ^ b) // 2

        @pl.when(core == lax.rem(b, 2))
        def _():
            keep[pl.ds(slot, 1)] = across[None]

        @pl.when(core != lax.rem(b, 2))
        def _():
            send[pl.ds(slot, 1)] = across[None]

        return carry

    lax.fori_loop(0, 8, step, 0)


def inner_stage(at, values, bias, blocks):
    size, width = values.shape
    hidden = bias.shape[1]
    args = [at, values, bias] + flat_blocks(blocks)
    half = sds((4, hidden // 8, size))
    return call(
        inner_kernel,
        "inner",
        args,
        [smem()] + [vmem()] * (2 + PIECES),
        (sds((size, hidden)), sds((size, hidden)), sds((width, hidden)), half, half),
        scratch=[pltpu.SemaphoreType.DMA((PIECES,))],
        limit=14,
    )


def outer_kernel(at_ref, len_ref, activ, values, lines, cot, *refs):
    pieces, (output, resid_grad, outer_grad, sums, acc) = refs[:PIECES], refs[PIECES:]
    size = values.shape[0]
    part = activ.shape[1] // 8
    group = at_ref[0] // 4
    resid = values[...].astype(F32) + lines[5:6]
    for m, mine in enumerate(grouped(pieces)):
        given = activ[:, pl.ds(pl.multiple_of((group ^ m) * part, 128), part)]
        products = [dot(given, piece[...]) for piece in mine]
        resid += products[0] if len(products) == 1 else jnp.concatenate(products, axis=1)
    acc[...] = resid
    gain, shift = lines[6:7], lines[7:8]
    sums[...] = jnp.zeros_like(sums)
    step = 128

    def rows(i, carry):
        part = pl.ds(pl.multiple_of(i * step, step), step)
        unit, scale = normed(acc[part, :])
        valid = lax.broadcasted_iota(jnp.int32, (step, 1), 0) + i * step < len_ref[0]
        output[part, :] = jnp.where(valid, unit * gain + shift, 0.0).astype(BF16)
        grad = jnp.where(valid, cot[part, :].astype(F32), 0.0)
        sums[6:7] += jnp.sum(grad * unit, axis=0, keepdims=True)
        sums[7:8] += jnp.sum(grad, axis=0, keepdims=True)
        grad = norm_back(grad * gain, unit, scale)
        resid_grad[part, :] = grad
        rounded = grad.astype(BF16)
        outer_grad[part, :] = rounded
        sums[5:6] += jnp.sum(rounded.astype(F32), axis=0, keepdims=True)
        return carry

    lax.fori_loop(0, size // step, rows, 0)


def outer_stage(at, lengths, activ, values, lines, cot, blocks):
    size, width = values.shape
    hidden = activ.shape[1]
    args = [at, lengths, activ, values, lines, cot] + flat_blocks(blocks)
    return call(
        outer_kernel,
        "outer",
        args,
        [smem(), smem()] + [vmem()] * (4 + PIECES),
        (sds((size, width)), sds((size, width), F32), sds((size, width)), sds((8, width), F32)),
        scratch=[pltpu.VMEM((size, width), F32)],
        limit=10,
    )


def slope_kernel(at_ref, outer_grad, slope, *refs):
    pieces, (inner_grad, sums) = refs[:PIECES], refs[PIECES:]
    part = slope.shape[1] // 8
    group = at_ref[0] // 4
    grad = outer_grad[...]
    for m, mine in enumerate(grouped(pieces)):
        at = pl.multiple_of((group ^ m) * part, 128)
        back, col = 0.0, 0
        for piece in mine:
            cols = piece.shape[1]
            back += dot(grad[:, col : col + cols], piece[...], NT)
            col += cols
        rounded = (back * slope[:, pl.ds(at, part)].astype(F32)).astype(BF16)
        inner_grad[:, pl.ds(at, part)] = rounded
        sums[:, pl.ds(at, part)] = jnp.sum(rounded.astype(F32), axis=0, keepdims=True)


def slope_stage(at, outer_grad, slope, blocks):
    size, width = outer_grad.shape
    hidden = slope.shape[1]
    args = [at, outer_grad, slope] + flat_blocks(blocks)
    return call(
        slope_kernel,
        "slope",
        args,
        [smem()] + [vmem()] * (2 + PIECES),
        (sds((size, hidden)), sds((1, hidden), F32)),
        limit=10,
    )


def normed_back_kernel(inner_grad, resid_two, unit_ref, scale_ref, lines, w_out, weights, resid_grad, attn_low, attn_high, mixed_grad, sums):
    width = unit_ref.shape[1]
    hidden = inner_grad.shape[1]
    grad = resid_two[...]
    for c in range(0, hidden, width):
        grad += dot(inner_grad[:, c : c + width], weights[:, c : c + width], NT)
    half = attn_low.shape[1]
    resid_grad[...] = grad
    sums[...] = jnp.zeros_like(sums)
    step = 128

    def rows(i, carry):
        part = pl.ds(pl.multiple_of(i * step, step), step)
        unit = unit_ref[part, :]
        grad = resid_grad[part, :]
        sums[3:4] += jnp.sum(grad * unit, axis=0, keepdims=True)
        sums[4:5] += jnp.sum(grad, axis=0, keepdims=True)
        grad = norm_back(grad * lines[3:4], unit, scale_ref[part, 0:1])
        resid_grad[part, :] = grad
        rounded = grad.astype(BF16)
        attn_low[part, :] = rounded[:, :half]
        attn_high[part, :] = rounded[:, half:]
        sums[2:3] += jnp.sum(rounded.astype(F32), axis=0, keepdims=True)
        return carry

    lax.fori_loop(0, grad.shape[0] // step, rows, 0)
    back = dot(attn_low[...], w_out[:, :half], NT) + dot(attn_high[...], w_out[:, half:], NT)
    mixed_grad[...] = back.astype(BF16)


def normed_back(inner_grad, resid_two, unit, scale, lines, w_out, weights):
    size, width = unit.shape
    hidden = inner_grad.shape[1]
    args = [inner_grad, resid_two, unit, scale, lines, w_out, weights]
    return call(
        normed_back_kernel,
        "normed_back",
        args,
        [vmem()] * 7,
        (sds((size, width), F32),)
        + (sds((size, width // 2)),) * 2
        + (sds((size, width)), sds((8, width), F32)),
        limit=12,
    )


def attend_back_kernel(len_ref, q_ref, k_ref, v_ref, mixed_ref, grad_ref, lse_ref, grads_ref, qs_ref, vs_ref):
    length = len_ref[0]
    q, k, v, grad = q_ref[...], k_ref[...], v_ref[...], grad_ref[...]
    size = q.shape[0]
    keep = lax.broadcasted_iota(jnp.int32, (size, 1), 0) < length
    k_t = turned(k)
    prod_t = turned(grad).astype(F32) * mixed_ref[...].astype(F32)
    q_grad, k_grad, v_grad = [], 0.0, 0.0
    for h in range(2):
        mine = head_lanes(h)
        q_head = jnp.where(mine, q.astype(F32) * SCALE, 0.0).astype(BF16)
        g_head = jnp.where(mine, grad, jnp.zeros_like(grad))
        scores = jnp.where(keep, dot(k, q_head, NT), -1e30)
        probs = jnp.exp(scores - lse_ref[0, h : h + 1, :])
        delta = jnp.sum(prod_t[h * HEAD_DIM : (h + 1) * HEAD_DIM], axis=0, keepdims=True)
        prob_grad = dot(v, g_head, NT)
        score_grad = (probs * (prob_grad - delta)).astype(BF16)
        v_grad += dot(probs.astype(BF16), g_head)
        k_grad += dot(score_grad, q_head)
        q_grad.append(dot(k_t[h * HEAD_DIM : (h + 1) * HEAD_DIM], score_grad))
    q_rounded = (jnp.concatenate(q_grad, axis=0) * SCALE).T.astype(BF16)
    v_rounded = v_grad.astype(BF16)
    grads_ref[0] = q_rounded
    grads_ref[1] = k_grad.astype(BF16)
    grads_ref[2] = v_rounded
    qs_ref[...] = jnp.sum(q_rounded.astype(F32), axis=0, keepdims=True)
    vs_ref[...] = jnp.sum(v_rounded.astype(F32), axis=0, keepdims=True)


def attend_back(lengths, q, k, v, mixed_t, grad, lse):
    size, width = q.shape
    pairs = width // 128
    tile = pl.BlockSpec((size, 128), lambda i, n: (0, i))
    out = pl.BlockSpec((3, size, 128), lambda i, n: (0, 0, i))
    line = pl.BlockSpec((1, 128), lambda i, n: (0, i))
    return call(
        attend_back_kernel,
        "attend_back",
        [lengths, q, k, v, mixed_t, grad, lse],
        [tile] * 3
        + [
            pl.BlockSpec((128, size), lambda i, n: (i, 0)),
            tile,
            pl.BlockSpec((1, 2, size), lambda i, n: (i, 0, 0)),
        ],
        (sds((3, size, width)),) + (sds((1, width), F32),) * 2,
        out_specs=(out,) + (line,) * 2,
        grid=(pairs,),
        prefetch=1,
        limit=12,
    )


def tokens_kernel(at_ref, resid_grad, *refs):
    grads, pieces, (out, scr, sems) = refs[0], refs[1 : 1 + PIECES], refs[1 + PIECES :]
    width = resid_grad.shape[1]
    fetch_all(at_ref, pieces, scr, sems)
    total = resid_grad[...]
    for i in range(3):
        total += dot(grads[i], scr[:, i * width : (i + 1) * width], NT)
    out[...] = total.astype(BF16)


def tokens_back(at, resid_grad, grads, blocks):
    size, width = resid_grad.shape
    cols = blocks[0][0].shape[1]
    args = [at, resid_grad, grads] + flat_blocks(blocks)
    return call(
        tokens_kernel,
        "tokens_back",
        args,
        [smem()] + [vmem()] * 2 + [hbm()] * PIECES,
        sds((size, width)),
        scratch=[pltpu.VMEM((width, cols), BF16), pltpu.SemaphoreType.DMA((PIECES,))],
        limit=14,
    )


def small_kernel(one, two, q_sum, v_sum, bias, out):
    width = one.shape[1]
    out[0:8] = one[...] + two[...]
    out[8:16] = jnp.zeros((8, width), F32)
    out[0:1], out[1:2] = q_sum[...], v_sum[...]
    for r in range(4):
        out[12 + r : 13 + r] = bias[:, r * width : (r + 1) * width]


def stack_small(*args):
    one = args[0]
    return call(small_kernel, "stack_small", list(args), [vmem()] * 5, sds((16, one.shape[1]), F32), limit=4)


def put_slots(value, col, outs):
    s0, s1, s2, s3a, s3b = outs
    part, cols = s0.shape
    half = s3a.shape[1]
    width = value.shape[1]
    for s, out in enumerate((s0, s1, s2)):
        out[:, col : col + width] = value[s * part : (s + 1) * part]
    last = value[3 * part : 4 * part]
    cut = min(max(half - col, 0), width)
    if cut > 0:
        s3a[:, col : col + cut] = last[:, :cut]
    if cut < width:
        s3b[:, col + cut - half : col + width - half] = last[:, cut:]


def slot_shapes(part, cols):
    half = cols // 256 * 128
    return (sds((part, cols)),) * 3 + (sds((part, half)), sds((part, cols - half)))


def grad_kernel(plan, small, *refs):
    outs = refs[-5:]
    if small:
        outs, scr = refs[-6:-1], refs[-1]
    part = outs[0].shape[0]
    col = 0
    for left, lead, mine, came, which in plan:
        rows = 4 * part
        size = refs[left].shape[-1]
        a = refs[left][lead] if lead is not None else refs[left][...]
        b = refs[left + 1][lead] if lead is not None else refs[left + 1][...]
        a, b = a.reshape(rows, size), b.reshape(rows, size)
        total = refs[mine].shape[-1]
        step = min(total, 768)
        for start in range(0, total, step):
            at = which + (slice(None), slice(start, start + step))
            value = dot(a, refs[mine][at]) + dot(b, refs[came][at])
            put_slots(value.astype(BF16), col, outs)
            col += step
    if small:
        at_ref, own, came = refs[small], refs[small + 1], refs[small + 2]
        both = own[...] + came[...]
        padded = jnp.concatenate([both, jnp.zeros((SMALL - both.shape[0], both.shape[1]), F32)], axis=0)
        scr[...] = padded.T
        each = 4 * scr.shape[0] // 32
        wide = scr.shape[0]
        for d in range(32):
            row, lane = 12 + each * d // wide, each * d % wide
            scr[wide // 32 * d : wide // 32 * d + 1, BIAS_AT : BIAS_AT + each] = both[row : row + 1, lane : lane + each]
        group = at_ref[0] // 4
        value = jnp.concatenate(
            [scr[pl.ds(pl.multiple_of((group ^ (2 * s)) * part, 8), part), :] for s in range(4)], axis=0
        )
        put_slots(value.astype(BF16), col, outs)


def weight_grad(name, args, plan, part, cols, small=None):
    specs = [vmem()] * len(args)
    scratch = []
    if small:
        specs[small] = smem()
        scratch = [pltpu.VMEM((8 * part, SMALL), F32)]
    return call(
        functools.partial(grad_kernel, plan, small),
        name,
        args,
        specs,
        slot_shapes(part, cols),
        scratch=scratch,
        limit=14,
    )


def add_kernel(x_ref, p_ref, y_ref, q_ref, x_out, y_out):
    x_out[...] = (x_ref[...].astype(F32) + p_ref[...].astype(F32)).astype(BF16)
    y_out[...] = (y_ref[...].astype(F32) + q_ref[...].astype(F32)).astype(BF16)


def add_halves(x, p, y, q):
    part, cols = x.shape
    half = p.shape[1]
    rest = cols - half
    if half != rest:
        return add_uneven(x, p, y, q)
    low = pl.BlockSpec((part, half), lambda i: (0, 0))
    high = pl.BlockSpec((part, half), lambda i: (0, 1))
    return call(
        add_kernel,
        "add_halves",
        [x, p, y, q],
        [low, low, high, low],
        (sds(x.shape), sds(y.shape)),
        out_specs=(low, high),
        grid=(1,),
        alias={0: 0, 2: 1},
        limit=16,
    )


def uneven_kernel(x_ref, p_ref, y_ref, q_ref, x_out, y_out):
    half = p_ref.shape[1]
    x_out[...] = x_ref[...]
    y_out[...] = y_ref[...]
    x_out[:, :half] = (x_ref[:, :half].astype(F32) + p_ref[...].astype(F32)).astype(BF16)
    y_out[:, half:] = (y_ref[:, half:].astype(F32) + q_ref[...].astype(F32)).astype(BF16)


def add_uneven(x, p, y, q):
    return call(
        uneven_kernel,
        "add_halves",
        [x, p, y, q],
        [vmem()] * 4,
        (sds(x.shape), sds(y.shape)),
        limit=16,
    )


def plane_sum_kernel(near, at_ref, a0, a1, a2, keep, send, total):
    total[...] = a0[...].astype(F32) + (a1[...].astype(F32) + a2[...].astype(F32))
    rows = keep.shape[0] // 2
    z = lax.rem(at_ref[0], 4)
    for m in range(4):
        side, place = (m % 2, m // 2) if near else (m // 2, m % 2)
        out = (keep, send)[side]
        part = total[pl.ds(pl.multiple_of((z ^ m) * rows, 8), rows), :]
        out[place * rows : (place + 1) * rows] = part.astype(BF16)


def plane_sum(at, pieces, near=False):
    part, cols = pieces[0].shape
    return call(
        functools.partial(plane_sum_kernel, near),
        "plane_sum",
        [at] + pieces,
        [smem()] + [vmem()] * 3,
        (sds((part // 2, cols)),) * 2,
        scratch=[pltpu.VMEM((part, cols), F32)],
        limit=6,
    )


def pair_sum_kernel(keep, came, own, send):
    rows = own.shape[0]
    total = keep[...].astype(F32) + came[...].astype(F32)
    own[...] = total[:rows]
    send[...] = total[rows:].astype(BF16)


def pair_sum(keep, came):
    rows, cols = keep.shape[0] // 2, keep.shape[1]
    return call(
        pair_sum_kernel,
        "pair_sum",
        [keep, came],
        [vmem()] * 2,
        (sds((rows, cols), F32), sds((rows, cols))),
        limit=8,
    )


def finish_kernel(widths, tail, own, came, *outs):
    total = own[...] + came[...].astype(F32)
    rows = total.shape[0]
    col = 0
    for width, out in zip(widths, outs):
        blocks = width // 128
        for c in range(blocks):
            out[pl.ds(c, rows, stride=blocks), :] = total[:, col + c * 128 : col + (c + 1) * 128]
        col += width
    if tail:
        block = jnp.concatenate([total[:, col : col + SMALL], jnp.zeros((SMALL - rows, SMALL), F32)], axis=0).T
        for i in range(8):
            outs[len(widths) + i][...] = block[i : i + 1, :rows].reshape(rows)
        outs[len(widths) + 8][...] = total[0:1, col + BIAS_AT : col + BIAS_AT + 4 * rows].reshape(4 * rows)


def finish(pieces, widths, tail=False):
    rows = pieces[0].shape[0]
    shapes = [sds((rows * w // 128, 128), F32) for w in widths]
    if tail:
        shapes += [sds((rows,), F32)] * 8 + [sds((4 * rows,), F32)]
    outs = call(
        functools.partial(finish_kernel, widths, tail),
        "finish",
        pieces,
        [vmem()] * 2,
        tuple(shapes),
        limit=6,
    )
    return [o.reshape(-1) for o in outs]


def scatter_plane(slots, *done):
    s0, s1, s2, s3a, s3b = slots
    p, q = swap(s3a, 16), swap(s3b, 8)
    s1 = after(s1, *done)
    x, y = add_halves(s1, p, s2, q)
    return [s0, swap(x, 8), swap(y, 16), x]


def first_z(sums, *done, near=False):
    keep, send = sums
    return pair_sum(after(keep, *done), swap(send, 1 if near else 2))


def blocked_layer(
    tokens,
    lengths,
    query_weight,
    query_bias,
    key_weight,
    value_weight,
    value_bias,
    output_weight,
    output_bias,
    attn_gain,
    attn_shift,
    inner_weight,
    inner_bias,
    outer_weight,
    outer_bias,
    ffn_gain,
    ffn_shift,
    cotangent,
):
    size, width = tokens.shape
    rows = query_weight.shape[0] // width
    hidden = inner_weight.shape[0] // rows
    ratio = hidden // width
    at = lax.axis_index(AXES).astype(jnp.int32).reshape(1)

    first, second, third = pack(
        [query_weight, key_weight, value_weight, output_weight, inner_weight, outer_weight],
        [query_bias, value_bias, output_bias, attn_gain, attn_shift, outer_bias, ffn_gain, ffn_shift, inner_bias],
        rows,
        width,
        hidden,
    )
    z_first = z_join(at, z_swaps(first))
    x_first, y_first = swap(z_first, 8), swap(z_first, 16)
    second = after(second, z_first)
    second = pair_join(second, swap(second, 2))
    x_first, second = lax.optimization_barrier((x_first, second))
    f_first = forward_halves(x_first, y_first)
    first_blocks = row_blocks(z_first, x_first, y_first, f_first)
    z_second = z_join_pairs(at, second, swap(second, 1))
    x_second, y_second = swap(z_second, 8), swap(z_second, 16)
    third = after(third, z_second, first_blocks[7][0], first_blocks[7][1])
    third_came = swap(third, 2)

    tok_keep, tok_send = turn_tokens(at, tokens)
    tok_came = swap(tok_send, 4)
    queries, key_rows, value_rows, lines, bias, w_out = project(at, tokens, first_blocks)
    mixed, mixed_t, lse = attend(lengths, queries, key_rows, value_rows)
    third = pair_join(third, after(third_came, mixed))
    mixed, x_second, y_second, third = lax.optimization_barrier((mixed, x_second, y_second, third))
    f_second = forward_halves(x_second, y_second)
    unit, scale, values, b_keep, b_send = mix_stage(at, tokens, after(mixed, tok_came), mixed_t, lines, w_out)
    b_came = swap(b_send, 4)
    second_blocks = row_blocks(z_second, x_second, y_second, f_second)
    z_third = z_join_pairs(at, third, after(swap(third, 1), *f_second))
    x_third, y_third = swap(z_third, 8), swap(z_third, 16)
    activ, slope, w_inner, a_keep, a_send = inner_stage(at, after(values, z_third), bias, second_blocks)
    activ, x_third, y_third = lax.optimization_barrier((activ, x_third, y_third))
    f_third = forward_halves(x_third, y_third)
    third_blocks = row_blocks(z_third, x_third, y_third, f_third)
    a_came = swap(after(a_send, x_third), 4)
    activ = after(activ, a_came)
    output, resid_two_grad, outer_grad, sums_two = outer_stage(at, lengths, activ, values, lines, cotangent, third_blocks)

    outer_came = swap(outer_grad, 4)
    inner_grad, bias_grad = slope_stage(at, outer_grad, slope, third_blocks)
    inner_came = swap(after(inner_grad, outer_came), 4)
    slots_a = weight_grad(
        "grad_outer",
        [a_keep, a_came, outer_grad, after(outer_came, inner_grad)],
        [(0, None, 2, 3, ())],
        hidden // 8,
        width,
    )
    resid_one_grad, attn_low, attn_high, mixed_grad, sums_one = normed_back(
        after(inner_grad, slots_a[0]), resid_two_grad, unit, scale, lines, w_out, w_inner
    )
    plane_a = scatter_plane(slots_a, attn_low)
    low_came, high_came = (swap(after(g, plane_a[3]), 4) for g in (attn_low, attn_high))
    slots_b = weight_grad(
        "grad_inner",
        [b_keep, b_came, attn_low, low_came, attn_high, high_came, inner_grad, inner_came],
        [(0, 0, 2, 3, ()), (0, 0, 4, 5, ()), (0, 1, 6, 7, ())],
        width // 8,
        width + hidden,
    )
    grads, q_sum, v_sum = attend_back(
        lengths, queries, key_rows, value_rows, mixed_t, after(mixed_grad, slots_b[0]), lse
    )
    plane_b = scatter_plane(slots_b, grads)
    sums_a = plane_sum(at, [after(plane_a[0], plane_b[3])] + plane_a[1:3])
    grads_came = swap(after(grads, sums_a[0]), 4)
    small = stack_small(sums_one, sums_two, q_sum, v_sum, bias_grad)
    small_came = swap(small, 4)
    args = [tok_keep, tok_came, grads, grads_came]
    plan = [(0, None, 2, 3, (i,)) for i in range(3)]
    slots_c = weight_grad(
        "grad_first",
        args + [at, small, small_came],
        plan,
        width // 8,
        3 * width + SMALL,
        small=len(args),
    )
    tokens_grad = tokens_back(at, after(resid_one_grad, slots_c[0]), grads, first_blocks)
    own_a, last_a = first_z(sums_a, tokens_grad)
    slots_c = list(slots_c)
    slots_c[3], slots_c[4], _ = lax.optimization_barrier((slots_c[3], slots_c[4], own_a))
    sums_b = plane_sum(at, [after(plane_b[0], own_a)] + plane_b[1:3], True)
    plane_c = scatter_plane(slots_c, sums_b[0])
    (own_u,) = finish([own_a, swap(after(last_a, sums_b[0]), 1)], [width])
    own_b, last_b = first_z(sums_b, near=True)
    own_o, own_i = finish([own_b, swap(last_b, 2)], [width, hidden])
    sums_c = plane_sum(at, [after(plane_c[0], own_o, own_u)] + plane_c[1:3], True)
    own_c, last_c = first_z(sums_c, near=True)
    own_q, own_k, own_v, qb, vb, ob, ag, ash, ub, fg, fs, ib = finish(
        [own_c, swap(last_c, 2)], [width] * 3, tail=True
    )
    return (output, tokens_grad, own_q, qb, own_k, own_v, vb, own_o, ob, ag, ash, own_i, ib, own_u, ub, fg, fs)


def layer_norm(values, norm_gain, norm_shift):
    row_mean = jnp.mean(values, axis=-1, keepdims=True)
    centred = values - row_mean
    row_var = jnp.mean(centred * centred, axis=-1, keepdims=True)
    return centred * lax.rsqrt(row_var + EPSILON) * norm_gain + norm_shift


def gelu_exact(values):
    return jax.nn.gelu(values, approximate=False)


def matmul(left, right):
    return jnp.dot(left, right, preferred_element_type=jnp.float32)


def left_product(left, right):
    return jnp.einsum("rd,rf->df", left, right, preferred_element_type=jnp.float32)


def right_product(left, right):
    return jnp.einsum("rf,df->rd", left, right, preferred_element_type=jnp.float32)


def column_sums(values):
    return jnp.sum(values.astype(jnp.float32), axis=0)


def unpack(gathered, model_width):
    (
        query_weight,
        query_bias,
        key_weight,
        value_weight,
        value_bias,
        output_weight,
        output_bias,
        attn_gain,
        attn_shift,
        inner_weight,
        inner_bias,
        outer_weight,
        outer_bias,
        ffn_gain,
        ffn_shift,
    ) = gathered
    hidden_width = inner_bias.shape[0]
    return (
        query_weight.reshape(model_width, model_width),
        query_bias,
        key_weight.reshape(model_width, model_width),
        value_weight.reshape(model_width, model_width),
        value_bias,
        output_weight.reshape(model_width, model_width),
        output_bias,
        attn_gain.astype(jnp.float32),
        attn_shift.astype(jnp.float32),
        inner_weight.reshape(model_width, hidden_width),
        inner_bias,
        outer_weight.reshape(hidden_width, model_width),
        outer_bias,
        ffn_gain.astype(jnp.float32),
        ffn_shift.astype(jnp.float32),
    )


def scores_of(query_seq, key_seq, keep_row):
    scores = (
        jnp.einsum("qhd,khd->hqk", query_seq, key_seq, preferred_element_type=jnp.float32) * SCALE
    )
    return jnp.where(keep_row[None, None, :], scores, -1e30)


def attend_forward(seq_item):
    query_seq, key_seq, value_seq, keep_row = seq_item
    scores = scores_of(query_seq, key_seq, keep_row)
    top = jnp.max(scores, axis=-1, keepdims=True)
    shifted_exp = jnp.exp(scores - top)
    total = jnp.sum(shifted_exp, axis=-1, keepdims=True)
    probs = (shifted_exp / total).astype(jnp.bfloat16)
    mixed = jnp.einsum("hqk,khd->qhd", probs, value_seq, preferred_element_type=jnp.float32)
    return (mixed.astype(jnp.bfloat16), (top + jnp.log(total))[..., 0])


def attend_backward(seq_item):
    query_seq, key_seq, value_seq, keep_row, log_total, mixed_grad = seq_item
    scores = scores_of(query_seq, key_seq, keep_row)
    probs = jnp.exp(scores - log_total[..., None])
    value_grad = jnp.einsum(
        "hqk,qhd->khd", probs.astype(jnp.bfloat16), mixed_grad, preferred_element_type=jnp.float32
    )
    prob_grad = jnp.einsum(
        "qhd,khd->hqk", mixed_grad, value_seq, preferred_element_type=jnp.float32
    )
    row_delta = jnp.sum(probs * prob_grad, axis=-1, keepdims=True)
    score_grad = (probs * (prob_grad - row_delta)).astype(jnp.bfloat16)
    query_grad = (
        jnp.einsum("hqk,khd->qhd", score_grad, key_seq, preferred_element_type=jnp.float32) * SCALE
    )
    key_grad = (
        jnp.einsum("hqk,qhd->khd", score_grad, query_seq, preferred_element_type=jnp.float32)
        * SCALE
    )
    return (
        query_grad.astype(jnp.bfloat16),
        key_grad.astype(jnp.bfloat16),
        value_grad.astype(jnp.bfloat16),
    )


def plain_layer(
    tokens,
    lengths,
    query_weight,
    query_bias,
    key_weight,
    value_weight,
    value_bias,
    output_weight,
    output_bias,
    attn_gain,
    attn_shift,
    inner_weight,
    inner_bias,
    outer_weight,
    outer_bias,
    ffn_gain,
    ffn_shift,
    cotangent,
):
    row_count = tokens.shape[0]
    model_width = tokens.shape[1]
    seq_count = lengths.shape[0]
    seq_len = row_count // seq_count
    gathered = (
        lax.all_gather(query_weight, ("wide", "narrow"), axis=0, tiled=True),
        lax.all_gather(query_bias, ("wide", "narrow"), axis=0, tiled=True),
        lax.all_gather(key_weight, ("wide", "narrow"), axis=0, tiled=True),
        lax.all_gather(value_weight, ("wide", "narrow"), axis=0, tiled=True),
        lax.all_gather(value_bias, ("wide", "narrow"), axis=0, tiled=True),
        lax.all_gather(output_weight, ("wide", "narrow"), axis=0, tiled=True),
        lax.all_gather(output_bias, ("wide", "narrow"), axis=0, tiled=True),
        lax.all_gather(attn_gain, ("wide", "narrow"), axis=0, tiled=True),
        lax.all_gather(attn_shift, ("wide", "narrow"), axis=0, tiled=True),
        lax.all_gather(inner_weight, ("wide", "narrow"), axis=0, tiled=True),
        lax.all_gather(inner_bias, ("wide", "narrow"), axis=0, tiled=True),
        lax.all_gather(outer_weight, ("wide", "narrow"), axis=0, tiled=True),
        lax.all_gather(outer_bias, ("wide", "narrow"), axis=0, tiled=True),
        lax.all_gather(ffn_gain, ("wide", "narrow"), axis=0, tiled=True),
        lax.all_gather(ffn_shift, ("wide", "narrow"), axis=0, tiled=True),
    )
    (
        full_qw,
        full_qb,
        full_kw,
        full_vw,
        full_vb,
        full_ow,
        full_ob,
        full_ag,
        full_as,
        full_iw,
        full_ib,
        full_uw,
        full_ub,
        full_fg,
        full_fs,
    ) = unpack(gathered, model_width)
    positions = jnp.arange(seq_len, dtype=jnp.int32)
    keep = positions[None, :] < lengths[:, None]
    row_valid = keep.reshape(row_count, 1).astype(jnp.float32)
    shape_four = (seq_count, seq_len, HEADS, HEAD_DIM)
    queries = (matmul(tokens, full_qw) + full_qb).astype(jnp.bfloat16)
    key_rows = matmul(tokens, full_kw).astype(jnp.bfloat16)
    value_rows = (matmul(tokens, full_vw) + full_vb).astype(jnp.bfloat16)
    query_four = queries.reshape(shape_four)
    key_four = key_rows.reshape(shape_four)
    value_four = value_rows.reshape(shape_four)
    mixed, log_total = lax.map(attend_forward, (query_four, key_four, value_four, keep))
    mixed_flat = mixed.reshape(row_count, model_width)
    resid_one = tokens.astype(jnp.float32) + matmul(mixed_flat, full_ow) + full_ob
    normed_one = layer_norm(resid_one, full_ag, full_as).astype(jnp.bfloat16)
    inner = matmul(normed_one, full_iw) + full_ib
    activ = gelu_exact(inner).astype(jnp.bfloat16)
    resid_two = normed_one.astype(jnp.float32) + matmul(activ, full_uw) + full_ub
    output = (layer_norm(resid_two, full_fg, full_fs) * row_valid).astype(jnp.bfloat16)
    (
        back_qw,
        back_qb,
        back_kw,
        back_vw,
        back_vb,
        back_ow,
        back_ob,
        back_ag,
        back_as,
        back_iw,
        back_ib,
        back_uw,
        back_ub,
        back_fg,
        back_fs,
    ) = unpack(gathered, model_width)
    out_grad = cotangent.astype(jnp.float32) * row_valid
    ignored, pull_two = jax.vjp(layer_norm, resid_two, back_fg, back_fs)
    resid_two_grad, ffn_gain_grad, ffn_shift_grad = pull_two(out_grad)
    outer_grad = resid_two_grad.astype(jnp.bfloat16)
    outer_weight_grad = left_product(activ, outer_grad)
    outer_bias_grad = column_sums(outer_grad)
    activ_grad = right_product(outer_grad, back_uw)
    ignored, pull_gelu = jax.vjp(gelu_exact, inner)
    inner_grad = pull_gelu(activ_grad)[0].astype(jnp.bfloat16)
    inner_weight_grad = left_product(normed_one, inner_grad)
    inner_bias_grad = column_sums(inner_grad)
    normed_grad = resid_two_grad + right_product(inner_grad, back_iw)
    ignored, pull_one = jax.vjp(layer_norm, resid_one, back_ag, back_as)
    resid_one_grad, attn_gain_grad, attn_shift_grad = pull_one(normed_grad)
    attn_grad = resid_one_grad.astype(jnp.bfloat16)
    output_weight_grad = left_product(mixed_flat, attn_grad)
    output_bias_grad = column_sums(attn_grad)
    mixed_grad = right_product(attn_grad, back_ow).astype(jnp.bfloat16)
    query_grad, key_grad, value_grad = lax.map(
        attend_backward,
        (query_four, key_four, value_four, keep, log_total, mixed_grad.reshape(shape_four)),
    )
    query_grad = query_grad.reshape(row_count, model_width)
    key_grad = key_grad.reshape(row_count, model_width)
    value_grad = value_grad.reshape(row_count, model_width)
    query_weight_grad = left_product(tokens, query_grad)
    key_weight_grad = left_product(tokens, key_grad)
    value_weight_grad = left_product(tokens, value_grad)
    query_bias_grad = column_sums(query_grad)
    value_bias_grad = column_sums(value_grad)
    tokens_grad = (
        resid_one_grad
        + right_product(query_grad, back_qw)
        + right_product(key_grad, back_kw)
        + right_product(value_grad, back_vw)
    ).astype(jnp.bfloat16)
    (
        own_qw,
        own_qb,
        own_kw,
        own_vw,
        own_vb,
        own_ow,
        own_ob,
        own_ag,
        own_as,
        own_iw,
        own_ib,
        own_uw,
        own_ub,
        own_fg,
        own_fs,
    ) = (
        lax.psum_scatter(
            query_weight_grad.reshape(-1), ("wide", "narrow"), scatter_dimension=0, tiled=True
        ),
        lax.psum_scatter(query_bias_grad, ("wide", "narrow"), scatter_dimension=0, tiled=True),
        lax.psum_scatter(
            key_weight_grad.reshape(-1), ("wide", "narrow"), scatter_dimension=0, tiled=True
        ),
        lax.psum_scatter(
            value_weight_grad.reshape(-1), ("wide", "narrow"), scatter_dimension=0, tiled=True
        ),
        lax.psum_scatter(value_bias_grad, ("wide", "narrow"), scatter_dimension=0, tiled=True),
        lax.psum_scatter(
            output_weight_grad.reshape(-1), ("wide", "narrow"), scatter_dimension=0, tiled=True
        ),
        lax.psum_scatter(output_bias_grad, ("wide", "narrow"), scatter_dimension=0, tiled=True),
        lax.psum_scatter(attn_gain_grad, ("wide", "narrow"), scatter_dimension=0, tiled=True),
        lax.psum_scatter(attn_shift_grad, ("wide", "narrow"), scatter_dimension=0, tiled=True),
        lax.psum_scatter(
            inner_weight_grad.reshape(-1), ("wide", "narrow"), scatter_dimension=0, tiled=True
        ),
        lax.psum_scatter(inner_bias_grad, ("wide", "narrow"), scatter_dimension=0, tiled=True),
        lax.psum_scatter(
            outer_weight_grad.reshape(-1), ("wide", "narrow"), scatter_dimension=0, tiled=True
        ),
        lax.psum_scatter(outer_bias_grad, ("wide", "narrow"), scatter_dimension=0, tiled=True),
        lax.psum_scatter(ffn_gain_grad, ("wide", "narrow"), scatter_dimension=0, tiled=True),
        lax.psum_scatter(ffn_shift_grad, ("wide", "narrow"), scatter_dimension=0, tiled=True),
    )
    return (
        output,
        tokens_grad,
        own_qw,
        own_qb,
        own_kw,
        own_vw,
        own_vb,
        own_ow,
        own_ob,
        own_ag,
        own_as,
        own_iw,
        own_ib,
        own_uw,
        own_ub,
        own_fg,
        own_fs,
    )


def solution(mesh):
    split = P(AXES)
    rows = P(AXES, None)
    blocked = mesh.shape["wide"] == 8 and mesh.shape["narrow"] == 4
    return jax.shard_map(
        blocked_layer if blocked else plain_layer,
        mesh=mesh,
        in_specs=(rows,) + (split,) * 16 + (rows,),
        out_specs=(rows, rows) + (split,) * 15,
        check_vma=False,
    )
```
